32 devices in a mesh: tm: 16 (over z, y, x), order: 2 (over core).
Axes of the slice: x: 2, y: 2, z: 4, core: 2. Of those that a mesh axis runs over, the one named last changes fastest.
Arguments:
- solution: float32 [16, 2, 5760], P(None, 'order'), may hold values from -6 to 6
- residual: float32 [16, 2, 5760], P(None, 'order'), may hold values from -3 to 3
- direction: float32 [16, 2, 5760], P(None, 'order'), may hold values from -6 to 6
- precond: float32 [2, 5760], P('order'), may hold values from 0.25 to 4
- design: bfloat16 [4, 1024, 2, 5760], P(None, 'tm', 'order'), may hold values from -0.078125 to 0.078125
- epoch_counts: int32 [16], P('tm'), may hold values from 32 to 64, as said below
- segment_orders: int32 [4, 2], replicated, may hold values from 1 to 2, as said below
- pole_life: float32 [4, 2, 2], replicated, may hold values from 8 to 8192
- zero_ratio: float32 [4, 2, 2], replicated, may hold values from 0.1 to 2
- fir_taps: float32 [4, 9], replicated, may hold values from -2 to 2
Outputs:
- new_solution: float32 [16, 2, 5760], P(None, 'order', 'tm')
- new_residual: float32 [16, 2, 5760], P(None, 'order', 'tm')
- new_direction: float32 [16, 2, 5760], P(None, 'order', 'tm')
The draws below stay inside these ranges and needn't reach their ends.
Inputs may be any that keep to these rules, and one draw needn't show every extreme that they name: `epoch_counts`: valid epochs at the start of each block of 64 epochs; some block is complete. `segment_orders`: active sections of each segment; some segment of some component has all 2.
All inputs are finite; a program needn't handle non-finite values.
Results may differ from the reference program's by a relative error of at most 0.00105.
The reference program's roundings to bfloat16 on the way count: a program that leaves them out, or rounds other values in their place, can miss the bound.
Values may be sent and summed in bfloat16 or wider, within the bound.
No kernel may reach another device: no remote copies, remote signals or barrier semaphores. Data moves between devices by JAX's collectives and lax.ppermute only.
A program may use at most 64 MiB of HBM per device.

```python
import math
import jax
import jax.numpy as jnp
from jax import lax

EPOCH_DEV = 64
CB = 5760
RHS = 16
COMPS = 4
SEGMENTS = 2
SECT = 2
REACH = 8
TM_BLOCKS = 16
ORDER_BLOCKS = 2
EPOCHS = 1024
NC = 11520


def draw_epoch_counts(key, part):
    counts_key, chosen_key = jax.random.split(key)
    counts = jax.random.randint(counts_key, (TM_BLOCKS,), EPOCH_DEV // 2, EPOCH_DEV + 1)
    chosen = jax.random.randint(chosen_key, (), 0, TM_BLOCKS)
    return jnp.where(jnp.arange(TM_BLOCKS) == chosen, EPOCH_DEV, counts).astype(jnp.int32)


def draw_segment_orders(key, part):
    orders_key, chosen_key = jax.random.split(key)
    orders = jax.random.randint(orders_key, (COMPS, SEGMENTS), 1, SECT + 1)
    chosen = jax.random.randint(chosen_key, (), 0, COMPS * SEGMENTS)
    slots = jnp.arange(COMPS * SEGMENTS).reshape(COMPS, SEGMENTS)
    return jnp.where(slots == chosen, SECT, orders).astype(jnp.int32)


def with_spikes(drawn, own_key, source, target, shards_of, factor):
    owner, partner = [(jnp.arange(drawn.shape[dim]) // (drawn.shape[dim] // shards_of)).reshape([-1 if axis == dim else 1 for axis in range(drawn.ndim)]) for dim in (source, target)]
    chosen = jax.random.permutation(own_key, shards_of)[partner]
    strong = (owner == chosen) | (owner == (partner + shards_of // 2) % shards_of)
    return jnp.where(strong, factor * drawn, drawn)


def block_scale(key, shape, shards, smallest, largest):
    loudness = 1.0
    for axis_at, shards_of in shards:
        draws = jax.random.uniform(jax.random.fold_in(jax.random.fold_in(key, 6), axis_at), (shards_of,), jnp.float32, smallest / len(shards), largest / len(shards))
        loudness = loudness * jnp.repeat(jnp.exp(draws), shape[axis_at] // shards_of).reshape((-1,) + (1,) * (len(shape) - 1 - axis_at))
    return loudness


def scatter_about(stream_key, extent, spread, limit, cuts=(), held_as=jnp.bfloat16):
    array = spread * jax.random.normal(stream_key, extent, jnp.float32)
    if cuts:
        array = array * block_scale(stream_key, extent, cuts, -0.22, 0.18)
    return jnp.clip(array, -limit, limit).astype(held_as)


def bell_draw_with(key, dims, scale, most, pieces, heavy, held_as=jnp.bfloat16):
    array = scale * jax.random.normal(key, dims, jnp.float32)
    if pieces:
        array = array * block_scale(key, dims, pieces, -0.22, 0.18)
    return jnp.clip(with_spikes(array, jax.random.fold_in(key, 3), *heavy), -most, most).astype(held_as)


def setup_inputs(seed: int = 0) -> dict:
    keys = jax.random.split(jax.random.key(seed), 11)
    solution = scatter_about(keys[0], (RHS, ORDER_BLOCKS, CB), 1.0, 6.0, ((1, 2),), jnp.float32)
    residual = scatter_about(keys[1], (RHS, ORDER_BLOCKS, CB), 0.5, 3.0, ((1, 2),), jnp.float32)
    direction = scatter_about(keys[2], (RHS, ORDER_BLOCKS, CB), 1.0, 6.0, ((1, 2),), jnp.float32)
    precond = jnp.clip(jnp.exp(math.log(4.0) - 2.7725887 * jax.random.uniform(keys[3], (ORDER_BLOCKS, CB), jnp.float32) ** block_scale(keys[3], (ORDER_BLOCKS, CB), ((0, 2),), -0.2, 0.2)), 0.25, 4.0)
    design = bell_draw_with(keys[4], (COMPS, EPOCHS, ORDER_BLOCKS, CB), NC ** -0.5, 0.078125, ((1, 16), (2, 2)), (1, 3, 16, 2.0))
    epoch_counts = draw_epoch_counts(jax.random.fold_in(keys[10], 71), 0)
    segment_orders = draw_segment_orders(jax.random.fold_in(keys[10], 71), 0)
    pole_life = jnp.clip(jnp.exp(jax.random.uniform(keys[7], (COMPS, SEGMENTS, SECT), jnp.float32, math.log(8.0), math.log(8192.0))), 8.0, 8192.0)
    zero_ratio = jnp.clip(jnp.exp(jax.random.uniform(keys[8], (COMPS, SEGMENTS, SECT), jnp.float32, math.log(0.1), math.log(2.0))), 0.1, 2.0)
    fir_taps = scatter_about(keys[9], (COMPS, REACH + 1), (REACH + 1) ** -0.5, 2.0, (), jnp.float32)
    return dict(solution=solution, residual=residual, direction=direction, precond=precond, design=design, epoch_counts=epoch_counts, segment_orders=segment_orders, pole_life=pole_life, zero_ratio=zero_ratio, fir_taps=fir_taps)


HIGHEST = lax.Precision.HIGHEST


def filter_rates(segment_orders, pole_life, zero_ratio):
    components = pole_life.shape[0]
    sections = pole_life.shape[2]
    pole_all = jnp.exp(-1.0 / pole_life)
    active = jnp.arange(sections)[None, None, :] < segment_orders[:, :, None]
    pole_rate = jnp.where(active, pole_all, jnp.zeros_like(pole_all)).reshape(components, -1)
    zero_all = 1.0 - zero_ratio * (1.0 - pole_all)
    zero_rate = jnp.where(active, zero_all, jnp.zeros_like(zero_all)).reshape(components, -1)
    return pole_rate, zero_rate


def run_cascade(series, pole_rate, zero_rate):
    current = series
    for section in range(pole_rate.shape[1]):
        before = jnp.concatenate([jnp.zeros_like(current[:, :, :1]), current[:, :, :-1]], axis=2)
        driven = current - zero_rate[:, section][None, :, None] * before
        decay_now = pole_rate[:, section][None, :]

        def advance(carried, value, decay_now=decay_now):
            updated = decay_now * carried + value
            return updated, updated

        _, output = lax.scan(advance, jnp.zeros(driven.shape[:2], driven.dtype), jnp.moveaxis(driven, 2, 0))
        current = jnp.moveaxis(output, 0, 2)
    return current


def fir_forward(series, fir_taps):
    fir_reach = fir_taps.shape[1] - 1
    running = fir_taps[:, 0][None, :, None] * series
    for lag in range(1, fir_reach + 1):
        delayed = jnp.concatenate([jnp.zeros_like(series[:, :, :lag]), series[:, :, :-lag]], axis=2)
        running = running + fir_taps[:, lag][None, :, None] * delayed
    return running


def reference(solution, residual, direction, precond, design, epoch_counts, segment_orders, pole_life, zero_ratio, fir_taps):
    count = direction.shape[0]
    components = design.shape[0]
    design_rows = design.reshape(components, design.shape[1], -1)
    search = direction.reshape(count, -1)
    search_wide = search.astype(jnp.bfloat16).astype(jnp.float32)
    predicted = jnp.stack([jnp.dot(search_wide, design_rows[comp].astype(jnp.float32).T, precision=HIGHEST) for comp in range(components)], axis=1)
    epochs = design_rows.shape[1]
    per_block = epochs // epoch_counts.shape[0]
    position = jnp.arange(epochs).astype(jnp.int32)
    live_mask = (position % per_block < epoch_counts[position // per_block]).astype(predicted.dtype)
    pole_rate, zero_rate = filter_rates(segment_orders, pole_life, zero_ratio)
    observed = predicted * live_mask[None, None, :]
    whitened = run_cascade(observed, pole_rate, zero_rate)
    filtered = fir_forward(whitened, fir_taps)
    returned = jnp.flip(fir_forward(jnp.flip(filtered, 2), fir_taps), 2)
    weighted = jnp.flip(run_cascade(jnp.flip(returned, 2), pole_rate, zero_rate), 2) * live_mask[None, None, :]
    weighted_wide = weighted.astype(jnp.bfloat16).astype(jnp.float32)
    normal = jnp.zeros((count, design_rows.shape[2]), jnp.float32)
    for comp in range(components):
        normal = normal + jnp.dot(weighted_wide[:, comp, :], design_rows[comp].astype(jnp.float32), precision=HIGHEST)
    current = solution.reshape(count, -1)
    remaining = residual.reshape(count, -1)
    inverse_diag = precond.reshape(-1)
    energy = jnp.sum(remaining * inverse_diag[None, :] * remaining, axis=1)
    curvature = jnp.sum(search * normal, axis=1)
    step_length = (energy / curvature)[:, None]
    new_solution = current + step_length * search
    new_residual = remaining - step_length * normal
    conditioned = inverse_diag[None, :] * new_residual
    energy_next = jnp.sum(new_residual * conditioned, axis=1)
    new_direction = conditioned + (energy_next / energy)[:, None] * search
    return (new_solution.reshape(direction.shape), new_residual.reshape(direction.shape), new_direction.reshape(direction.shape))
```

```python
import functools

import jax
import jax.numpy as jnp
from jax import lax
from jax.experimental import pallas as pl
from jax.experimental.pallas import tpu as pltpu
from jax.sharding import PartitionSpec as P

HIGHEST = lax.Precision.HIGHEST
F32 = jnp.float32
BF16 = jnp.bfloat16
LANES = 128
SLOT = 16
VMEM_LIMIT = 48 * 1024 * 1024


def vmem():
    return pl.BlockSpec(memory_space=pltpu.VMEM)


def smem():
    return pl.BlockSpec(memory_space=pltpu.SMEM)


def call(kernel, outs, *args, specs=None, scratch=()):
    return pl.pallas_call(
        kernel,
        out_shape=outs,
        in_specs=specs or [vmem()] * len(args),
        out_specs=jax.tree.map(lambda _: vmem(), outs),
        scratch_shapes=scratch,
        compiler_params=pltpu.CompilerParams(vmem_limit_bytes=VMEM_LIMIT),
    )(*args)


def shape(*dims):
    return jax.ShapeDtypeStruct(dims, F32)


def predict_kernel(direction_ref, residual_ref, precond_ref, design_ref, out_ref):
    search = direction_ref[...]
    high = search.astype(BF16)
    rest = search - high.astype(F32)
    middle = rest.astype(BF16)
    low = (rest - middle.astype(F32)).astype(BF16)
    stacked = jnp.concatenate([high, middle, low], axis=0)
    count = search.shape[0]
    sums = lax.dot_general(
        design_ref[...], stacked, (((1,), (1,)), ((), ())), preferred_element_type=F32
    )
    length = sums.shape[0] * count // (LANES // 2)
    pieces = [sums[start : start + length] for start in range(0, sums.shape[0], length)]
    coarse = [piece[:, :count] for piece in pieces]
    fine = [piece[:, count : 2 * count] + piece[:, 2 * count :] for piece in pieces]
    out_ref[:length, :] = jnp.concatenate(coarse + fine, axis=1)
    remaining = residual_ref[...]
    energy = jnp.sum(remaining * precond_ref[...] * remaining, axis=1, keepdims=True)
    out_ref[length:, :] = jnp.broadcast_to(energy, (count, LANES))


def rows_of(value):
    return lax.broadcasted_iota(jnp.int32, value.shape, 0)


def down(value, by):
    moved = pltpu.roll(value, by, 0)
    return jnp.where(rows_of(value) >= by, moved, 0.0)


def up(value, by):
    length = value.shape[0]
    moved = pltpu.roll(value, length - by, 0)
    return jnp.where(rows_of(value) < length - by, moved, 0.0)


def recur(value, powers, move):
    by = 1
    for power in powers:
        value = value + power * move(value, by)
        by *= 2
    return value


def forward_block(series, starts, history, poles, zeros, taps):
    length = series.shape[0]
    first = rows_of(series) == 0
    current, states = (series, [series[length - 1 :]])
    for section, (powers, zero) in enumerate(zip(poles, zeros)):
        before = jnp.where(first, starts[section], pltpu.roll(current, 1, 0))
        driven = current - zero * before
        driven = driven + jnp.where(first, powers[0] * starts[section + 1], 0.0)
        current = recur(driven, powers, down)
        states.append(current[length - 1 :])
    extended = jnp.concatenate([history, current], axis=0)
    reach = history.shape[0]
    filtered = taps[0] * current
    for lag in range(1, len(taps)):
        filtered = filtered + taps[lag] * pltpu.roll(extended, lag, 0)[reach:]
    for back in range(1, reach):
        states.append(current[length - 1 - back : length - back])
    return (filtered, states)


def backward_block(filtered, ends, poles, zeros, taps):
    length = filtered.shape[0]
    reach = len(taps) - 1
    border = jnp.zeros((reach, LANES), F32)
    padded = jnp.concatenate([border, filtered, border], axis=0)
    total = padded.shape[0]
    spread = taps[0] * padded
    for lag in range(1, reach + 1):
        spread = spread + taps[lag] * pltpu.roll(padded, total - lag, 0)
    history = spread[:reach]
    current = spread[reach : reach + length]
    sections = len(poles)
    rows = rows_of(current)
    if ends is not None:
        for back in range(reach):
            current = current + jnp.where(rows == length - 1 - back, ends[sections + back], 0.0)
    states = [None] * (sections + reach)
    from_later = None
    for section in reversed(range(sections)):
        value = recur(current, poles[section], up)
        current = value - zeros[section] * up(value, 1)
        if ends is not None:
            current = current + jnp.where(rows == length - 1, ends[section], 0.0)
        to_output = poles[section][0] * value[:1]
        states[section + 1] = to_output if from_later is None else to_output + from_later
        from_later = -zeros[section] * value[:1]
    states[0] = from_later
    states[sections] = states[sections] + history[reach - 1 :]
    for back in range(1, reach):
        states[sections + back] = history[reach - 1 - back : reach - back]
    return (current, states)


def pack(states):
    rows = lax.broadcasted_iota(jnp.int32, (SLOT, LANES), 0)
    packed = jnp.zeros((SLOT, LANES), F32)
    for at, state in enumerate(states):
        packed = jnp.where(rows == at, state, packed)
    return packed


def filter_kernel(sections, taps_count, parts, *refs):
    counts_ref, table_ref = refs[:2]
    gathered = refs[2 : 2 + parts]
    send_ref, keep_ref, spread_ref, steps_ref, energy_ref = refs[2 + parts :]
    length = keep_ref.shape[0]
    half = LANES // 2
    received = gathered[0][...]
    for other in gathered[1:]:
        received = received + other[...]
    energy_ref[...] = received[length:]
    received = received[:length]
    lane = lax.broadcasted_iota(jnp.int32, (1, LANES), 1)
    live = rows_of(received) < counts_ref[0]
    data = jnp.where(live & (lane < half), received, 0.0)

    table = table_ref[...]
    life = table[:sections]
    ratio = table[sections : 2 * sections]
    active = table[2 * sections : 3 * sections] > 0.5
    taps = [table[3 * sections + at :][:1] for at in range(taps_count)]
    pole_all = jnp.exp(-1.0 / life)
    pole_rate = jnp.where(active, pole_all, 0.0)
    zero_rate = jnp.where(active, 1.0 - ratio * (1.0 - pole_all), 0.0)
    poles, zeros = ([], [])
    for section in range(sections):
        power, powers, by = (pole_rate[section : section + 1], [], 1)
        while by < length:
            powers.append(power)
            power, by = (power * power, 2 * by)
        poles.append(powers)
        zeros.append(zero_rate[section : section + 1])

    reach = taps_count - 1
    kinds = sections + reach
    slot = jnp.where(lane >= half, lane % SLOT, SLOT)
    units = [jnp.where(slot == at, 1.0, 0.0) for at in range(kinds)]
    rows = lax.broadcasted_iota(jnp.int32, (reach, LANES), 0)
    history = jnp.where(slot == kinds - 1 - rows, 1.0, 0.0)
    filtered, ends = forward_block(data, units[: sections + 1], history, poles, zeros, taps)
    local, heads = backward_block(filtered, None, poles, zeros, taps)
    reply, replies = backward_block(jnp.zeros_like(filtered), units, poles, zeros, taps)
    ends, heads, replies = (pack(ends), pack(heads), pack(replies))

    low_half = lane < half
    send_ref[...] = jnp.where(low_half, ends, pltpu.roll(heads, half, 1))
    spread_ref[...] = jnp.where(low_half, pltpu.roll(local, half, 1), reply)
    full = received + pltpu.roll(received, half, 1)
    keep_ref[...] = jnp.where(low_half, local, full)
    stacked = jnp.concatenate([ends, heads, replies], axis=0)
    source = lax.broadcasted_iota(jnp.int32, (LANES, kinds * LANES), 0)
    target = lax.broadcasted_iota(jnp.int32, (LANES, kinds * LANES), 1)
    within = target % LANES
    wanted = half + within // SLOT * SLOT + target // LANES
    pick = jnp.where((within < half) & (source == wanted), 1.0, 0.0)
    steps_ref[...] = jnp.dot(stacked, pick, precision=HIGHEST, preferred_element_type=F32)


def blocks_of(value, width, padded):
    wide = value.shape[1]
    window = min(padded + LANES, wide)
    for block in range(wide // width):
        start = block * width
        base = min(start // LANES * LANES, wide - window)
        part = value[:, base : base + window]
        if start != base:
            part = pltpu.roll(part, window - (start - base), 1)
        yield part[:, :padded]


def normal_kernel(kinds, width, layout, *refs):
    place_ref, counts_ref, all_ref, keep_ref, spread_ref, steps_ref, design_ref = refs[:7]
    out_ref, entering_ref = refs[7:]
    blocks = all_ref.shape[0]
    mine = place_ref[0]
    half = LANES // 2

    def apply(which, state):
        total = None
        for at in range(kinds):
            column = steps_ref[which * SLOT : (which + 1) * SLOT, at * LANES : (at + 1) * LANES]
            term = column * state[at : at + 1]
            total = term if total is None else total + term
        return total

    def advance(block, state):
        entering_ref[block] = state
        return apply(0, state) + all_ref[block]

    def retreat(step, state):
        block = blocks - 1 - step
        later = apply(2, state) + (apply(1, entering_ref[block]) + pltpu.roll(all_ref[block], half, 1))
        return jnp.where(block > mine, later, state)

    empty = jnp.zeros((SLOT, LANES), F32)
    unroll = blocks if blocks <= 16 else 4
    lax.fori_loop(0, blocks, advance, empty, unroll=unroll)
    leaving = lax.fori_loop(0, blocks, retreat, empty, unroll=unroll)
    entering = entering_ref[mine]

    groups = half // SLOT
    row = lax.broadcasted_iota(jnp.int32, (half, LANES), 0)
    lane = lax.broadcasted_iota(jnp.int32, (half, LANES), 1)
    own = row // SLOT == lane // SLOT
    expanded = [
        jnp.where(own, jnp.concatenate([state] * groups, axis=0), 0.0)
        for state in (entering, leaving)
    ]
    correction = jnp.dot(
        spread_ref[...],
        jnp.concatenate(expanded, axis=0),
        precision=HIGHEST,
        preferred_element_type=F32,
    )
    kept = keep_ref[...]
    live = rows_of(kept) < counts_ref[0]
    weighted = jnp.where(live & (lane < half), kept + correction, 0.0)
    weighted = weighted.astype(BF16).astype(F32)
    product = weighted * pltpu.roll(kept, half, 1)
    turned = jnp.transpose(weighted)
    count = out_ref.shape[-2]
    low = jnp.concatenate(
        [turned[at * count : (at + 1) * count] for at in range(half // count)], axis=1
    ).astype(BF16)
    curve = lax.dot_general(
        product,
        jnp.ones((product.shape[0], LANES), F32),
        (((0,), (0,)), ((), ())),
        precision=HIGHEST,
        preferred_element_type=F32,
    )
    curvature = curve[:count]
    for at in range(1, half // count):
        curvature = curvature + curve[at * count : (at + 1) * count]
    normal = jnp.dot(low, design_ref[...], preferred_element_type=F32)
    padded = out_ref.shape[-1]
    column = lax.broadcasted_iota(jnp.int32, (count, padded), 1)
    curvature = jnp.broadcast_to(curvature[:, :1], (count, padded))
    for block, part in enumerate(blocks_of(normal, width, padded)):
        out_ref[layout(block)] = jnp.where(column < width, part, curvature)


def slices_kernel(width, first_bits, place_ref, *refs):
    count = len(refs) // 2
    mine = place_ref[0]
    low = mine % first_bits
    for source_ref, target_ref in zip(refs[:count], refs[count:]):
        wide = source_ref.shape[-1]
        padded = target_ref.shape[-1]
        window = min(padded + LANES, wide)
        for at in range(target_ref.shape[0]):
            block = at * first_bits + low if target_ref.shape[0] > 1 else mine
            start = block * width
            base = jnp.minimum(start // LANES * LANES, wide - window)
            part = source_ref[:, pl.ds(pl.multiple_of(base, LANES), window)]
            part = jnp.broadcast_to(part, (target_ref.shape[1], window))
            moved = pltpu.roll(part, (window - (start - base)) % window, 1)
            target_ref[at] = moved[:, :padded]


def update_kernel(width, first_bits, *refs):
    place_ref, held_ref, got_ref, energy_ref = refs[:4]
    remaining_ref, diagonal_ref, current_ref, search_ref = refs[4:8]
    next_ref, new_solution_ref, new_residual_ref, conditioned_ref, entering_ref = refs[8:]
    parts, count, padded = held_ref.shape
    column = lax.broadcasted_iota(jnp.int32, (count, padded), 1)
    at_curve = column == width
    normal = held_ref[0] + got_ref[0]
    curvature = jnp.sum(jnp.where(at_curve, normal, 0.0), axis=1, keepdims=True)
    step = energy_ref[:, :1] / curvature
    total = jnp.zeros((count, padded), F32)
    for at in range(parts):
        normal = held_ref[at] + got_ref[at]
        changed = remaining_ref[at] - step * normal
        scaled = diagonal_ref[at] * changed
        entering_ref[at] = changed
        total = total + jnp.where(column < width, changed * scaled, 0.0)
    share = jnp.sum(total, axis=1, keepdims=True)
    next_ref[...] = jnp.broadcast_to(share, next_ref.shape)
    own = place_ref[0] // first_bits
    changed = entering_ref[own]
    new_residual_ref[...] = changed
    conditioned_ref[...] = diagonal_ref[own] * changed
    new_solution_ref[...] = current_ref[0] + step * search_ref[0]


def exchange(value, axis, bit):
    size = lax.axis_size(axis)
    return lax.ppermute(value, axis, [(at, at ^ bit) for at in range(size)])


def over_order(value):
    if lax.axis_size("order") == 2:
        return [value, exchange(value, "order", 1)]
    return [lax.psum(value, "order")]


def shards(
    solution,
    residual,
    direction,
    precond,
    design,
    epoch_counts,
    segment_orders,
    pole_life,
    zero_ratio,
    fir_taps,
):
    count, _, wide = direction.shape
    components, length = design.shape[:2]
    sections = pole_life.shape[1] * pole_life.shape[2]
    taps_count = fir_taps.shape[1]
    kinds = sections + taps_count - 1
    blocks = lax.axis_size("tm")
    width = wide // blocks
    padded = (width // LANES + 1) * LANES
    bits = blocks.bit_length() - 1
    halved = bits // 2
    classes = 1 << halved
    parts = blocks // classes
    place = lax.axis_index("tm").astype(jnp.int32).reshape(1)
    design_rows = design.reshape(components * length, wide)
    search = direction[:, 0, :]
    remaining = residual[:, 0, :]

    predicted = call(
        predict_kernel, shape(length + count, LANES), search, remaining, precond, design_rows
    )
    arrived = over_order(predicted)

    active = jnp.arange(pole_life.shape[2])[None, None, :] < segment_orders[:, :, None]
    columns = jnp.concatenate(
        [
            pole_life.reshape(components, -1),
            zero_ratio.reshape(components, -1),
            active.astype(F32).reshape(components, -1),
            fir_taps,
        ],
        axis=1,
    )
    table = jnp.broadcast_to(
        columns.T[:, None, :, None], (columns.shape[1], 2, components, count)
    ).reshape(columns.shape[1], LANES)

    send, keep, spread, steps, energy = call(
        functools.partial(filter_kernel, sections, taps_count, len(arrived)),
        (
            shape(SLOT, LANES),
            shape(length, LANES),
            shape(length, LANES),
            shape(3 * SLOT, kinds * LANES),
            shape(count, LANES),
        ),
        epoch_counts,
        table,
        *arrived,
        specs=[smem()] + [vmem()] * (1 + len(arrived)),
    )
    everyone = lax.all_to_all(jnp.broadcast_to(send, (blocks, SLOT, LANES)), "tm", 0, 0)

    def layout(block):
        low = [block >> bit & 1 for bit in range(halved)]
        return (*low, block >> halved)

    buffer = call(
        functools.partial(normal_kernel, kinds, width, layout),
        shape(*(2,) * halved, parts, count, padded),
        place,
        epoch_counts,
        everyone,
        keep,
        spread,
        steps,
        design_rows,
        specs=[smem()] * 2 + [vmem()] * 5,
        scratch=[pltpu.VMEM((blocks, SLOT, LANES), F32)],
    )
    diagonal_parts, remaining_parts, search_own, current_own = call(
        functools.partial(slices_kernel, width, classes),
        (
            shape(parts, count, padded),
            shape(parts, count, padded),
            shape(1, count, padded),
            shape(1, count, padded),
        ),
        place,
        precond,
        remaining,
        search,
        solution[:, 0, :],
        specs=[smem()] + [vmem()] * 4,
    )
    for bit in range(halved):
        side = place[0] >> bit & 1
        mine = lax.dynamic_index_in_dim(buffer, side, 0, False)
        other = lax.dynamic_index_in_dim(buffer, 1 - side, 0, False)
        buffer = mine + exchange(other, "tm", 1 << bit)
    for bit in range(halved, bits - 1):
        buffer = buffer + exchange(buffer, "tm", 1 << bit)
    arriving = exchange(buffer, "tm", 1 << bits - 1)
    share, new_solution, new_residual, conditioned = call(
        functools.partial(update_kernel, width, classes),
        (
            shape(count, LANES),
            shape(count, padded),
            shape(count, padded),
            shape(count, padded),
        ),
        place,
        buffer,
        arriving,
        energy,
        remaining_parts,
        diagonal_parts,
        current_own,
        search_own,
        specs=[smem()] + [vmem()] * 7,
        scratch=[pltpu.VMEM((parts, count, padded), F32)],
    )
    for bit in range(halved):
        share = share + exchange(share, "tm", 1 << bit)
    energy_next = sum(over_order(share))
    new_direction = conditioned + (energy_next / energy)[:, :1] * search_own[0]
    return tuple(
        vector[:, None, :width] for vector in (new_solution, new_residual, new_direction)
    )


def solution(mesh):
    placed = (
        P(None, "order", None),
        P(None, "order", None),
        P(None, "order", None),
        P("order", None),
        P(None, "tm", "order", None),
        P("tm"),
        P(),
        P(),
        P(),
        P(),
    )
    return jax.shard_map(
        shards,
        mesh=mesh,
        in_specs=placed,
        out_specs=(P(None, "order", "tm"), P(None, "order", "tm"), P(None, "order", "tm")),
        check_vma=False,
    )
```

```python
import functools

import jax
import jax.numpy as jnp
from jax import lax
from jax.experimental import pallas as pl
from jax.experimental.pallas import tpu as pltpu
from jax.sharding import PartitionSpec as P

HIGHEST = lax.Precision.HIGHEST
F32 = jnp.float32
BF16 = jnp.bfloat16
LANES = 128
SLOT = 16
VMEM_LIMIT = 16 * 1024 * 1024


def vmem():
    return pl.BlockSpec(memory_space=pltpu.VMEM)


def smem():
    return pl.BlockSpec(memory_space=pltpu.SMEM)


def call(kernel, outs, *args, specs=None, scratch=()):
    return pl.pallas_call(
        kernel,
        out_shape=outs,
        in_specs=specs or [vmem()] * len(args),
        out_specs=jax.tree.map(lambda _: vmem(), outs),
        scratch_shapes=scratch,
        compiler_params=pltpu.CompilerParams(vmem_limit_bytes=VMEM_LIMIT),
    )(*args)


def shape(*dims):
    return jax.ShapeDtypeStruct(dims, F32)


def predict_kernel(stacked_ref, energy_ref, design_ref, out_ref):
    count = stacked_ref.shape[0] // 3
    sums = lax.dot_general(
        design_ref[...], stacked_ref[...], (((1,), (1,)), ((), ())), preferred_element_type=F32
    )
    length = sums.shape[0] * count // (LANES // 2)
    pieces = [sums[start : start + length] for start in range(0, sums.shape[0], length)]
    coarse = [piece[:, :count] for piece in pieces]
    fine = [piece[:, count : 2 * count] + piece[:, 2 * count :] for piece in pieces]
    out_ref[:length, :] = jnp.concatenate(coarse + fine, axis=1)
    out_ref[length:, :] = energy_ref[...]


def rows_of(value):
    return lax.broadcasted_iota(jnp.int32, value.shape, 0)


def down(value, by):
    moved = pltpu.roll(value, by, 0)
    return jnp.where(rows_of(value) >= by, moved, 0.0)


def up(value, by):
    length = value.shape[0]
    moved = pltpu.roll(value, length - by, 0)
    return jnp.where(rows_of(value) < length - by, moved, 0.0)


def recur(value, powers, move):
    by = 1
    for power in powers:
        value = value + power * move(value, by)
        by *= 2
    return value


def forward_block(series, starts, history, poles, zeros, taps):
    length = series.shape[0]
    first = rows_of(series) == 0
    current, states = (series, [series[length - 1 :]])
    for section, (powers, zero) in enumerate(zip(poles, zeros)):
        if starts is None:
            driven = current - zero * down(current, 1)
        else:
            before = jnp.where(first, starts[section], pltpu.roll(current, 1, 0))
            driven = current - zero * before
            driven = driven + jnp.where(first, powers[0] * starts[section + 1], 0.0)
        current = recur(driven, powers, down)
        states.append(current[length - 1 :])
    reach = history.shape[0]
    extended = jnp.concatenate([history, current], axis=0)
    filtered = taps[0] * current
    for lag in range(1, len(taps)):
        filtered = filtered + taps[lag] * pltpu.roll(extended, lag, 0)[reach:]
    for back in range(1, reach):
        states.append(current[length - 1 - back : length - back])
    return (filtered, states)


def backward_block(filtered, ends, poles, zeros, taps):
    length = filtered.shape[0]
    reach = len(taps) - 1
    border = jnp.zeros((reach, LANES), F32)
    padded = jnp.concatenate([border, filtered, border], axis=0)
    total = padded.shape[0]
    spread = taps[0] * padded
    for lag in range(1, reach + 1):
        spread = spread + taps[lag] * pltpu.roll(padded, total - lag, 0)
    history = spread[:reach]
    current = spread[reach : reach + length]
    sections = len(poles)
    rows = rows_of(current)
    if ends is not None:
        for back in range(reach):
            current = current + jnp.where(rows == length - 1 - back, ends[sections + back], 0.0)
    states = [None] * (sections + reach)
    from_later = None
    for section in reversed(range(sections)):
        value = recur(current, poles[section], up)
        current = value - zeros[section] * up(value, 1)
        if ends is not None:
            current = current + jnp.where(rows == length - 1, ends[section], 0.0)
        to_output = poles[section][0] * value[:1]
        states[section + 1] = to_output if from_later is None else to_output + from_later
        from_later = -zeros[section] * value[:1]
    states[0] = from_later
    states[sections] = states[sections] + history[reach - 1 :]
    for back in range(1, reach):
        states[sections + back] = history[reach - 1 - back : reach - back]
    return (current, states)


def pack(states):
    rows = lax.broadcasted_iota(jnp.int32, (SLOT, LANES), 0)
    packed = jnp.zeros((SLOT, LANES), F32)
    for at, state in enumerate(states):
        packed = jnp.where(rows == at, state, packed)
    return packed


def rates_of(table, sections, taps_count, levels):
    rows = [table[at : at + 1] for at in range(sections * (levels + 1) + taps_count)]
    poles = [rows[at * levels : (at + 1) * levels] for at in range(sections)]
    zeros = rows[sections * levels : sections * (levels + 1)]
    return (poles, zeros, rows[sections * (levels + 1) :])


def prepare_kernel(width, first_bits, length, *refs):
    place_ref, orders_hbm, lives_hbm, ratios_hbm, taps_hbm, counts_hbm = refs[:6]
    vectors_hbm, diagonal_hbm = (refs[6:9], refs[9])
    outs, scratch = (refs[10:20], refs[20:])
    stacked_ref, energy_ref, live_ref, rates_ref, spread_ref, steps_ref = outs[:6]
    slices = outs[6:]
    orders_ref, lives_ref, ratios_ref, taps_ref, counts_ref = scratch[:5]
    current_ref, remaining_ref, search_ref, diagonal_ref, sems = scratch[5:]
    copies = [
        pltpu.make_async_copy(source, target, sems.at[at])
        for at, (source, target) in enumerate(
            [
                (orders_hbm, orders_ref),
                (lives_hbm, lives_ref),
                (ratios_hbm, ratios_ref),
                (taps_hbm, taps_ref),
                (counts_hbm, counts_ref),
                (vectors_hbm[2].at[:, 0, :], search_ref),
                (vectors_hbm[1].at[:, 0, :], remaining_ref),
                (diagonal_hbm, diagonal_ref),
                (vectors_hbm[0].at[:, 0, :], current_ref),
            ]
        )
    ]
    for copy in copies:
        copy.start()
    half = LANES // 2
    segments, sections_each, components = lives_ref.shape
    sections = segments * sections_each
    taps_count = taps_ref.shape[1]
    reach = taps_count - 1
    kinds = sections + reach
    for copy in copies[:5]:
        copy.wait()
    lane = lax.broadcasted_iota(jnp.int32, (components, LANES), 1)
    component = lax.broadcasted_iota(jnp.int32, (components, LANES), 0)
    count = half // components
    spreader = jnp.where(lane % half // count == component, 1.0, 0.0)

    def over_lanes(rows):
        return jnp.dot(rows, spreader, precision=HIGHEST, preferred_element_type=F32)

    def flat(ref):
        return jnp.concatenate([ref[at] for at in range(segments)], axis=0)

    life = over_lanes(flat(lives_ref))
    ratio = over_lanes(flat(ratios_ref))
    orders = over_lanes(orders_ref[...].astype(F32))
    tap_rows = lax.dot_general(
        taps_ref[...], spreader, (((0,), (0,)), ((), ())), precision=HIGHEST,
        preferred_element_type=F32,
    )
    spare = jnp.concatenate(
        [orders[at : at + 1] - (each + 0.5) for at in range(segments) for each in range(sections_each)],
        axis=0,
    )
    active = spare > 0.0
    pole_all = jnp.exp(-1.0 / life)
    pole_rate = jnp.where(active, pole_all, 0.0)
    zero_rate = jnp.where(active, 1.0 - ratio * (1.0 - pole_all), 0.0)
    levels = length.bit_length() - 1
    table = []
    for section in range(sections):
        power = pole_rate[section : section + 1]
        for _ in range(levels):
            table.append(power)
            power = power * power
    table = table + [zero_rate[section : section + 1] for section in range(sections)]
    table = table + [tap_rows[tap : tap + 1] for tap in range(taps_count)]
    for at, row in enumerate(table):
        rates_ref[at : at + 1, :] = row
    poles = [table[at * levels : (at + 1) * levels] for at in range(sections)]
    zeros = table[sections * levels : sections * (levels + 1)]
    taps = table[sections * (levels + 1) :]

    lane = lax.broadcasted_iota(jnp.int32, (1, LANES), 1)
    slot = jnp.where(lane >= half, lane % SLOT, SLOT)
    units = [jnp.where(slot == at, 1.0, 0.0) for at in range(kinds)]
    rows = lax.broadcasted_iota(jnp.int32, (reach, LANES), 0)
    history = jnp.where(slot == kinds - 1 - rows, 1.0, 0.0)
    nothing = jnp.zeros((length, LANES), F32)
    filtered, ends = forward_block(nothing, units[: sections + 1], history, poles, zeros, taps)
    local, heads = backward_block(filtered, None, poles, zeros, taps)
    reply, replies = backward_block(nothing, units, poles, zeros, taps)
    spread_ref[...] = jnp.where(lane < half, pltpu.roll(local, half, 1), reply)
    stacked = jnp.concatenate([pack(ends), pack(heads), pack(replies)], axis=0)
    source = lax.broadcasted_iota(jnp.int32, (LANES, kinds * LANES), 0)
    target = lax.broadcasted_iota(jnp.int32, (LANES, kinds * LANES), 1)
    within = target % LANES
    wanted = half + within // SLOT * SLOT + target // LANES
    pick = jnp.where((within < half) & (source == wanted), 1.0, 0.0)
    steps_ref[...] = jnp.dot(stacked, pick, precision=HIGHEST, preferred_element_type=F32)
    live_ref[...] = jnp.where(rows_of(nothing) < counts_ref[0], 1.0, 0.0)

    copies[5].wait()
    search = search_ref[...]
    high = search.astype(BF16)
    rest = search - high.astype(F32)
    middle = rest.astype(BF16)
    stacked_ref[...] = jnp.concatenate(
        [high, middle, (rest - middle.astype(F32)).astype(BF16)], axis=0
    )
    copies[6].wait()
    copies[7].wait()
    remaining = remaining_ref[...]
    energy = jnp.sum(remaining * diagonal_ref[...] * remaining, axis=1, keepdims=True)
    energy_ref[...] = jnp.broadcast_to(energy, energy_ref.shape)
    copies[8].wait()
    cut_slices(width, first_bits, place_ref[0], [diagonal_ref, remaining_ref, search_ref, current_ref], slices)


def filter_kernel(sections, taps_count, parts, *refs):
    rates_ref, live_ref = refs[:2]
    gathered = refs[2 : 2 + parts]
    send_ref, keep_ref, energy_ref = refs[2 + parts :]
    length = keep_ref.shape[0]
    half = LANES // 2
    received = gathered[0][...]
    for other in gathered[1:]:
        received = received + other[...]
    energy_ref[...] = received[length:]
    received = received[:length]
    low_half = lax.broadcasted_iota(jnp.int32, (1, LANES), 1) < half
    data = jnp.where(low_half, received * live_ref[...], 0.0)
    poles, zeros, taps = rates_of(rates_ref, sections, taps_count, length.bit_length() - 1)
    history = jnp.zeros((taps_count - 1, LANES), F32)
    filtered, ends = forward_block(data, None, history, poles, zeros, taps)
    local, heads = backward_block(filtered, None, poles, zeros, taps)
    sent = jnp.where(low_half, pack(ends), pltpu.roll(pack(heads), half, 1))
    for block in range(send_ref.shape[0]):
        send_ref[block] = sent
    keep_ref[...] = jnp.where(low_half, local, received + pltpu.roll(received, half, 1))


def blocks_of(value, width, padded):
    wide = value.shape[1]
    window = min(padded + LANES, wide)
    for block in range(wide // width):
        start = block * width
        base = min(start // LANES * LANES, wide - window)
        part = value[:, base : base + window]
        if start != base:
            part = pltpu.roll(part, window - (start - base), 1)
        yield part[:, :padded]


def normal_kernel(kinds, width, first_bits, *refs):
    place_ref, live_ref, all_ref, keep_ref, spread_ref, steps_ref, design_ref = refs[:7]
    out_refs, entering_ref = (refs[7:-1], refs[-1])
    blocks = all_ref.shape[0]
    mine = place_ref[0]
    half = LANES // 2

    def apply(which, state):
        total = None
        for at in range(kinds):
            column = steps_ref[which * SLOT : (which + 1) * SLOT, at * LANES : (at + 1) * LANES]
            term = column * state[at : at + 1]
            total = term if total is None else total + term
        return total

    def advance(block, state):
        entering_ref[block] = state
        return apply(0, state) + all_ref[block]

    def retreat(step, state):
        block = blocks - 1 - step
        later = apply(2, state) + (apply(1, entering_ref[block]) + pltpu.roll(all_ref[block], half, 1))
        return jnp.where(block > mine, later, state)

    empty = jnp.zeros((SLOT, LANES), F32)
    unroll = blocks if blocks <= 16 else 4
    lax.fori_loop(0, blocks, advance, empty, unroll=unroll)
    leaving = lax.fori_loop(0, blocks, retreat, empty, unroll=unroll)
    entering = entering_ref[mine]

    groups = half // SLOT
    row = lax.broadcasted_iota(jnp.int32, (half, LANES), 0)
    lane = lax.broadcasted_iota(jnp.int32, (half, LANES), 1)
    own = row // SLOT == lane // SLOT
    expanded = [
        jnp.where(own, jnp.concatenate([state] * groups, axis=0), 0.0)
        for state in (entering, leaving)
    ]
    correction = jnp.dot(
        spread_ref[...],
        jnp.concatenate(expanded, axis=0),
        precision=HIGHEST,
        preferred_element_type=F32,
    )
    kept = keep_ref[...]
    weighted = jnp.where(lane < half, (kept + correction) * live_ref[...], 0.0)
    weighted = weighted.astype(BF16).astype(F32)
    product = weighted * pltpu.roll(kept, half, 1)
    turned = jnp.transpose(weighted)
    count = out_refs[0].shape[-2]
    low = jnp.concatenate(
        [turned[at * count : (at + 1) * count] for at in range(half // count)], axis=1
    ).astype(BF16)
    curve = lax.dot_general(
        product,
        jnp.ones((product.shape[0], LANES), F32),
        (((0,), (0,)), ((), ())),
        precision=HIGHEST,
        preferred_element_type=F32,
    )
    curvature = curve[:count]
    for at in range(1, half // count):
        curvature = curvature + curve[at * count : (at + 1) * count]
    normal = jnp.dot(low, design_ref[...], preferred_element_type=F32)
    padded = out_refs[0].shape[-1]
    column = lax.broadcasted_iota(jnp.int32, (count, padded), 1)
    curvature = jnp.broadcast_to(curvature[:, :1], (count, padded))
    low_bits = mine % first_bits
    for block, part in enumerate(blocks_of(normal, width, padded)):
        part = jnp.where(column < width, part, curvature)
        for apart, out_ref in enumerate(out_refs):

            @pl.when((low_bits ^ apart) == block % first_bits)
            def _(out_ref=out_ref, part=part, block=block):
                out_ref[block // first_bits] = part


def cut_slices(width, first_bits, mine, sources, targets):
    low = mine % first_bits
    for source_ref, target_ref in zip(sources, targets):
        wide = source_ref.shape[-1]
        padded = target_ref.shape[-1]
        window = min(padded + LANES, wide)
        for at in range(target_ref.shape[0]):
            block = at * first_bits + low if target_ref.shape[0] > 1 else mine
            start = block * width
            base = jnp.minimum(start // LANES * LANES, wide - window)
            part = source_ref[:, pl.ds(pl.multiple_of(base, LANES), window)]
            part = jnp.broadcast_to(part, (target_ref.shape[1], window))
            moved = pltpu.roll(part, (window - (start - base)) % window, 1)
            target_ref[at] = moved[:, :padded]


def update_kernel(width, first_bits, *refs):
    place_ref, held_ref, got_ref, energy_ref = refs[:4]
    remaining_ref, diagonal_ref, current_ref, search_ref = refs[4:8]
    next_ref, new_solution_ref, new_residual_ref, conditioned_ref, entering_ref = refs[8:]
    parts, count, padded = held_ref.shape
    column = lax.broadcasted_iota(jnp.int32, (count, padded), 1)
    at_curve = column == width
    normal = held_ref[0] + got_ref[0]
    curvature = jnp.sum(jnp.where(at_curve, normal, 0.0), axis=1, keepdims=True)
    step = energy_ref[:, :1] / curvature
    total = jnp.zeros((count, padded), F32)
    for at in range(parts):
        normal = held_ref[at] + got_ref[at]
        changed = remaining_ref[at] - step * normal
        scaled = diagonal_ref[at] * changed
        entering_ref[at] = changed
        total = total + jnp.where(column < width, changed * scaled, 0.0)
    share = jnp.sum(total, axis=1, keepdims=True)
    next_ref[...] = jnp.broadcast_to(share, next_ref.shape)
    own = place_ref[0] // first_bits
    changed = entering_ref[own]
    new_residual_ref[...] = changed
    conditioned_ref[...] = diagonal_ref[own] * changed
    new_solution_ref[...] = current_ref[0] + step * search_ref[0]


def exchange(value, axis, bit):
    size = lax.axis_size(axis)
    return lax.ppermute(value, axis, [(at, at ^ bit) for at in range(size)])


def over_order(value):
    if lax.axis_size("order") == 2:
        return [value, exchange(value, "order", 1)]
    return [lax.psum(value, "order")]


def shards(
    solution,
    residual,
    direction,
    precond,
    design,
    epoch_counts,
    segment_orders,
    pole_life,
    zero_ratio,
    fir_taps,
):
    count, _, wide = direction.shape
    components, length = design.shape[:2]
    sections = pole_life.shape[1] * pole_life.shape[2]
    taps_count = fir_taps.shape[1]
    kinds = sections + taps_count - 1
    blocks = lax.axis_size("tm")
    width = wide // blocks
    padded = (width // LANES + 1) * LANES
    bits = blocks.bit_length() - 1
    halved = bits // 2
    classes = 1 << halved
    parts = blocks // classes
    place = lax.axis_index("tm").astype(jnp.int32).reshape(1)
    design_rows = design.reshape(components * length, wide)
    levels = length.bit_length() - 1
    anywhere = pl.BlockSpec(memory_space=pl.ANY)
    small = [
        segment_orders.T,
        jnp.transpose(pole_life, (1, 2, 0)),
        jnp.transpose(zero_ratio, (1, 2, 0)),
        fir_taps,
    ]

    (stacked, energy_own, live, rates, spread, steps, diagonal_parts, remaining_parts, search_own, current_own) = call(
        functools.partial(prepare_kernel, width, classes, length),
        (
            jax.ShapeDtypeStruct((3 * count, wide), BF16),
            shape(count, LANES),
            shape(length, LANES),
            shape(sections * (levels + 1) + taps_count, LANES),
            shape(length, LANES),
            shape(3 * SLOT, kinds * LANES),
            shape(parts, count, padded),
            shape(parts, count, padded),
            shape(1, count, padded),
            shape(1, count, padded),
        ),
        place,
        *small,
        epoch_counts,
        solution,
        residual,
        direction,
        precond,
        specs=[smem()] + [anywhere] * 9,
        scratch=[pltpu.VMEM(each.shape, each.dtype) for each in small]
        + [pltpu.SMEM((1,), jnp.int32)]
        + [pltpu.VMEM((count, wide), F32)] * 3
        + [pltpu.VMEM((1, wide), F32), pltpu.SemaphoreType.DMA((9,))],
    )
    predicted = call(
        predict_kernel, shape(length + count, LANES), stacked, energy_own, design_rows
    )
    arrived = over_order(predicted)
    send, keep, energy = call(
        functools.partial(filter_kernel, sections, taps_count, len(arrived)),
        (shape(blocks, SLOT, LANES), shape(length, LANES), shape(count, LANES)),
        rates,
        live,
        *arrived,
    )
    everyone = lax.all_to_all(send, "tm", 0, 0)
    pieces = call(
        functools.partial(normal_kernel, kinds, width, classes),
        [shape(parts, count, padded)] * classes,
        place,
        live,
        everyone,
        keep,
        spread,
        steps,
        design_rows,
        specs=[smem()] + [vmem()] * 6,
        scratch=[pltpu.VMEM((blocks, SLOT, LANES), F32)],
    )
    arriving = [exchange(pieces[apart], "tm", apart) for apart in range(1, classes)]
    buffer = pieces[0] + sum(arriving[1:], arriving[0])
    for bit in range(halved, bits - 1):
        buffer = buffer + exchange(buffer, "tm", 1 << bit)
    arriving = exchange(buffer, "tm", 1 << bits - 1)
    share, new_solution, new_residual, conditioned = call(
        functools.partial(update_kernel, width, classes),
        (
            shape(count, LANES),
            shape(count, padded),
            shape(count, padded),
            shape(count, padded),
        ),
        place,
        buffer,
        arriving,
        energy,
        remaining_parts,
        diagonal_parts,
        current_own,
        search_own,
        specs=[smem()] + [vmem()] * 7,
        scratch=[pltpu.VMEM((parts, count, padded), F32)],
    )
    for bit in range(halved):
        share = share + exchange(share, "tm", 1 << bit)
    energy_next = sum(over_order(share))
    new_direction = conditioned + (energy_next / energy)[:, :1] * search_own[0]
    return tuple(
        vector[:, None, :width] for vector in (new_solution, new_residual, new_direction)
    )


def solution(mesh):
    placed = (
        P(None, "order", None),
        P(None, "order", None),
        P(None, "order", None),
        P("order", None),
        P(None, "tm", "order", None),
        P("tm"),
        P(),
        P(),
        P(),
        P(),
    )
    return jax.shard_map(
        shards,
        mesh=mesh,
        in_specs=placed,
        out_specs=(P(None, "order", "tm"), P(None, "order", "tm"), P(None, "order", "tm")),
        check_vma=False,
    )
```

```python
import functools

import jax
import jax.numpy as jnp
from jax import lax
from jax.experimental import pallas as pl
from jax.experimental.pallas import tpu as pltpu
from jax.sharding import PartitionSpec as P

HIGHEST = lax.Precision.HIGHEST
F32 = jnp.float32
BF16 = jnp.bfloat16
LANES = 128
SLOT = 16
VMEM_LIMIT = 16 * 1024 * 1024


def vmem():
    return pl.BlockSpec(memory_space=pltpu.VMEM)


def smem():
    return pl.BlockSpec(memory_space=pltpu.SMEM)


def call(kernel, outs, *args, specs=None, scratch=()):
    args = [
        pltpu.with_memory_space_constraint(arg, pltpu.HBM)
        if specs and specs[at].memory_space == pltpu.HBM
        else arg
        for at, arg in enumerate(args)
    ]
    return pl.pallas_call(
        kernel,
        out_shape=outs,
        in_specs=specs or [vmem()] * len(args),
        out_specs=jax.tree.map(lambda _: vmem(), outs),
        scratch_shapes=scratch,
        compiler_params=pltpu.CompilerParams(vmem_limit_bytes=VMEM_LIMIT),
    )(*args)


def shape(*dims):
    return jax.ShapeDtypeStruct(dims, F32)


def rows_of(value):
    return lax.broadcasted_iota(jnp.int32, value.shape, 0)


def down(value, by):
    moved = pltpu.roll(value, by, 0)
    return jnp.where(rows_of(value) >= by, moved, 0.0)


def up(value, by):
    length = value.shape[0]
    moved = pltpu.roll(value, length - by, 0)
    return jnp.where(rows_of(value) < length - by, moved, 0.0)


def recur(value, powers, move):
    by = 1
    for power in powers:
        value = value + power * move(value, by)
        by *= 2
    return value


def forward_block(series, starts, history, poles, zeros, taps):
    length = series.shape[0]
    first = rows_of(series) == 0
    current, states = (series, [series[length - 1 :]])
    for section, (powers, zero) in enumerate(zip(poles, zeros)):
        if starts is None:
            driven = current - zero * down(current, 1)
        else:
            before = jnp.where(first, starts[section], pltpu.roll(current, 1, 0))
            driven = current - zero * before
            driven = driven + jnp.where(first, powers[0] * starts[section + 1], 0.0)
        current = recur(driven, powers, down)
        states.append(current[length - 1 :])
    reach = history.shape[0]
    extended = jnp.concatenate([history, current], axis=0)
    filtered = taps[0] * current
    for lag in range(1, len(taps)):
        filtered = filtered + taps[lag] * pltpu.roll(extended, lag, 0)[reach:]
    for back in range(1, reach):
        states.append(current[length - 1 - back : length - back])
    return (filtered, states)


def backward_block(filtered, ends, poles, zeros, taps):
    length = filtered.shape[0]
    reach = len(taps) - 1
    border = jnp.zeros((reach, LANES), F32)
    padded = jnp.concatenate([border, filtered, border], axis=0)
    total = padded.shape[0]
    spread = taps[0] * padded
    for lag in range(1, reach + 1):
        spread = spread + taps[lag] * pltpu.roll(padded, total - lag, 0)
    history = spread[:reach]
    current = spread[reach : reach + length]
    sections = len(poles)
    rows = rows_of(current)
    if ends is not None:
        for back in range(reach):
            current = current + jnp.where(rows == length - 1 - back, ends[sections + back], 0.0)
    states = [None] * (sections + reach)
    from_later = None
    for section in reversed(range(sections)):
        value = recur(current, poles[section], up)
        current = value - zeros[section] * up(value, 1)
        if ends is not None:
            current = current + jnp.where(rows == length - 1, ends[section], 0.0)
        to_output = poles[section][0] * value[:1]
        states[section + 1] = to_output if from_later is None else to_output + from_later
        from_later = -zeros[section] * value[:1]
    states[0] = from_later
    states[sections] = states[sections] + history[reach - 1 :]
    for back in range(1, reach):
        states[sections + back] = history[reach - 1 - back : reach - back]
    return (current, states)


def pack(states):
    rows = lax.broadcasted_iota(jnp.int32, (SLOT, LANES), 0)
    packed = jnp.zeros((SLOT, LANES), F32)
    for at, state in enumerate(states):
        packed = jnp.where(rows == at, state, packed)
    return packed


def rates_of(table, sections, taps_count, levels):
    rows = [table[at : at + 1] for at in range(sections * (levels + 1) + taps_count)]
    poles = [rows[at * levels : (at + 1) * levels] for at in range(sections)]
    zeros = rows[sections * levels : sections * (levels + 1)]
    return (poles, zeros, rows[sections * (levels + 1) :])


def prepare_kernel(width, first_bits, length, *refs):
    place_ref, orders_hbm, lives_hbm, ratios_hbm, taps_hbm = refs[:5]
    vectors_hbm, diagonal_hbm, design_hbm = (refs[5:8], refs[8], refs[9])
    outs, scratch = (refs[10:18], refs[18:])
    predicted_ref, rates_ref, spread_ref, steps_ref = outs[:4]
    slices = outs[4:]
    orders_ref, lives_ref, ratios_ref, taps_ref = scratch[:4]
    current_ref, remaining_ref, search_ref, diagonal_ref, design_ref, sems = scratch[4:]
    components = design_ref.shape[0]
    copies = [
        pltpu.make_async_copy(source, target, sems.at[at])
        for at, (source, target) in enumerate(
            [
                (orders_hbm, orders_ref),
                (lives_hbm, lives_ref),
                (ratios_hbm, ratios_ref),
                (taps_hbm, taps_ref),
                (vectors_hbm[2].at[:, 0, :], search_ref),
                *[(design_hbm.at[at], design_ref.at[at]) for at in range(components)],
                (vectors_hbm[1].at[:, 0, :], remaining_ref),
                (diagonal_hbm, diagonal_ref),
                (vectors_hbm[0].at[:, 0, :], current_ref),
            ]
        )
    ]
    for copy in copies:
        copy.start()
    half = LANES // 2
    segments, sections_each, _ = lives_ref.shape
    sections = segments * sections_each
    taps_count = taps_ref.shape[1]
    reach = taps_count - 1
    kinds = sections + reach
    for copy in copies[:4]:
        copy.wait()
    lane = lax.broadcasted_iota(jnp.int32, (components, LANES), 1)
    component = lax.broadcasted_iota(jnp.int32, (components, LANES), 0)
    count = half // components
    spreader = jnp.where(lane % half // count == component, 1.0, 0.0)

    def over_lanes(rows):
        return jnp.dot(rows, spreader, precision=HIGHEST, preferred_element_type=F32)

    def flat(ref):
        return jnp.concatenate([ref[at] for at in range(segments)], axis=0)

    life = over_lanes(flat(lives_ref))
    ratio = over_lanes(flat(ratios_ref))
    orders = over_lanes(orders_ref[...].astype(F32))
    tap_rows = lax.dot_general(
        taps_ref[...], spreader, (((0,), (0,)), ((), ())), precision=HIGHEST,
        preferred_element_type=F32,
    )
    spare = jnp.concatenate(
        [orders[at : at + 1] - (each + 0.5) for at in range(segments) for each in range(sections_each)],
        axis=0,
    )
    active = spare > 0.0
    pole_all = jnp.exp(-1.0 / life)
    pole_rate = jnp.where(active, pole_all, 0.0)
    zero_rate = jnp.where(active, 1.0 - ratio * (1.0 - pole_all), 0.0)
    levels = length.bit_length() - 1
    table = []
    for section in range(sections):
        power = pole_rate[section : section + 1]
        for _ in range(levels):
            table.append(power)
            power = power * power
    table = table + [zero_rate[section : section + 1] for section in range(sections)]
    table = table + [tap_rows[tap : tap + 1] for tap in range(taps_count)]
    for at, row in enumerate(table):
        rates_ref[at : at + 1, :] = row
    poles = [table[at * levels : (at + 1) * levels] for at in range(sections)]
    zeros = table[sections * levels : sections * (levels + 1)]
    taps = table[sections * (levels + 1) :]

    lane = lax.broadcasted_iota(jnp.int32, (1, LANES), 1)
    slot = jnp.where(lane >= half, lane % SLOT, SLOT)
    units = [jnp.where(slot == at, 1.0, 0.0) for at in range(kinds)]
    rows = lax.broadcasted_iota(jnp.int32, (reach, LANES), 0)
    history = jnp.where(slot == kinds - 1 - rows, 1.0, 0.0)
    nothing = jnp.zeros((length, LANES), F32)
    filtered, ends = forward_block(nothing, units[: sections + 1], history, poles, zeros, taps)
    local, heads = backward_block(filtered, None, poles, zeros, taps)
    reply, replies = backward_block(nothing, units, poles, zeros, taps)
    spread_ref[...] = jnp.where(lane < half, pltpu.roll(local, half, 1), reply)
    stacked = jnp.concatenate([pack(ends), pack(heads), pack(replies)], axis=0)
    source = lax.broadcasted_iota(jnp.int32, (LANES, kinds * LANES), 0)
    target = lax.broadcasted_iota(jnp.int32, (LANES, kinds * LANES), 1)
    within = target % LANES
    wanted = half + within // SLOT * SLOT + target // LANES
    pick = jnp.where((within < half) & (source == wanted), 1.0, 0.0)
    steps_ref[...] = jnp.dot(stacked, pick, precision=HIGHEST, preferred_element_type=F32)

    copies[4].wait()
    search = search_ref[...]
    high = search.astype(BF16)
    rest = search - high.astype(F32)
    middle = rest.astype(BF16)
    low = (rest - middle.astype(F32)).astype(BF16)
    split = jnp.concatenate([high, middle, low], axis=0)
    coarse, fine = ([], [])
    for at in range(components):
        copies[5 + at].wait()
        sums = lax.dot_general(
            design_ref[at], split, (((1,), (1,)), ((), ())), preferred_element_type=F32
        )
        coarse.append(sums[:, :count])
        fine.append(sums[:, count : 2 * count] + sums[:, 2 * count :])
    predicted_ref[:length, :] = jnp.concatenate(coarse + fine, axis=1)
    for copy in copies[5 + components :]:
        copy.wait()
    remaining = remaining_ref[...]
    energy = jnp.sum(remaining * diagonal_ref[...] * remaining, axis=1, keepdims=True)
    predicted_ref[length:, :] = jnp.broadcast_to(energy, (count, LANES))
    sources = [diagonal_ref, remaining_ref, search_ref, current_ref]
    cut_slices(width, first_bits, place_ref[0], sources, slices)


def filter_kernel(sections, taps_count, parts, *refs):
    counts_ref, rates_ref = refs[:2]
    gathered = refs[2 : 2 + parts]
    send_ref, keep_ref, energy_ref = refs[2 + parts :]
    length = keep_ref.shape[0]
    half = LANES // 2
    received = gathered[0][...]
    for other in gathered[1:]:
        received = received + other[...]
    energy_ref[...] = received[length:]
    received = received[:length]
    low_half = lax.broadcasted_iota(jnp.int32, (1, LANES), 1) < half
    data = jnp.where(low_half & (rows_of(received) < counts_ref[0]), received, 0.0)
    poles, zeros, taps = rates_of(rates_ref, sections, taps_count, length.bit_length() - 1)
    history = jnp.zeros((taps_count - 1, LANES), F32)
    filtered, ends = forward_block(data, None, history, poles, zeros, taps)
    local, heads = backward_block(filtered, None, poles, zeros, taps)
    sent = jnp.where(low_half, pack(ends), pltpu.roll(pack(heads), half, 1))
    for block in range(send_ref.shape[0]):
        send_ref[block] = sent
    keep_ref[...] = jnp.where(low_half, local, received + pltpu.roll(received, half, 1))


def blocks_of(value, width, padded):
    wide = value.shape[1]
    window = min(padded + LANES, wide)
    for block in range(wide // width):
        start = block * width
        base = min(start // LANES * LANES, wide - window)
        part = value[:, base : base + window]
        if start != base:
            part = pltpu.roll(part, window - (start - base), 1)
        yield part[:, :padded]


def normal_kernel(kinds, width, first_bits, *refs):
    place_ref, counts_ref, all_ref, keep_ref, spread_ref, steps_ref, design_hbm = refs[:7]
    out_refs, (entering_ref, design_ref, sem) = (refs[7:-3], refs[-3:])
    fetch = pltpu.make_async_copy(design_hbm, design_ref, sem)
    fetch.start()
    blocks = all_ref.shape[0]
    mine = place_ref[0]
    half = LANES // 2

    def apply(which, state):
        total = None
        for at in range(kinds):
            column = steps_ref[which * SLOT : (which + 1) * SLOT, at * LANES : (at + 1) * LANES]
            term = column * state[at : at + 1]
            total = term if total is None else total + term
        return total

    def advance(block, state):
        entering_ref[block] = state
        return apply(0, state) + all_ref[block]

    def retreat(step, state):
        block = blocks - 1 - step
        later = apply(2, state) + (apply(1, entering_ref[block]) + pltpu.roll(all_ref[block], half, 1))
        return jnp.where(block > mine, later, state)

    empty = jnp.zeros((SLOT, LANES), F32)
    unroll = blocks if blocks <= 16 else 4
    lax.fori_loop(0, blocks, advance, empty, unroll=unroll)
    leaving = lax.fori_loop(0, blocks, retreat, empty, unroll=unroll)
    entering = entering_ref[mine]

    groups = half // SLOT
    row = lax.broadcasted_iota(jnp.int32, (half, LANES), 0)
    lane = lax.broadcasted_iota(jnp.int32, (half, LANES), 1)
    own = row // SLOT == lane // SLOT
    expanded = [
        jnp.where(own, jnp.concatenate([state] * groups, axis=0), 0.0)
        for state in (entering, leaving)
    ]
    correction = jnp.dot(
        spread_ref[...],
        jnp.concatenate(expanded, axis=0),
        precision=HIGHEST,
        preferred_element_type=F32,
    )
    kept = keep_ref[...]
    live = (row < counts_ref[0]) & (lane < half)
    weighted = jnp.where(live, kept + correction, 0.0)
    weighted = weighted.astype(BF16).astype(F32)
    product = weighted * pltpu.roll(kept, half, 1)
    turned = jnp.transpose(weighted)
    count = out_refs[0].shape[-2]
    low = jnp.concatenate(
        [turned[at * count : (at + 1) * count] for at in range(half // count)], axis=1
    ).astype(BF16)
    curve = lax.dot_general(
        product,
        jnp.ones((product.shape[0], LANES), F32),
        (((0,), (0,)), ((), ())),
        precision=HIGHEST,
        preferred_element_type=F32,
    )
    curvature = curve[:count]
    for at in range(1, half // count):
        curvature = curvature + curve[at * count : (at + 1) * count]
    fetch.wait()
    normal = jnp.dot(low, design_ref[...], preferred_element_type=F32)
    padded = out_refs[0].shape[-1]
    column = lax.broadcasted_iota(jnp.int32, (count, padded), 1)
    curvature = jnp.broadcast_to(curvature[:, :1], (count, padded))
    low_bits = mine % first_bits
    for block, part in enumerate(blocks_of(normal, width, padded)):
        part = jnp.where(column < width, part, curvature)
        for apart, out_ref in enumerate(out_refs):

            @pl.when((low_bits ^ apart) == block % first_bits)
            def _(out_ref=out_ref, part=part, block=block):
                out_ref[block // first_bits] = part


def cut_slices(width, first_bits, mine, sources, targets):
    low = mine % first_bits
    for source_ref, target_ref in zip(sources, targets):
        wide = source_ref.shape[-1]
        padded = target_ref.shape[-1]
        window = min(padded + LANES, wide)
        for at in range(target_ref.shape[0]):
            block = at * first_bits + low if target_ref.shape[0] > 1 else mine
            start = block * width
            base = jnp.minimum(start // LANES * LANES, wide - window)
            part = source_ref[:, pl.ds(pl.multiple_of(base, LANES), window)]
            part = jnp.broadcast_to(part, (target_ref.shape[1], window))
            moved = pltpu.roll(part, (window - (start - base)) % window, 1)
            target_ref[at] = moved[:, :padded]


def update_kernel(width, first_bits, *refs):
    place_ref, held_ref, got_ref, energy_ref = refs[:4]
    remaining_ref, diagonal_ref, current_ref, search_ref = refs[4:8]
    next_ref, new_solution_ref, new_residual_ref, conditioned_ref, entering_ref = refs[8:]
    parts, count, padded = held_ref.shape
    column = lax.broadcasted_iota(jnp.int32, (count, padded), 1)
    at_curve = column == width
    normal = held_ref[0] + got_ref[0]
    curvature = jnp.sum(jnp.where(at_curve, normal, 0.0), axis=1, keepdims=True)
    step = energy_ref[:, :1] / curvature
    total = jnp.zeros((count, padded), F32)
    for at in range(parts):
        normal = held_ref[at] + got_ref[at]
        changed = remaining_ref[at] - step * normal
        scaled = diagonal_ref[at] * changed
        entering_ref[at] = changed
        total = total + jnp.where(column < width, changed * scaled, 0.0)
    share = jnp.sum(total, axis=1, keepdims=True)
    next_ref[...] = jnp.broadcast_to(share, next_ref.shape)
    own = place_ref[0] // first_bits
    changed = entering_ref[own]
    new_residual_ref[...] = changed
    conditioned_ref[...] = diagonal_ref[own] * changed
    new_solution_ref[...] = current_ref[0] + step * search_ref[0]


def exchange(value, axis, bit):
    size = lax.axis_size(axis)
    return lax.ppermute(value, axis, [(at, at ^ bit) for at in range(size)])


def over_order(value):
    if lax.axis_size("order") == 2:
        return [value, exchange(value, "order", 1)]
    return [lax.psum(value, "order")]


def shards(
    solution,
    residual,
    direction,
    precond,
    design,
    epoch_counts,
    segment_orders,
    pole_life,
    zero_ratio,
    fir_taps,
):
    count, _, wide = direction.shape
    components, length = design.shape[:2]
    sections = pole_life.shape[1] * pole_life.shape[2]
    taps_count = fir_taps.shape[1]
    kinds = sections + taps_count - 1
    blocks = lax.axis_size("tm")
    width = wide // blocks
    padded = (width // LANES + 1) * LANES
    bits = blocks.bit_length() - 1
    halved = bits // 2
    classes = 1 << halved
    parts = blocks // classes
    place = lax.axis_index("tm").astype(jnp.int32).reshape(1)
    levels = length.bit_length() - 1
    hbm = pl.BlockSpec(memory_space=pltpu.HBM)
    small = [
        segment_orders.T,
        jnp.transpose(pole_life, (1, 2, 0)),
        jnp.transpose(zero_ratio, (1, 2, 0)),
        fir_taps,
    ]

    (predicted, rates, spread, steps, diagonal_parts, remaining_parts, search_own, current_own) = call(
        functools.partial(prepare_kernel, width, classes, length),
        (
            shape(length + count, LANES),
            shape(sections * (levels + 1) + taps_count, LANES),
            shape(length, LANES),
            shape(3 * SLOT, kinds * LANES),
            shape(parts, count, padded),
            shape(parts, count, padded),
            shape(1, count, padded),
            shape(1, count, padded),
        ),
        place,
        *small,
        solution,
        residual,
        direction,
        precond,
        design[:, :, 0, :],
        specs=[smem()] + [hbm] * 9,
        scratch=[pltpu.VMEM(each.shape, each.dtype) for each in small]
        + [pltpu.VMEM((count, wide), F32)] * 3
        + [pltpu.VMEM((1, wide), F32), pltpu.VMEM((components, length, wide), BF16)]
        + [pltpu.SemaphoreType.DMA((8 + components,))],
    )
    arrived = over_order(predicted)
    send, keep, energy = call(
        functools.partial(filter_kernel, sections, taps_count, len(arrived)),
        (shape(blocks, SLOT, LANES), shape(length, LANES), shape(count, LANES)),
        epoch_counts,
        rates,
        *arrived,
        specs=[smem()] + [vmem()] * (1 + len(arrived)),
    )
    everyone = lax.all_to_all(send, "tm", 0, 0)
    pieces = call(
        functools.partial(normal_kernel, kinds, width, classes),
        [shape(parts, count, padded)] * classes,
        place,
        epoch_counts,
        everyone,
        keep,
        spread,
        steps,
        design.reshape(components * length, wide),
        specs=[smem()] * 2 + [vmem()] * 4 + [hbm],
        scratch=[
            pltpu.VMEM((blocks, SLOT, LANES), F32),
            pltpu.VMEM((components * length, wide), BF16),
            pltpu.SemaphoreType.DMA,
        ],
    )
    arriving = [exchange(pieces[apart], "tm", apart) for apart in range(1, classes)]
    buffer = pieces[0] + sum(arriving[1:], arriving[0])
    for bit in range(halved, bits - 1):
        buffer = buffer + exchange(buffer, "tm", 1 << bit)
    arriving = exchange(buffer, "tm", 1 << bits - 1)
    share, new_solution, new_residual, conditioned = call(
        functools.partial(update_kernel, width, classes),
        (
            shape(count, LANES),
            shape(count, padded),
            shape(count, padded),
            shape(count, padded),
        ),
        place,
        buffer,
        arriving,
        energy,
        remaining_parts,
        diagonal_parts,
        current_own,
        search_own,
        specs=[smem()] + [vmem()] * 7,
        scratch=[pltpu.VMEM((parts, count, padded), F32)],
    )
    for bit in range(halved):
        share = share + exchange(share, "tm", 1 << bit)
    energy_next = sum(over_order(share))
    new_direction = conditioned + (energy_next / energy)[:, :1] * search_own[0]
    return tuple(
        vector[:, None, :width] for vector in (new_solution, new_residual, new_direction)
    )


def solution(mesh):
    placed = (
        P(None, "order", None),
        P(None, "order", None),
        P(None, "order", None),
        P("order", None),
        P(None, "tm", "order", None),
        P("tm"),
        P(),
        P(),
        P(),
        P(),
    )
    return jax.shard_map(
        shards,
        mesh=mesh,
        in_specs=placed,
        out_specs=(P(None, "order", "tm"), P(None, "order", "tm"), P(None, "order", "tm")),
        check_vma=False,
    )
```

```python
import functools

import jax
import jax.numpy as jnp
from jax import lax
from jax.experimental import pallas as pl
from jax.experimental.pallas import tpu as pltpu
from jax.sharding import PartitionSpec as P

HIGHEST = lax.Precision.HIGHEST
F32 = jnp.float32
BF16 = jnp.bfloat16
LANES = 128
SLOT = 16
VMEM_LIMIT = 16 * 1024 * 1024


def vmem():
    return pl.BlockSpec(memory_space=pltpu.VMEM)


def smem():
    return pl.BlockSpec(memory_space=pltpu.SMEM)


def call(kernel, outs, *args, specs=None, scratch=()):
    args = [
        pltpu.with_memory_space_constraint(arg, pltpu.HBM)
        if specs and specs[at].memory_space == pltpu.HBM
        else arg
        for at, arg in enumerate(args)
    ]
    return pl.pallas_call(
        kernel,
        out_shape=outs,
        in_specs=specs or [vmem()] * len(args),
        out_specs=jax.tree.map(
            lambda out: pl.BlockSpec(memory_space=getattr(out, "memory_space", pltpu.VMEM)), outs
        ),
        scratch_shapes=scratch,
        compiler_params=pltpu.CompilerParams(vmem_limit_bytes=VMEM_LIMIT),
    )(*args)


def shape(*dims):
    return jax.ShapeDtypeStruct(dims, F32)


def column_block(source_ref, block, width, padded):
    wide = source_ref.shape[-1]
    window = min(padded + LANES, wide)
    start = block * width
    base = jnp.minimum(start // LANES * LANES, wide - window)
    part = source_ref[:, pl.ds(pl.multiple_of(base, LANES), window)]
    return pltpu.roll(part, (window - (start - base)) % window, 1)[:, :padded]


def rows_of(value):
    return lax.broadcasted_iota(jnp.int32, value.shape, 0)


def down(value, by):
    moved = pltpu.roll(value, by, 0)
    return jnp.where(rows_of(value) >= by, moved, 0.0)


def up(value, by):
    length = value.shape[0]
    moved = pltpu.roll(value, length - by, 0)
    return jnp.where(rows_of(value) < length - by, moved, 0.0)


def recur(value, powers, move):
    by = 1
    for power in powers:
        value = value + power * move(value, by)
        by *= 2
    return value


def forward_block(series, starts, history, poles, zeros, taps):
    length = series.shape[0]
    first = rows_of(series) == 0
    current, states = (series, [series[length - 1 :]])
    for section, (powers, zero) in enumerate(zip(poles, zeros)):
        if starts is None:
            driven = current - zero * down(current, 1)
        else:
            before = jnp.where(first, starts[section], pltpu.roll(current, 1, 0))
            driven = current - zero * before
            driven = driven + jnp.where(first, powers[0] * starts[section + 1], 0.0)
        current = recur(driven, powers, down)
        states.append(current[length - 1 :])
    reach = history.shape[0]
    extended = jnp.concatenate([history, current], axis=0)
    filtered = taps[0] * current
    for lag in range(1, len(taps)):
        filtered = filtered + taps[lag] * pltpu.roll(extended, lag, 0)[reach:]
    for back in range(1, reach):
        states.append(current[length - 1 - back : length - back])
    return (filtered, states)


def backward_block(filtered, ends, poles, zeros, taps):
    length = filtered.shape[0]
    reach = len(taps) - 1
    border = jnp.zeros((reach, LANES), F32)
    padded = jnp.concatenate([border, filtered, border], axis=0)
    total = padded.shape[0]
    spread = taps[0] * padded
    for lag in range(1, reach + 1):
        spread = spread + taps[lag] * pltpu.roll(padded, total - lag, 0)
    history = spread[:reach]
    current = spread[reach : reach + length]
    sections = len(poles)
    rows = rows_of(current)
    if ends is not None:
        for back in range(reach):
            current = current + jnp.where(rows == length - 1 - back, ends[sections + back], 0.0)
    states = [None] * (sections + reach)
    from_later = None
    for section in reversed(range(sections)):
        value = recur(current, poles[section], up)
        current = value - zeros[section] * up(value, 1)
        if ends is not None:
            current = current + jnp.where(rows == length - 1, ends[section], 0.0)
        to_output = poles[section][0] * value[:1]
        states[section + 1] = to_output if from_later is None else to_output + from_later
        from_later = -zeros[section] * value[:1]
    states[0] = from_later
    states[sections] = states[sections] + history[reach - 1 :]
    for back in range(1, reach):
        states[sections + back] = history[reach - 1 - back : reach - back]
    return (current, states)


def pack(states):
    rows = lax.broadcasted_iota(jnp.int32, (SLOT, LANES), 0)
    packed = jnp.zeros((SLOT, LANES), F32)
    for at, state in enumerate(states):
        packed = jnp.where(rows == at, state, packed)
    return packed


def rates_of(table, sections, taps_count, levels):
    rows = [table[at : at + 1] for at in range(sections * (levels + 1) + taps_count)]
    poles = [rows[at * levels : (at + 1) * levels] for at in range(sections)]
    zeros = rows[sections * levels : sections * (levels + 1)]
    return (poles, zeros, rows[sections * (levels + 1) :])


def predict_kernel(*refs):
    orders_hbm, lives_hbm, ratios_hbm, taps_hbm = refs[:4]
    residual_hbm, direction_hbm, diagonal_hbm, design_hbm = refs[4:8]
    predicted_ref, rates_ref, design_ref = refs[8:11]
    orders_ref, lives_ref, ratios_ref, taps_ref, remaining_ref, search_ref, diagonal_ref, sems = refs[11:]
    components, length, _ = design_ref.shape
    copies = [
        pltpu.make_async_copy(source, target, sems.at[at])
        for at, (source, target) in enumerate(
            [
                (direction_hbm.at[:, 0, :], search_ref),
                (orders_hbm, orders_ref),
                (lives_hbm, lives_ref),
                (ratios_hbm, ratios_ref),
                (taps_hbm, taps_ref),
                *[(design_hbm.at[at], design_ref.at[at]) for at in range(components)],
                (residual_hbm.at[:, 0, :], remaining_ref),
                (diagonal_hbm, diagonal_ref),
            ]
        )
    ]
    for copy in copies:
        copy.start()
    half = LANES // 2
    segments, sections_each, _ = lives_ref.shape
    sections = segments * sections_each
    taps_count = taps_ref.shape[1]
    for copy in copies[1:5]:
        copy.wait()
    lane = lax.broadcasted_iota(jnp.int32, (components, LANES), 1)
    component = lax.broadcasted_iota(jnp.int32, (components, LANES), 0)
    count = half // components
    spreader = jnp.where(lane % half // count == component, 1.0, 0.0)

    def over_lanes(rows):
        return jnp.dot(rows, spreader, precision=HIGHEST, preferred_element_type=F32)

    def flat(ref):
        return jnp.concatenate([ref[at] for at in range(segments)], axis=0)

    life = over_lanes(flat(lives_ref))
    ratio = over_lanes(flat(ratios_ref))
    orders = over_lanes(orders_ref[...].astype(F32))
    tap_rows = lax.dot_general(
        taps_ref[...], spreader, (((0,), (0,)), ((), ())), precision=HIGHEST,
        preferred_element_type=F32,
    )
    spare = jnp.concatenate(
        [orders[at : at + 1] - (each + 0.5) for at in range(segments) for each in range(sections_each)],
        axis=0,
    )
    active = spare > 0.0
    pole_all = jnp.exp(-1.0 / life)
    pole_rate = jnp.where(active, pole_all, 0.0)
    zero_rate = jnp.where(active, 1.0 - ratio * (1.0 - pole_all), 0.0)
    levels = length.bit_length() - 1
    power = pole_rate
    for level in range(levels):
        for section in range(sections):
            at = section * levels + level
            rates_ref[at : at + 1, :] = power[section : section + 1]
        power = power * power
    rates_ref[sections * levels : sections * (levels + 1), :] = zero_rate
    rates_ref[sections * (levels + 1) : sections * (levels + 1) + taps_count, :] = tap_rows

    copies[0].wait()
    search = search_ref[...]
    high = search.astype(BF16)
    rest = search - high.astype(F32)
    middle = rest.astype(BF16)
    low = (rest - middle.astype(F32)).astype(BF16)
    split = jnp.concatenate([high, middle, low], axis=0)
    coarse, fine = ([], [])
    for at in range(components):
        copies[5 + at].wait()
        sums = lax.dot_general(
            design_ref[at], split, (((1,), (1,)), ((), ())), preferred_element_type=F32
        )
        coarse.append(sums[:, :count])
        fine.append(sums[:, count : 2 * count] + sums[:, 2 * count :])
    predicted_ref[:length, :] = jnp.concatenate(coarse + fine, axis=1)
    for copy in copies[5 + components :]:
        copy.wait()
    remaining = remaining_ref[...]
    energy = jnp.sum(remaining * diagonal_ref[...] * remaining, axis=1, keepdims=True)
    predicted_ref[length:, :] = jnp.broadcast_to(energy, (count, LANES))


def tables_kernel(width, first_bits, sections, taps_count, length, *refs):
    place_ref, rates_ref, keep_hbm = refs[:3]
    vectors_hbm, diagonal_hbm = (refs[3:6], refs[6])
    spread_ref, steps_ref, energy_ref = refs[7:10]
    slices = refs[10:14]
    current_ref, remaining_ref, search_ref, diagonal_ref, sems = refs[14:]
    sources = [current_ref, remaining_ref, search_ref]
    copies = [
        pltpu.make_async_copy(vector.at[:, 0, :], target, sems.at[at])
        for at, (vector, target) in enumerate(zip(vectors_hbm, sources))
    ]
    copies.append(pltpu.make_async_copy(diagonal_hbm, diagonal_ref, sems.at[len(sources)]))
    tail = keep_hbm.at[pl.ds(length, energy_ref.shape[0]), :]
    copies.append(pltpu.make_async_copy(tail, energy_ref, sems.at[len(sources) + 1]))
    for copy in copies:
        copy.start()
    half = LANES // 2
    reach = taps_count - 1
    kinds = sections + reach
    poles, zeros, taps = rates_of(rates_ref, sections, taps_count, length.bit_length() - 1)
    lane = lax.broadcasted_iota(jnp.int32, (1, LANES), 1)
    slot = jnp.where(lane >= half, lane % SLOT, SLOT)
    units = [jnp.where(slot == at, 1.0, 0.0) for at in range(kinds)]
    rows = lax.broadcasted_iota(jnp.int32, (reach, LANES), 0)
    history = jnp.where(slot == kinds - 1 - rows, 1.0, 0.0)
    nothing = jnp.zeros((length, LANES), F32)
    filtered, ends = forward_block(nothing, units[: sections + 1], history, poles, zeros, taps)
    local, heads = backward_block(filtered, None, poles, zeros, taps)
    reply, replies = backward_block(nothing, units, poles, zeros, taps)
    spread_ref[...] = jnp.where(lane < half, pltpu.roll(local, half, 1), reply)
    stacked = jnp.concatenate([pack(ends), pack(heads), pack(replies)], axis=0)
    source = lax.broadcasted_iota(jnp.int32, (LANES, kinds * LANES), 0)
    target = lax.broadcasted_iota(jnp.int32, (LANES, kinds * LANES), 1)
    within = target % LANES
    wanted = half + within // SLOT * SLOT + target // LANES
    pick = jnp.where((within < half) & (source == wanted), 1.0, 0.0)
    steps_ref[...] = jnp.dot(stacked, pick, precision=HIGHEST, preferred_element_type=F32)
    for copy in copies:
        copy.wait()
    mine = place_ref[0]
    vectors = [diagonal_ref, remaining_ref, search_ref, current_ref]
    for source_ref, target_ref in zip(vectors, slices):
        for at in range(target_ref.shape[0]):
            block = mine if target_ref.shape[0] == 1 else at * first_bits + mine % first_bits
            part = column_block(source_ref, block, width, target_ref.shape[2])
            target_ref[at] = jnp.broadcast_to(part, target_ref.shape[1:])


def filter_kernel(sections, taps_count, length, parts, *refs):
    counts_ref, rates_ref = refs[:2]
    gathered = refs[2 : 2 + parts]
    send_ref, keep_hbm, keep_ref, sem = refs[2 + parts :]
    half = LANES // 2
    received = gathered[0][...]
    for other in gathered[1:]:
        received = received + other[...]
    keep_ref[length:, :] = received[length:]
    received = received[:length]
    low_half = lax.broadcasted_iota(jnp.int32, (1, LANES), 1) < half
    data = jnp.where(low_half & (rows_of(received) < counts_ref[0]), received, 0.0)
    poles, zeros, taps = rates_of(rates_ref, sections, taps_count, length.bit_length() - 1)
    history = jnp.zeros((taps_count - 1, LANES), F32)
    filtered, ends = forward_block(data, None, history, poles, zeros, taps)
    local, heads = backward_block(filtered, None, poles, zeros, taps)
    sent = jnp.where(low_half, pack(ends), pltpu.roll(pack(heads), half, 1))
    for block in range(send_ref.shape[0]):
        send_ref[block] = sent
    keep_ref[:length, :] = jnp.where(low_half, local, received + pltpu.roll(received, half, 1))
    copy = pltpu.make_async_copy(keep_ref, keep_hbm, sem)
    copy.start()
    copy.wait()


def normal_kernel(kinds, width, first_bits, *refs):
    place_ref, counts_ref, all_ref, keep_hbm, spread_ref, steps_ref, design_ref = refs[:7]
    out_refs, (entering_ref, normal_ref, keep_ref, sem) = (refs[7:-4], refs[-4:])
    fetch = pltpu.make_async_copy(keep_hbm.at[pl.ds(0, keep_ref.shape[0]), :], keep_ref, sem)
    fetch.start()
    blocks = all_ref.shape[0]
    mine = place_ref[0]
    half = LANES // 2

    def apply(which, state):
        total = None
        for at in range(kinds):
            column = steps_ref[which * SLOT : (which + 1) * SLOT, at * LANES : (at + 1) * LANES]
            term = column * state[at : at + 1]
            total = term if total is None else total + term
        return total

    def advance(block, state):
        entering_ref[block] = state
        return apply(0, state) + all_ref[block]

    def retreat(step, state):
        block = blocks - 1 - step
        later = apply(2, state) + (apply(1, entering_ref[block]) + pltpu.roll(all_ref[block], half, 1))
        return jnp.where(block > mine, later, state)

    empty = jnp.zeros((SLOT, LANES), F32)
    unroll = blocks if blocks <= 16 else 4
    lax.fori_loop(0, blocks, advance, empty, unroll=unroll)
    leaving = lax.fori_loop(0, blocks, retreat, empty, unroll=unroll)
    entering = entering_ref[mine]

    groups = half // SLOT
    row = lax.broadcasted_iota(jnp.int32, (half, LANES), 0)
    lane = lax.broadcasted_iota(jnp.int32, (half, LANES), 1)
    own = row // SLOT == lane // SLOT
    expanded = [
        jnp.where(own, jnp.concatenate([state] * groups, axis=0), 0.0)
        for state in (entering, leaving)
    ]
    correction = jnp.dot(
        spread_ref[...],
        jnp.concatenate(expanded, axis=0),
        precision=HIGHEST,
        preferred_element_type=F32,
    )
    fetch.wait()
    kept = keep_ref[...]
    live = (row < counts_ref[0]) & (lane < half)
    weighted = jnp.where(live, kept + correction, 0.0)
    weighted = weighted.astype(BF16).astype(F32)
    product = weighted * pltpu.roll(kept, half, 1)
    turned = jnp.transpose(weighted)
    count = out_refs[0].shape[-2]
    low = jnp.concatenate(
        [turned[at * count : (at + 1) * count] for at in range(half // count)], axis=1
    ).astype(BF16)
    curve = lax.dot_general(
        product,
        jnp.ones((product.shape[0], LANES), F32),
        (((0,), (0,)), ((), ())),
        precision=HIGHEST,
        preferred_element_type=F32,
    )
    curvature = curve[:count]
    for at in range(1, half // count):
        curvature = curvature + curve[at * count : (at + 1) * count]
    rows = jnp.concatenate([design_ref[at] for at in range(design_ref.shape[0])], axis=0)
    normal_ref[...] = jnp.dot(low, rows, preferred_element_type=F32)
    padded = out_refs[0].shape[-1]
    column = lax.broadcasted_iota(jnp.int32, (count, padded), 1)
    curvature = jnp.broadcast_to(curvature[:, :1], (count, padded))
    low_bits = mine % first_bits
    for apart, out_ref in enumerate(out_refs):
        for at in range(out_ref.shape[0]):
            block = at * first_bits + (low_bits ^ apart)
            part = column_block(normal_ref, block, width, padded)
            out_ref[at] = jnp.where(column < width, part, curvature)


def update_kernel(width, first_bits, *refs):
    place_ref, held_ref, got_ref, energy_ref = refs[:4]
    remaining_ref, diagonal_ref, current_ref, search_ref = refs[4:8]
    next_ref, new_solution_ref, new_residual_ref, conditioned_ref, entering_ref = refs[8:]
    parts, count, padded = held_ref.shape
    column = lax.broadcasted_iota(jnp.int32, (count, padded), 1)
    at_curve = column == width
    normal = held_ref[0] + got_ref[0]
    curvature = jnp.sum(jnp.where(at_curve, normal, 0.0), axis=1, keepdims=True)
    step = energy_ref[:, :1] / curvature
    total = jnp.zeros((count, padded), F32)
    for at in range(parts):
        normal = held_ref[at] + got_ref[at]
        changed = remaining_ref[at] - step * normal
        scaled = diagonal_ref[at] * changed
        entering_ref[at] = changed
        total = total + jnp.where(column < width, changed * scaled, 0.0)
    share = jnp.sum(total, axis=1, keepdims=True)
    next_ref[...] = jnp.broadcast_to(share, next_ref.shape)
    own = place_ref[0] // first_bits
    changed = entering_ref[own]
    new_residual_ref[...] = changed
    conditioned_ref[...] = diagonal_ref[own] * changed
    new_solution_ref[...] = current_ref[0] + step * search_ref[0]


def exchange(value, axis, bit):
    size = lax.axis_size(axis)
    return lax.ppermute(value, axis, [(at, at ^ bit) for at in range(size)])


def over_order(value):
    if lax.axis_size("order") == 2:
        return [value, exchange(value, "order", 1)]
    return [lax.psum(value, "order")]


def shards(
    solution,
    residual,
    direction,
    precond,
    design,
    epoch_counts,
    segment_orders,
    pole_life,
    zero_ratio,
    fir_taps,
):
    count, _, wide = direction.shape
    components, length = design.shape[:2]
    sections = pole_life.shape[1] * pole_life.shape[2]
    taps_count = fir_taps.shape[1]
    kinds = sections + taps_count - 1
    blocks = lax.axis_size("tm")
    width = wide // blocks
    padded = (width // LANES + 1) * LANES
    bits = blocks.bit_length() - 1
    halved = bits // 2
    classes = 1 << halved
    parts = blocks // classes
    place = lax.axis_index("tm").astype(jnp.int32).reshape(1)
    levels = length.bit_length() - 1
    hbm = pl.BlockSpec(memory_space=pltpu.HBM)
    small = [
        segment_orders.T,
        jnp.transpose(pole_life, (1, 2, 0)),
        jnp.transpose(zero_ratio, (1, 2, 0)),
        fir_taps,
    ]

    predicted, rates, design_kept = call(
        predict_kernel,
        (
            shape(length + count, LANES),
            shape(sections * (levels + 1) + taps_count, LANES),
            jax.ShapeDtypeStruct((components, length, wide), BF16),
        ),
        *small,
        residual,
        direction,
        precond,
        design[:, :, 0, :],
        specs=[hbm] * 8,
        scratch=[pltpu.VMEM(each.shape, each.dtype) for each in small]
        + [pltpu.VMEM((count, wide), F32)] * 2
        + [pltpu.VMEM((1, wide), F32), pltpu.SemaphoreType.DMA((7 + components,))],
    )
    arrived = over_order(predicted)
    send, keep = call(
        functools.partial(filter_kernel, sections, taps_count, length, len(arrived)),
        (shape(blocks, SLOT, LANES), pltpu.HBM((length + count, LANES), F32)),
        epoch_counts,
        rates,
        *arrived,
        specs=[smem()] + [vmem()] * (1 + len(arrived)),
        scratch=[pltpu.VMEM((length + count, LANES), F32), pltpu.SemaphoreType.DMA],
    )
    everyone = lax.all_to_all(send, "tm", 0, 0)
    spread, steps, energy, diagonal_parts, remaining_parts, search_own, current_own = call(
        functools.partial(tables_kernel, width, classes, sections, taps_count, length),
        (
            shape(length, LANES),
            shape(3 * SLOT, kinds * LANES),
            shape(count, LANES),
            shape(parts, count, padded),
            shape(parts, count, padded),
            shape(1, count, padded),
            shape(1, count, padded),
        ),
        place,
        rates,
        keep,
        solution,
        residual,
        direction,
        precond,
        specs=[smem(), vmem()] + [hbm] * 5,
        scratch=[pltpu.VMEM((count, wide), F32)] * 3
        + [pltpu.VMEM((1, wide), F32), pltpu.SemaphoreType.DMA((5,))],
    )
    pieces = call(
        functools.partial(normal_kernel, kinds, width, classes),
        [shape(parts, count, padded)] * classes,
        place,
        epoch_counts,
        everyone,
        keep,
        spread,
        steps,
        design_kept,
        specs=[smem()] * 2 + [vmem(), hbm] + [vmem()] * 3,
        scratch=[
            pltpu.VMEM((blocks, SLOT, LANES), F32),
            pltpu.VMEM((count, wide), F32),
            pltpu.VMEM((length, LANES), F32),
            pltpu.SemaphoreType.DMA,
        ],
    )
    arriving = [exchange(pieces[apart], "tm", apart) for apart in range(1, classes)]
    buffer = pieces[0] + sum(arriving[1:], arriving[0])
    for bit in range(halved, bits - 1):
        buffer = buffer + exchange(buffer, "tm", (2 << bit) - classes)
    arriving = exchange(buffer, "tm", blocks - classes)
    share, new_solution, new_residual, conditioned = call(
        functools.partial(update_kernel, width, classes),
        (
            shape(count, LANES),
            shape(count, padded),
            shape(count, padded),
            shape(count, padded),
        ),
        place,
        buffer,
        arriving,
        energy,
        remaining_parts,
        diagonal_parts,
        current_own,
        search_own,
        specs=[smem()] + [vmem()] * 7,
        scratch=[pltpu.VMEM((parts, count, padded), F32)],
    )
    for bit in range(halved):
        share = share + exchange(share, "tm", 1 << bit)
    energy_next = sum(over_order(share))
    new_direction = conditioned + (energy_next / energy)[:, :1] * search_own[0]
    return tuple(
        vector[:, None, :width] for vector in (new_solution, new_residual, new_direction)
    )


def solution(mesh):
    placed = (
        P(None, "order", None),
        P(None, "order", None),
        P(None, "order", None),
        P("order", None),
        P(None, "tm", "order", None),
        P("tm"),
        P(),
        P(),
        P(),
        P(),
    )
    return jax.shard_map(
        shards,
        mesh=mesh,
        in_specs=placed,
        out_specs=(P(None, "order", "tm"), P(None, "order", "tm"), P(None, "order", "tm")),
        check_vma=False,
    )
```

```python
import functools

import jax
import jax.numpy as jnp
from jax import lax
from jax.experimental import pallas as pl
from jax.experimental.pallas import tpu as pltpu
from jax.sharding import PartitionSpec as P

HIGHEST = lax.Precision.HIGHEST
F32 = jnp.float32
BF16 = jnp.bfloat16
LANES = 128
SLOT = 16
VMEM_LIMIT = 16 * 1024 * 1024


def vmem():
    return pl.BlockSpec(memory_space=pltpu.VMEM)


def smem():
    return pl.BlockSpec(memory_space=pltpu.SMEM)


def call(kernel, outs, *args, specs=None, scratch=()):
    args = [
        pltpu.with_memory_space_constraint(arg, pltpu.HBM)
        if specs and specs[at].memory_space == pltpu.HBM
        else arg
        for at, arg in enumerate(args)
    ]
    return pl.pallas_call(
        kernel,
        out_shape=outs,
        in_specs=specs or [vmem()] * len(args),
        out_specs=jax.tree.map(
            lambda out: pl.BlockSpec(memory_space=getattr(out, "memory_space", pltpu.VMEM)), outs
        ),
        scratch_shapes=scratch,
        compiler_params=pltpu.CompilerParams(vmem_limit_bytes=VMEM_LIMIT),
    )(*args)


def shape(*dims):
    return jax.ShapeDtypeStruct(dims, F32)


def column_block(source_ref, block, width, padded):
    wide = source_ref.shape[-1]
    window = min(padded + LANES, wide)
    start = block * width
    base = jnp.minimum(start // LANES * LANES, wide - window)
    part = source_ref[:, pl.ds(pl.multiple_of(base, LANES), window)]
    return pltpu.roll(part, (window - (start - base)) % window, 1)[:, :padded]


def rows_of(value):
    return lax.broadcasted_iota(jnp.int32, value.shape, 0)


def down(value, by):
    moved = pltpu.roll(value, by, 0)
    return jnp.where(rows_of(value) >= by, moved, 0.0)


def up(value, by):
    length = value.shape[0]
    moved = pltpu.roll(value, length - by, 0)
    return jnp.where(rows_of(value) < length - by, moved, 0.0)


def recur(value, powers, move):
    by = 1
    for power in powers:
        value = value + power * move(value, by)
        by *= 2
    return value


def forward_block(series, starts, history, poles, zeros, taps):
    length = series.shape[0]
    first = rows_of(series) == 0
    current, states = (series, [series[length - 1 :]])
    for section, (powers, zero) in enumerate(zip(poles, zeros)):
        if starts is None:
            driven = current - zero * down(current, 1)
        else:
            before = jnp.where(first, starts[section], pltpu.roll(current, 1, 0))
            driven = current - zero * before
            driven = driven + jnp.where(first, powers[0] * starts[section + 1], 0.0)
        current = recur(driven, powers, down)
        states.append(current[length - 1 :])
    reach = history.shape[0]
    extended = jnp.concatenate([history, current], axis=0)
    filtered = taps[0] * current
    for lag in range(1, len(taps)):
        filtered = filtered + taps[lag] * pltpu.roll(extended, lag, 0)[reach:]
    for back in range(1, reach):
        states.append(current[length - 1 - back : length - back])
    return (filtered, states)


def backward_block(filtered, ends, poles, zeros, taps):
    length = filtered.shape[0]
    reach = len(taps) - 1
    border = jnp.zeros((reach, LANES), F32)
    padded = jnp.concatenate([border, filtered, border], axis=0)
    total = padded.shape[0]
    spread = taps[0] * padded
    for lag in range(1, reach + 1):
        spread = spread + taps[lag] * pltpu.roll(padded, total - lag, 0)
    history = spread[:reach]
    current = spread[reach : reach + length]
    sections = len(poles)
    rows = rows_of(current)
    if ends is not None:
        for back in range(reach):
            current = current + jnp.where(rows == length - 1 - back, ends[sections + back], 0.0)
    states = [None] * (sections + reach)
    from_later = None
    for section in reversed(range(sections)):
        value = recur(current, poles[section], up)
        current = value - zeros[section] * up(value, 1)
        if ends is not None:
            current = current + jnp.where(rows == length - 1, ends[section], 0.0)
        to_output = poles[section][0] * value[:1]
        states[section + 1] = to_output if from_later is None else to_output + from_later
        from_later = -zeros[section] * value[:1]
    states[0] = from_later
    states[sections] = states[sections] + history[reach - 1 :]
    for back in range(1, reach):
        states[sections + back] = history[reach - 1 - back : reach - back]
    return (current, states)


def pack(states):
    rows = lax.broadcasted_iota(jnp.int32, (SLOT, LANES), 0)
    packed = jnp.zeros((SLOT, LANES), F32)
    for at, state in enumerate(states):
        packed = jnp.where(rows == at, state, packed)
    return packed


def rates_of(table, sections, taps_count, levels):
    rows = [table[at : at + 1] for at in range(sections * (levels + 1) + taps_count)]
    poles = [rows[at * levels : (at + 1) * levels] for at in range(sections)]
    zeros = rows[sections * levels : sections * (levels + 1)]
    return (poles, zeros, rows[sections * (levels + 1) :])


def predict_kernel(*refs):
    orders_hbm, lives_hbm, ratios_hbm, taps_hbm = refs[:4]
    residual_hbm, direction_hbm, diagonal_hbm, design_hbm = refs[4:8]
    predicted_ref, rates_ref, spread_ref, steps_ref, design_ref = refs[8:13]
    orders_ref, lives_ref, ratios_ref, taps_ref, remaining_ref, search_ref, diagonal_ref, sems = refs[13:]
    components = taps_ref.shape[0]
    length = design_ref.shape[0] // components
    copies = [
        pltpu.make_async_copy(source, target, sems.at[at])
        for at, (source, target) in enumerate(
            [
                (direction_hbm.at[:, 0, :], search_ref),
                (orders_hbm, orders_ref),
                (lives_hbm, lives_ref),
                (ratios_hbm, ratios_ref),
                (taps_hbm, taps_ref),
                (design_hbm, design_ref),
                (residual_hbm.at[:, 0, :], remaining_ref),
                (diagonal_hbm, diagonal_ref),
            ]
        )
    ]
    for copy in copies:
        copy.start()
    half = LANES // 2
    segments, sections_each, _ = lives_ref.shape
    sections = segments * sections_each
    taps_count = taps_ref.shape[1]
    for copy in copies[1:5]:
        copy.wait()
    lane = lax.broadcasted_iota(jnp.int32, (components, LANES), 1)
    component = lax.broadcasted_iota(jnp.int32, (components, LANES), 0)
    count = half // components
    spreader = jnp.where(lane % half // count == component, 1.0, 0.0)

    def over_lanes(rows):
        return jnp.dot(rows, spreader, precision=HIGHEST, preferred_element_type=F32)

    def flat(ref):
        return jnp.concatenate([ref[at] for at in range(segments)], axis=0)

    life = over_lanes(flat(lives_ref))
    ratio = over_lanes(flat(ratios_ref))
    orders = over_lanes(orders_ref[...].astype(F32))
    tap_rows = lax.dot_general(
        taps_ref[...], spreader, (((0,), (0,)), ((), ())), precision=HIGHEST,
        preferred_element_type=F32,
    )
    spare = jnp.concatenate(
        [orders[at : at + 1] - (each + 0.5) for at in range(segments) for each in range(sections_each)],
        axis=0,
    )
    active = spare > 0.0
    pole_all = jnp.exp(-1.0 / life)
    pole_rate = jnp.where(active, pole_all, 0.0)
    zero_rate = jnp.where(active, 1.0 - ratio * (1.0 - pole_all), 0.0)
    levels = length.bit_length() - 1
    power = pole_rate
    for level in range(levels):
        for section in range(sections):
            at = section * levels + level
            rates_ref[at : at + 1, :] = power[section : section + 1]
        power = power * power
    rates_ref[sections * levels : sections * (levels + 1), :] = zero_rate
    rates_ref[sections * (levels + 1) : sections * (levels + 1) + taps_count, :] = tap_rows

    reach = taps_count - 1
    kinds = sections + reach
    poles, zeros, taps = rates_of(rates_ref, sections, taps_count, length.bit_length() - 1)
    lane = lax.broadcasted_iota(jnp.int32, (1, LANES), 1)
    slot = jnp.where(lane >= half, lane % SLOT, SLOT)
    units = [jnp.where(slot == at, 1.0, 0.0) for at in range(kinds)]
    rows = lax.broadcasted_iota(jnp.int32, (reach, LANES), 0)
    history = jnp.where(slot == kinds - 1 - rows, 1.0, 0.0)
    nothing = jnp.zeros((length, LANES), F32)
    filtered, ends = forward_block(nothing, units[: sections + 1], history, poles, zeros, taps)
    local, heads = backward_block(filtered, None, poles, zeros, taps)
    reply, replies = backward_block(nothing, units, poles, zeros, taps)
    spread_ref[...] = jnp.where(lane < half, pltpu.roll(local, half, 1), reply)
    stacked = jnp.concatenate([pack(ends), pack(heads), pack(replies)], axis=0)
    source = lax.broadcasted_iota(jnp.int32, (LANES, kinds * LANES), 0)
    target = lax.broadcasted_iota(jnp.int32, (LANES, kinds * LANES), 1)
    within = target % LANES
    wanted = half + within // SLOT * SLOT + target // LANES
    pick = jnp.where((within < half) & (source == wanted), 1.0, 0.0)
    steps_ref[...] = jnp.dot(stacked, pick, precision=HIGHEST, preferred_element_type=F32)

    copies[0].wait()
    search = search_ref[...]
    high = search.astype(BF16)
    rest = search - high.astype(F32)
    middle = rest.astype(BF16)
    low = (rest - middle.astype(F32)).astype(BF16)
    split = jnp.concatenate([high, middle, low], axis=0)
    copies[5].wait()
    sums = lax.dot_general(
        design_ref[...], split, (((1,), (1,)), ((), ())), preferred_element_type=F32
    )
    pieces = [sums[at * length : (at + 1) * length] for at in range(components)]
    coarse = [piece[:, :count] for piece in pieces]
    fine = [piece[:, count : 2 * count] + piece[:, 2 * count :] for piece in pieces]
    predicted_ref[:length, :] = jnp.concatenate(coarse + fine, axis=1)
    for copy in copies[6:]:
        copy.wait()
    remaining = remaining_ref[...]
    energy = jnp.sum(remaining * diagonal_ref[...] * remaining, axis=1, keepdims=True)
    predicted_ref[length:, :] = jnp.broadcast_to(energy, (count, LANES))


def slices_kernel(width, first_bits, *refs):
    place_ref, vectors_hbm, diagonal_hbm = (refs[0], refs[1:4], refs[4])
    slices = refs[5:9]
    current_ref, remaining_ref, search_ref, diagonal_ref, sems = refs[9:]
    sources = [current_ref, remaining_ref, search_ref]
    copies = [
        pltpu.make_async_copy(vector.at[:, 0, :], target, sems.at[at])
        for at, (vector, target) in enumerate(zip(vectors_hbm, sources))
    ]
    copies.append(pltpu.make_async_copy(diagonal_hbm, diagonal_ref, sems.at[len(sources)]))
    for copy in copies:
        copy.start()
    for copy in copies:
        copy.wait()
    mine = place_ref[0]
    vectors = [diagonal_ref, remaining_ref, search_ref, current_ref]
    for source_ref, target_ref in zip(vectors, slices):
        for at in range(target_ref.shape[0]):
            block = mine if target_ref.shape[0] == 1 else at * first_bits + mine % first_bits
            part = column_block(source_ref, block, width, target_ref.shape[2])
            target_ref[at] = jnp.broadcast_to(part, target_ref.shape[1:])


def filter_kernel(sections, taps_count, length, parts, *refs):
    counts_ref, rates_ref = refs[:2]
    gathered = refs[2 : 2 + parts]
    send_ref, keep_ref, energy_ref = refs[2 + parts :]
    half = LANES // 2
    received = gathered[0][...]
    for other in gathered[1:]:
        received = received + other[...]
    energy_ref[...] = received[length:]
    received = received[:length]
    low_half = lax.broadcasted_iota(jnp.int32, (1, LANES), 1) < half
    data = jnp.where(low_half & (rows_of(received) < counts_ref[0]), received, 0.0)
    poles, zeros, taps = rates_of(rates_ref, sections, taps_count, length.bit_length() - 1)
    history = jnp.zeros((taps_count - 1, LANES), F32)
    filtered, ends = forward_block(data, None, history, poles, zeros, taps)
    local, heads = backward_block(filtered, None, poles, zeros, taps)
    sent = jnp.where(low_half, pack(ends), pltpu.roll(pack(heads), half, 1))
    for block in range(send_ref.shape[0]):
        send_ref[block] = sent
    keep_ref[...] = jnp.where(low_half, local, received + pltpu.roll(received, half, 1))


def normal_kernel(kinds, width, first_bits, *refs):
    place_ref, counts_ref, all_ref, keep_ref, spread_ref, steps_ref, design_ref = refs[:7]
    out_refs, (entering_ref, normal_ref) = (refs[7:-2], refs[-2:])
    blocks = all_ref.shape[0]
    mine = place_ref[0]
    half = LANES // 2

    def apply(which, state):
        total = None
        for at in range(kinds):
            column = steps_ref[which * SLOT : (which + 1) * SLOT, at * LANES : (at + 1) * LANES]
            term = column * state[at : at + 1]
            total = term if total is None else total + term
        return total

    def advance(block, state):
        entering_ref[block] = state
        return apply(0, state) + all_ref[block]

    def retreat(step, state):
        block = blocks - 1 - step
        later = apply(2, state) + (apply(1, entering_ref[block]) + pltpu.roll(all_ref[block], half, 1))
        return jnp.where(block > mine, later, state)

    empty = jnp.zeros((SLOT, LANES), F32)
    unroll = blocks if blocks <= 16 else 4
    lax.fori_loop(0, blocks, advance, empty, unroll=unroll)
    leaving = lax.fori_loop(0, blocks, retreat, empty, unroll=unroll)
    entering = entering_ref[mine]

    groups = half // SLOT
    row = lax.broadcasted_iota(jnp.int32, (half, LANES), 0)
    lane = lax.broadcasted_iota(jnp.int32, (half, LANES), 1)
    own = row // SLOT == lane // SLOT
    expanded = [
        jnp.where(own, jnp.concatenate([state] * groups, axis=0), 0.0)
        for state in (entering, leaving)
    ]
    correction = jnp.dot(
        spread_ref[...],
        jnp.concatenate(expanded, axis=0),
        precision=HIGHEST,
        preferred_element_type=F32,
    )
    kept = keep_ref[...]
    live = (row < counts_ref[0]) & (lane < half)
    weighted = jnp.where(live, kept + correction, 0.0)
    weighted = weighted.astype(BF16).astype(F32)
    product = weighted * pltpu.roll(kept, half, 1)
    turned = jnp.transpose(weighted)
    count = out_refs[0].shape[-2]
    low = jnp.concatenate(
        [turned[at * count : (at + 1) * count] for at in range(half // count)], axis=1
    ).astype(BF16)
    curve = lax.dot_general(
        product,
        jnp.ones((product.shape[0], LANES), F32),
        (((0,), (0,)), ((), ())),
        precision=HIGHEST,
        preferred_element_type=F32,
    )
    curvature = curve[:count]
    for at in range(1, half // count):
        curvature = curvature + curve[at * count : (at + 1) * count]
    normal_ref[...] = jnp.dot(low, design_ref[...], preferred_element_type=F32)
    padded = out_refs[0].shape[-1]
    column = lax.broadcasted_iota(jnp.int32, (count, padded), 1)
    curvature = jnp.broadcast_to(curvature[:, :1], (count, padded))
    low_bits = mine % first_bits
    for apart, out_ref in enumerate(out_refs):
        for at in range(out_ref.shape[0]):
            block = at * first_bits + (low_bits ^ apart)
            part = column_block(normal_ref, block, width, padded)
            out_ref[at] = jnp.where(column < width, part, curvature)


def update_kernel(width, first_bits, *refs):
    place_ref, held_ref, got_ref, energy_ref = refs[:4]
    remaining_ref, diagonal_ref, current_ref, search_ref = refs[4:8]
    next_ref, new_solution_ref, new_residual_ref, conditioned_ref, entering_ref = refs[8:]
    parts, count, padded = held_ref.shape
    column = lax.broadcasted_iota(jnp.int32, (count, padded), 1)
    at_curve = column == width
    normal = held_ref[0] + got_ref[0]
    curvature = jnp.sum(jnp.where(at_curve, normal, 0.0), axis=1, keepdims=True)
    step = energy_ref[:, :1] / curvature
    total = jnp.zeros((count, padded), F32)
    for at in range(parts):
        normal = held_ref[at] + got_ref[at]
        changed = remaining_ref[at] - step * normal
        scaled = diagonal_ref[at] * changed
        entering_ref[at] = changed
        total = total + jnp.where(column < width, changed * scaled, 0.0)
    share = jnp.sum(total, axis=1, keepdims=True)
    next_ref[...] = jnp.broadcast_to(share, next_ref.shape)
    own = place_ref[0] // first_bits
    changed = entering_ref[own]
    new_residual_ref[...] = changed
    conditioned_ref[...] = diagonal_ref[own] * changed
    new_solution_ref[...] = current_ref[0] + step * search_ref[0]


def exchange(value, axis, bit):
    size = lax.axis_size(axis)
    return lax.ppermute(value, axis, [(at, at ^ bit) for at in range(size)])


def over_order(value):
    if lax.axis_size("order") == 2:
        return [value, exchange(value, "order", 1)]
    return [lax.psum(value, "order")]


def shards(
    solution,
    residual,
    direction,
    precond,
    design,
    epoch_counts,
    segment_orders,
    pole_life,
    zero_ratio,
    fir_taps,
):
    count, _, wide = direction.shape
    components, length = design.shape[:2]
    sections = pole_life.shape[1] * pole_life.shape[2]
    taps_count = fir_taps.shape[1]
    kinds = sections + taps_count - 1
    blocks = lax.axis_size("tm")
    width = wide // blocks
    padded = (width // LANES + 1) * LANES
    bits = blocks.bit_length() - 1
    halved = bits // 2
    classes = 1 << halved
    parts = blocks // classes
    place = lax.axis_index("tm").astype(jnp.int32).reshape(1)
    levels = length.bit_length() - 1
    hbm = pl.BlockSpec(memory_space=pltpu.HBM)
    small = [
        segment_orders.T,
        jnp.transpose(pole_life, (1, 2, 0)),
        jnp.transpose(zero_ratio, (1, 2, 0)),
        fir_taps,
    ]

    predicted, rates, spread, steps, design_kept = call(
        predict_kernel,
        (
            shape(length + count, LANES),
            shape(sections * (levels + 1) + taps_count, LANES),
            shape(length, LANES),
            shape(3 * SLOT, kinds * LANES),
            jax.ShapeDtypeStruct((components * length, wide), BF16),
        ),
        *small,
        residual,
        direction,
        precond,
        design.reshape(components * length, wide),
        specs=[hbm] * 8,
        scratch=[pltpu.VMEM(each.shape, each.dtype) for each in small]
        + [pltpu.VMEM((count, wide), F32)] * 2
        + [pltpu.VMEM((1, wide), F32), pltpu.SemaphoreType.DMA((8,))],
    )
    arrived = over_order(predicted)
    send, keep, energy = call(
        functools.partial(filter_kernel, sections, taps_count, length, len(arrived)),
        (shape(blocks, SLOT, LANES), shape(length, LANES), shape(count, LANES)),
        epoch_counts,
        rates,
        *arrived,
        specs=[smem()] + [vmem()] * (1 + len(arrived)),
    )
    everyone = lax.all_to_all(send, "tm", 0, 0)
    pieces = call(
        functools.partial(normal_kernel, kinds, width, classes),
        [shape(parts, count, padded)] * classes,
        place,
        epoch_counts,
        everyone,
        keep,
        spread,
        steps,
        design_kept,
        specs=[smem()] * 2 + [vmem()] * 5,
        scratch=[pltpu.VMEM((blocks, SLOT, LANES), F32), pltpu.VMEM((count, wide), F32)],
    )
    diagonal_parts, remaining_parts, search_own, current_own = call(
        functools.partial(slices_kernel, width, classes),
        (
            shape(parts, count, padded),
            shape(parts, count, padded),
            shape(1, count, padded),
            shape(1, count, padded),
        ),
        place,
        solution,
        residual,
        direction,
        precond,
        specs=[smem()] + [hbm] * 4,
        scratch=[pltpu.VMEM((count, wide), F32)] * 3
        + [pltpu.VMEM((1, wide), F32), pltpu.SemaphoreType.DMA((4,))],
    )
    arriving = [exchange(pieces[apart], "tm", apart) for apart in range(1, classes)]
    buffer = pieces[0] + sum(arriving[1:], arriving[0])
    for bit in range(halved, bits - 1):
        buffer = buffer + exchange(buffer, "tm", (2 << bit) - classes)
    arriving = exchange(buffer, "tm", blocks - classes)
    share, new_solution, new_residual, conditioned = call(
        functools.partial(update_kernel, width, classes),
        (
            shape(count, LANES),
            shape(count, padded),
            shape(count, padded),
            shape(count, padded),
        ),
        place,
        buffer,
        arriving,
        energy,
        remaining_parts,
        diagonal_parts,
        current_own,
        search_own,
        specs=[smem()] + [vmem()] * 7,
        scratch=[pltpu.VMEM((parts, count, padded), F32)],
    )
    for bit in range(halved):
        share = share + exchange(share, "tm", 1 << bit)
    energy_next = sum(over_order(share))
    new_direction = conditioned + (energy_next / energy)[:, :1] * search_own[0]
    return tuple(
        vector[:, None, :width] for vector in (new_solution, new_residual, new_direction)
    )


def solution(mesh):
    placed = (
        P(None, "order", None),
        P(None, "order", None),
        P(None, "order", None),
        P("order", None),
        P(None, "tm", "order", None),
        P("tm"),
        P(),
        P(),
        P(),
        P(),
    )
    return jax.shard_map(
        shards,
        mesh=mesh,
        in_specs=placed,
        out_specs=(P(None, "order", "tm"), P(None, "order", "tm"), P(None, "order", "tm")),
        check_vma=False,
    )
```

```python
import functools

import jax
import jax.numpy as jnp
from jax import lax
from jax.experimental import pallas as pl
from jax.experimental.pallas import tpu as pltpu
from jax.sharding import PartitionSpec as P

HIGHEST = lax.Precision.HIGHEST
F32 = jnp.float32
BF16 = jnp.bfloat16
LANES = 128
SLOT = 16
VMEM_LIMIT = 16 * 1024 * 1024


def vmem():
    return pl.BlockSpec(memory_space=pltpu.VMEM)


def smem():
    return pl.BlockSpec(memory_space=pltpu.SMEM)


def call(kernel, outs, *args, specs=None, scratch=()):
    args = [
        pltpu.with_memory_space_constraint(arg, pltpu.HBM)
        if specs and specs[at].memory_space == pltpu.HBM
        else arg
        for at, arg in enumerate(args)
    ]
    return pl.pallas_call(
        kernel,
        out_shape=outs,
        in_specs=specs or [vmem()] * len(args),
        out_specs=jax.tree.map(
            lambda out: pl.BlockSpec(memory_space=getattr(out, "memory_space", pltpu.VMEM)), outs
        ),
        scratch_shapes=scratch,
        compiler_params=pltpu.CompilerParams(vmem_limit_bytes=VMEM_LIMIT),
    )(*args)


def shape(*dims):
    return jax.ShapeDtypeStruct(dims, F32)


def column_block(source_ref, block, width, padded):
    wide = source_ref.shape[-1]
    window = min(padded + LANES, wide)
    start = block * width
    base = jnp.minimum(start // LANES * LANES, wide - window)
    part = source_ref[:, pl.ds(pl.multiple_of(base, LANES), window)]
    return pltpu.roll(part, (window - (start - base)) % window, 1)[:, :padded]


def rows_of(value):
    return lax.broadcasted_iota(jnp.int32, value.shape, 0)


def down(value, by):
    moved = pltpu.roll(value, by, 0)
    return jnp.where(rows_of(value) >= by, moved, 0.0)


def up(value, by):
    length = value.shape[0]
    moved = pltpu.roll(value, length - by, 0)
    return jnp.where(rows_of(value) < length - by, moved, 0.0)


def recur(value, powers, move):
    by = 1
    for power in powers:
        value = value + power * move(value, by)
        by *= 2
    return value


def forward_block(series, starts, history, poles, zeros, taps):
    length = series.shape[0]
    first = rows_of(series) == 0
    current, states = (series, [series[length - 1 :]])
    for section, (powers, zero) in enumerate(zip(poles, zeros)):
        if starts is None:
            driven = current - zero * down(current, 1)
        else:
            before = jnp.where(first, starts[section], pltpu.roll(current, 1, 0))
            driven = current - zero * before
            driven = driven + jnp.where(first, powers[0] * starts[section + 1], 0.0)
        current = recur(driven, powers, down)
        states.append(current[length - 1 :])
    reach = history.shape[0]
    extended = jnp.concatenate([history, current], axis=0)
    filtered = taps[0] * current
    for lag in range(1, len(taps)):
        filtered = filtered + taps[lag] * pltpu.roll(extended, lag, 0)[reach:]
    for back in range(1, reach):
        states.append(current[length - 1 - back : length - back])
    return (filtered, states)


def backward_block(filtered, ends, poles, zeros, taps):
    length = filtered.shape[0]
    reach = len(taps) - 1
    border = jnp.zeros((reach, LANES), F32)
    padded = jnp.concatenate([border, filtered, border], axis=0)
    total = padded.shape[0]
    spread = taps[0] * padded
    for lag in range(1, reach + 1):
        spread = spread + taps[lag] * pltpu.roll(padded, total - lag, 0)
    history = spread[:reach]
    current = spread[reach : reach + length]
    sections = len(poles)
    rows = rows_of(current)
    if ends is not None:
        for back in range(reach):
            current = current + jnp.where(rows == length - 1 - back, ends[sections + back], 0.0)
    states = [None] * (sections + reach)
    from_later = None
    for section in reversed(range(sections)):
        value = recur(current, poles[section], up)
        current = value - zeros[section] * up(value, 1)
        if ends is not None:
            current = current + jnp.where(rows == length - 1, ends[section], 0.0)
        to_output = poles[section][0] * value[:1]
        states[section + 1] = to_output if from_later is None else to_output + from_later
        from_later = -zeros[section] * value[:1]
    states[0] = from_later
    states[sections] = states[sections] + history[reach - 1 :]
    for back in range(1, reach):
        states[sections + back] = history[reach - 1 - back : reach - back]
    return (current, states)


def pack(states):
    rows = lax.broadcasted_iota(jnp.int32, (SLOT, LANES), 0)
    packed = jnp.zeros((SLOT, LANES), F32)
    for at, state in enumerate(states):
        packed = jnp.where(rows == at, state, packed)
    return packed


def rates_of(table, sections, taps_count, levels):
    rows = [table[at : at + 1] for at in range(sections * (levels + 1) + taps_count)]
    poles = [rows[at * levels : (at + 1) * levels] for at in range(sections)]
    zeros = rows[sections * levels : sections * (levels + 1)]
    return (poles, zeros, rows[sections * (levels + 1) :])


def predict_kernel(*refs):
    _, *refs = refs
    orders_hbm, lives_hbm, ratios_hbm, taps_hbm = refs[:4]
    residual_hbm, direction_hbm, diagonal_hbm, design_hbm = refs[4:8]
    predicted_ref, rates_ref, spread_ref, steps_ref, design_ref = refs[8:13]
    orders_ref, lives_ref, ratios_ref, taps_ref, remaining_ref, search_ref, diagonal_ref, sems = refs[13:]
    components = taps_ref.shape[0]
    length = design_ref.shape[0] // components
    copies = [
        pltpu.make_async_copy(source, target, sems.at[at])
        for at, (source, target) in enumerate(
            [
                (direction_hbm.at[:, 0, :], search_ref),
                (orders_hbm, orders_ref),
                (lives_hbm, lives_ref),
                (ratios_hbm, ratios_ref),
                (taps_hbm, taps_ref),
                (design_hbm, design_ref),
                (residual_hbm.at[:, 0, :], remaining_ref),
                (diagonal_hbm, diagonal_ref),
            ]
        )
    ]
    for copy in copies:
        copy.start()
    half = LANES // 2
    segments, sections_each, _ = lives_ref.shape
    sections = segments * sections_each
    taps_count = taps_ref.shape[1]
    for copy in copies[1:5]:
        copy.wait()
    lane = lax.broadcasted_iota(jnp.int32, (components, LANES), 1)
    component = lax.broadcasted_iota(jnp.int32, (components, LANES), 0)
    count = half // components
    spreader = jnp.where(lane % half // count == component, 1.0, 0.0)

    def over_lanes(rows):
        return jnp.dot(rows, spreader, precision=HIGHEST, preferred_element_type=F32)

    def flat(ref):
        return jnp.concatenate([ref[at] for at in range(segments)], axis=0)

    life = over_lanes(flat(lives_ref))
    ratio = over_lanes(flat(ratios_ref))
    orders = over_lanes(orders_ref[...].astype(F32))
    tap_rows = lax.dot_general(
        taps_ref[...], spreader, (((0,), (0,)), ((), ())), precision=HIGHEST,
        preferred_element_type=F32,
    )
    spare = jnp.concatenate(
        [orders[at : at + 1] - (each + 0.5) for at in range(segments) for each in range(sections_each)],
        axis=0,
    )
    active = spare > 0.0
    pole_all = jnp.exp(-1.0 / life)
    pole_rate = jnp.where(active, pole_all, 0.0)
    zero_rate = jnp.where(active, 1.0 - ratio * (1.0 - pole_all), 0.0)
    levels = length.bit_length() - 1
    power = pole_rate
    for level in range(levels):
        for section in range(sections):
            at = section * levels + level
            rates_ref[at : at + 1, :] = power[section : section + 1]
        power = power * power
    rates_ref[sections * levels : sections * (levels + 1), :] = zero_rate
    rates_ref[sections * (levels + 1) : sections * (levels + 1) + taps_count, :] = tap_rows

    reach = taps_count - 1
    kinds = sections + reach
    poles, zeros, taps = rates_of(rates_ref, sections, taps_count, length.bit_length() - 1)
    lane = lax.broadcasted_iota(jnp.int32, (1, LANES), 1)
    slot = jnp.where(lane >= half, lane % SLOT, SLOT)
    units = [jnp.where(slot == at, 1.0, 0.0) for at in range(kinds)]
    rows = lax.broadcasted_iota(jnp.int32, (reach, LANES), 0)
    history = jnp.where(slot == kinds - 1 - rows, 1.0, 0.0)
    nothing = jnp.zeros((length, LANES), F32)
    filtered, ends = forward_block(nothing, units[: sections + 1], history, poles, zeros, taps)
    local, heads = backward_block(filtered, None, poles, zeros, taps)
    reply, replies = backward_block(nothing, units, poles, zeros, taps)
    spread_ref[...] = jnp.where(lane < half, pltpu.roll(local, half, 1), reply)
    stacked = jnp.concatenate([pack(ends), pack(heads), pack(replies)], axis=0)
    source = lax.broadcasted_iota(jnp.int32, (LANES, kinds * LANES), 0)
    target = lax.broadcasted_iota(jnp.int32, (LANES, kinds * LANES), 1)
    within = target % LANES
    wanted = half + within // SLOT * SLOT + target // LANES
    pick = jnp.where((within < half) & (source == wanted), 1.0, 0.0)
    steps_ref[...] = jnp.dot(stacked, pick, precision=HIGHEST, preferred_element_type=F32)

    copies[0].wait()
    search = search_ref[...]
    high = search.astype(BF16)
    rest = search - high.astype(F32)
    middle = rest.astype(BF16)
    low = (rest - middle.astype(F32)).astype(BF16)
    split = jnp.concatenate([high, middle, low], axis=0)
    copies[5].wait()
    sums = lax.dot_general(
        design_ref[...], split, (((1,), (1,)), ((), ())), preferred_element_type=F32
    )
    pieces = [sums[at * length : (at + 1) * length] for at in range(components)]
    coarse = [piece[:, :count] for piece in pieces]
    fine = [piece[:, count : 2 * count] + piece[:, 2 * count :] for piece in pieces]
    predicted_ref[:length, :] = jnp.concatenate(coarse + fine, axis=1)
    for copy in copies[6:]:
        copy.wait()
    remaining = remaining_ref[...]
    energy = jnp.sum(remaining * diagonal_ref[...] * remaining, axis=1, keepdims=True)
    predicted_ref[length:, :] = jnp.broadcast_to(energy, (count, LANES))


def slices_kernel(width, first_bits, *refs):
    place_ref, vectors_hbm, diagonal_hbm = (refs[0], refs[1:4], refs[4])
    slices = refs[5:9]
    current_ref, remaining_ref, search_ref, diagonal_ref, sems = refs[9:]
    sources = [current_ref, remaining_ref, search_ref]
    copies = [
        pltpu.make_async_copy(vector.at[:, 0, :], target, sems.at[at])
        for at, (vector, target) in enumerate(zip(vectors_hbm, sources))
    ]
    copies.append(pltpu.make_async_copy(diagonal_hbm, diagonal_ref, sems.at[len(sources)]))
    for copy in copies:
        copy.start()
    for copy in copies:
        copy.wait()
    mine = place_ref[0]
    vectors = [diagonal_ref, remaining_ref, search_ref, current_ref]
    for source_ref, target_ref in zip(vectors, slices):
        for at in range(target_ref.shape[0]):
            block = mine if target_ref.shape[0] == 1 else at * first_bits + mine % first_bits
            part = column_block(source_ref, block, width, target_ref.shape[2])
            target_ref[at] = jnp.broadcast_to(part, target_ref.shape[1:])


def filter_kernel(sections, taps_count, length, parts, *refs):
    counts_ref, rates_ref = refs[:2]
    gathered = refs[2 : 2 + parts]
    send_ref, keep_ref, energy_ref = refs[2 + parts :]
    half = LANES // 2
    received = gathered[0][...]
    for other in gathered[1:]:
        received = received + other[...]
    energy_ref[...] = received[length:]
    received = received[:length]
    low_half = lax.broadcasted_iota(jnp.int32, (1, LANES), 1) < half
    data = jnp.where(low_half & (rows_of(received) < counts_ref[0]), received, 0.0)
    poles, zeros, taps = rates_of(rates_ref, sections, taps_count, length.bit_length() - 1)
    history = jnp.zeros((taps_count - 1, LANES), F32)
    filtered, ends = forward_block(data, None, history, poles, zeros, taps)
    local, heads = backward_block(filtered, None, poles, zeros, taps)
    sent = jnp.where(low_half, pack(ends), pltpu.roll(pack(heads), half, 1))
    for block in range(send_ref.shape[0]):
        send_ref[block] = sent
    keep_ref[...] = jnp.where(low_half, local, received + pltpu.roll(received, half, 1))


def normal_kernel(kinds, width, first_bits, *refs):
    place_ref, counts_ref, all_ref, keep_ref, spread_ref, steps_ref, design_ref = refs[:7]
    out_refs, (entering_ref, normal_ref) = (refs[7:-2], refs[-2:])
    blocks = all_ref.shape[0]
    mine = place_ref[0]
    half = LANES // 2

    def apply(which, state):
        total = None
        for at in range(kinds):
            column = steps_ref[which * SLOT : (which + 1) * SLOT, at * LANES : (at + 1) * LANES]
            term = column * state[at : at + 1]
            total = term if total is None else total + term
        return total

    def advance(block, state):
        entering_ref[block] = state
        return apply(0, state) + all_ref[block]

    def retreat(step, state):
        block = blocks - 1 - step
        later = apply(2, state) + (apply(1, entering_ref[block]) + pltpu.roll(all_ref[block], half, 1))
        return jnp.where(block > mine, later, state)

    empty = jnp.zeros((SLOT, LANES), F32)
    unroll = blocks if blocks <= 16 else 4
    lax.fori_loop(0, blocks, advance, empty, unroll=unroll)
    leaving = lax.fori_loop(0, blocks, retreat, empty, unroll=unroll)
    entering = entering_ref[mine]

    groups = half // SLOT
    row = lax.broadcasted_iota(jnp.int32, (half, LANES), 0)
    lane = lax.broadcasted_iota(jnp.int32, (half, LANES), 1)
    own = row // SLOT == lane // SLOT
    expanded = [
        jnp.where(own, jnp.concatenate([state] * groups, axis=0), 0.0)
        for state in (entering, leaving)
    ]
    correction = jnp.dot(
        spread_ref[...],
        jnp.concatenate(expanded, axis=0),
        precision=HIGHEST,
        preferred_element_type=F32,
    )
    kept = keep_ref[...]
    live = (row < counts_ref[0]) & (lane < half)
    weighted = jnp.where(live, kept + correction, 0.0)
    weighted = weighted.astype(BF16).astype(F32)
    product = weighted * pltpu.roll(kept, half, 1)
    turned = jnp.transpose(weighted)
    count = out_refs[0].shape[-2]
    low = jnp.concatenate(
        [turned[at * count : (at + 1) * count] for at in range(half // count)], axis=1
    ).astype(BF16)
    curve = lax.dot_general(
        product,
        jnp.ones((product.shape[0], LANES), F32),
        (((0,), (0,)), ((), ())),
        precision=HIGHEST,
        preferred_element_type=F32,
    )
    curvature = curve[:count]
    for at in range(1, half // count):
        curvature = curvature + curve[at * count : (at + 1) * count]
    normal_ref[...] = jnp.dot(low, design_ref[...], preferred_element_type=F32)
    padded = out_refs[0].shape[-1]
    column = lax.broadcasted_iota(jnp.int32, (count, padded), 1)
    curvature = jnp.broadcast_to(curvature[:, :1], (count, padded))
    low_bits = mine % first_bits
    for apart, out_ref in enumerate(out_refs):
        for at in range(out_ref.shape[0]):
            block = at * first_bits + (low_bits ^ apart)
            part = column_block(normal_ref, block, width, padded)
            out_ref[at] = jnp.where(column < width, part, curvature)


def update_kernel(width, first_bits, *refs):
    place_ref, held_ref, got_ref, energy_ref = refs[:4]
    remaining_ref, diagonal_ref, current_ref, search_ref = refs[4:8]
    next_ref, new_solution_ref, new_residual_ref, conditioned_ref, entering_ref = refs[8:]
    parts, count, padded = held_ref.shape
    column = lax.broadcasted_iota(jnp.int32, (count, padded), 1)
    at_curve = column == width
    normal = held_ref[0] + got_ref[0]
    curvature = jnp.sum(jnp.where(at_curve, normal, 0.0), axis=1, keepdims=True)
    step = energy_ref[:, :1] / curvature
    total = jnp.zeros((count, padded), F32)
    for at in range(parts):
        normal = held_ref[at] + got_ref[at]
        changed = remaining_ref[at] - step * normal
        scaled = diagonal_ref[at] * changed
        entering_ref[at] = changed
        total = total + jnp.where(column < width, changed * scaled, 0.0)
    share = jnp.sum(total, axis=1, keepdims=True)
    next_ref[...] = jnp.broadcast_to(share, next_ref.shape)
    own = place_ref[0] // first_bits
    changed = entering_ref[own]
    new_residual_ref[...] = changed
    conditioned_ref[...] = diagonal_ref[own] * changed
    new_solution_ref[...] = current_ref[0] + step * search_ref[0]


def exchange(value, axis, bit):
    size = lax.axis_size(axis)
    return lax.ppermute(value, axis, [(at, at ^ bit) for at in range(size)])


def over_order(value):
    if lax.axis_size("order") == 2:
        return [value, exchange(value, "order", 1)]
    return [lax.psum(value, "order")]


def shards(
    solution,
    residual,
    direction,
    precond,
    design,
    epoch_counts,
    segment_orders,
    pole_life,
    zero_ratio,
    fir_taps,
):
    count, _, wide = direction.shape
    components, length = design.shape[:2]
    sections = pole_life.shape[1] * pole_life.shape[2]
    taps_count = fir_taps.shape[1]
    kinds = sections + taps_count - 1
    blocks = lax.axis_size("tm")
    width = wide // blocks
    padded = (width // LANES + 1) * LANES
    bits = blocks.bit_length() - 1
    halved = bits // 2
    classes = 1 << halved
    parts = blocks // classes
    place = lax.axis_index("tm").astype(jnp.int32).reshape(1)
    levels = length.bit_length() - 1
    hbm = pl.BlockSpec(memory_space=pltpu.HBM)
    small = [
        segment_orders.T,
        jnp.transpose(pole_life, (1, 2, 0)),
        jnp.transpose(zero_ratio, (1, 2, 0)),
        fir_taps,
    ]

    predicted, rates, spread, steps, design_kept = call(
        predict_kernel,
        (
            shape(length + count, LANES),
            shape(sections * (levels + 1) + taps_count, LANES),
            shape(length, LANES),
            shape(3 * SLOT, kinds * LANES),
            jax.ShapeDtypeStruct((components * length, wide), BF16),
        ),
        place,
        *small,
        residual,
        direction,
        precond,
        design.reshape(components * length, wide),
        specs=[smem()] + [hbm] * 8,
        scratch=[pltpu.VMEM(each.shape, each.dtype) for each in small]
        + [pltpu.VMEM((count, wide), F32)] * 2
        + [pltpu.VMEM((1, wide), F32), pltpu.SemaphoreType.DMA((8,))],
    )
    arrived = over_order(predicted)
    send, keep, energy = call(
        functools.partial(filter_kernel, sections, taps_count, length, len(arrived)),
        (shape(blocks, SLOT, LANES), shape(length, LANES), shape(count, LANES)),
        epoch_counts,
        rates,
        *arrived,
        specs=[smem()] + [vmem()] * (1 + len(arrived)),
    )
    everyone = lax.all_to_all(send, "tm", 0, 0)
    pieces = call(
        functools.partial(normal_kernel, kinds, width, classes),
        [shape(parts, count, padded)] * classes,
        place,
        epoch_counts,
        everyone,
        keep,
        spread,
        steps,
        design_kept,
        specs=[smem()] * 2 + [vmem()] * 5,
        scratch=[pltpu.VMEM((blocks, SLOT, LANES), F32), pltpu.VMEM((count, wide), F32)],
    )
    diagonal_parts, remaining_parts, search_own, current_own = call(
        functools.partial(slices_kernel, width, classes),
        (
            shape(parts, count, padded),
            shape(parts, count, padded),
            shape(1, count, padded),
            shape(1, count, padded),
        ),
        place,
        solution,
        residual,
        direction,
        precond,
        specs=[smem()] + [hbm] * 4,
        scratch=[pltpu.VMEM((count, wide), F32)] * 3
        + [pltpu.VMEM((1, wide), F32), pltpu.SemaphoreType.DMA((4,))],
    )
    arriving = [exchange(pieces[apart], "tm", apart) for apart in range(1, classes)]
    buffer = pieces[0] + sum(arriving[1:], arriving[0])
    for bit in range(halved, bits - 1):
        buffer = buffer + exchange(buffer, "tm", 1 << bit)
    arriving = exchange(buffer, "tm", 1 << bits - 1)
    share, new_solution, new_residual, conditioned = call(
        functools.partial(update_kernel, width, classes),
        (
            shape(count, LANES),
            shape(count, padded),
            shape(count, padded),
            shape(count, padded),
        ),
        place,
        buffer,
        arriving,
        energy,
        remaining_parts,
        diagonal_parts,
        current_own,
        search_own,
        specs=[smem()] + [vmem()] * 7,
        scratch=[pltpu.VMEM((parts, count, padded), F32)],
    )
    for bit in range(halved):
        share = share + exchange(share, "tm", 1 << bit)
    energy_next = sum(over_order(share))
    new_direction = conditioned + (energy_next / energy)[:, :1] * search_own[0]
    return tuple(
        vector[:, None, :width] for vector in (new_solution, new_residual, new_direction)
    )


def solution(mesh):
    placed = (
        P(None, "order", None),
        P(None, "order", None),
        P(None, "order", None),
        P("order", None),
        P(None, "tm", "order", None),
        P("tm"),
        P(),
        P(),
        P(),
        P(),
    )
    return jax.shard_map(
        shards,
        mesh=mesh,
        in_specs=placed,
        out_specs=(P(None, "order", "tm"), P(None, "order", "tm"), P(None, "order", "tm")),
        check_vma=False,
    )
```

```python
import functools

import jax
import jax.numpy as jnp
from jax import lax
from jax.experimental import pallas as pl
from jax.experimental.pallas import tpu as pltpu
from jax.sharding import PartitionSpec as P

HIGHEST = lax.Precision.HIGHEST
F32 = jnp.float32
BF16 = jnp.bfloat16
LANES = 128
SLOT = 16
VMEM_LIMIT = 16 * 1024 * 1024


def vmem():
    return pl.BlockSpec(memory_space=pltpu.VMEM)


def smem():
    return pl.BlockSpec(memory_space=pltpu.SMEM)


def call(kernel, outs, *args, specs=None, scratch=()):
    args = [
        pltpu.with_memory_space_constraint(arg, pltpu.HBM)
        if specs and specs[at].memory_space == pltpu.HBM
        else arg
        for at, arg in enumerate(args)
    ]
    return pl.pallas_call(
        kernel,
        out_shape=outs,
        in_specs=specs or [vmem()] * len(args),
        out_specs=jax.tree.map(
            lambda out: pl.BlockSpec(memory_space=getattr(out, "memory_space", pltpu.VMEM)), outs
        ),
        scratch_shapes=scratch,
        compiler_params=pltpu.CompilerParams(vmem_limit_bytes=VMEM_LIMIT),
    )(*args)


def shape(*dims):
    return jax.ShapeDtypeStruct(dims, F32)


def column_block(source_ref, block, width, padded):
    wide = source_ref.shape[-1]
    window = min(padded + LANES, wide)
    start = block * width
    base = jnp.minimum(start // LANES * LANES, wide - window)
    part = source_ref[:, pl.ds(pl.multiple_of(base, LANES), window)]
    return pltpu.roll(part, (window - (start - base)) % window, 1)[:, :padded]


def rows_of(value):
    return lax.broadcasted_iota(jnp.int32, value.shape, 0)


def down(value, by):
    moved = pltpu.roll(value, by, 0)
    return jnp.where(rows_of(value) >= by, moved, 0.0)


def up(value, by):
    length = value.shape[0]
    moved = pltpu.roll(value, length - by, 0)
    return jnp.where(rows_of(value) < length - by, moved, 0.0)


def recur(value, powers, move):
    by = 1
    for power in powers:
        value = value + power * move(value, by)
        by *= 2
    return value


def forward_block(series, starts, history, poles, zeros, taps):
    length = series.shape[0]
    first = rows_of(series) == 0
    current, states = (series, [series[length - 1 :]])
    for section, (powers, zero) in enumerate(zip(poles, zeros)):
        if starts is None:
            driven = current - zero * down(current, 1)
        else:
            before = jnp.where(first, starts[section], pltpu.roll(current, 1, 0))
            driven = current - zero * before
            driven = driven + jnp.where(first, powers[0] * starts[section + 1], 0.0)
        current = recur(driven, powers, down)
        states.append(current[length - 1 :])
    reach = history.shape[0]
    extended = jnp.concatenate([history, current], axis=0)
    filtered = taps[0] * current
    for lag in range(1, len(taps)):
        filtered = filtered + taps[lag] * pltpu.roll(extended, lag, 0)[reach:]
    for back in range(1, reach):
        states.append(current[length - 1 - back : length - back])
    return (filtered, states)


def backward_block(filtered, ends, poles, zeros, taps):
    length = filtered.shape[0]
    reach = len(taps) - 1
    border = jnp.zeros((reach, LANES), F32)
    padded = jnp.concatenate([border, filtered, border], axis=0)
    total = padded.shape[0]
    spread = taps[0] * padded
    for lag in range(1, reach + 1):
        spread = spread + taps[lag] * pltpu.roll(padded, total - lag, 0)
    history = spread[:reach]
    current = spread[reach : reach + length]
    sections = len(poles)
    rows = rows_of(current)
    if ends is not None:
        for back in range(reach):
            current = current + jnp.where(rows == length - 1 - back, ends[sections + back], 0.0)
    states = [None] * (sections + reach)
    from_later = None
    for section in reversed(range(sections)):
        value = recur(current, poles[section], up)
        current = value - zeros[section] * up(value, 1)
        if ends is not None:
            current = current + jnp.where(rows == length - 1, ends[section], 0.0)
        to_output = poles[section][0] * value[:1]
        states[section + 1] = to_output if from_later is None else to_output + from_later
        from_later = -zeros[section] * value[:1]
    states[0] = from_later
    states[sections] = states[sections] + history[reach - 1 :]
    for back in range(1, reach):
        states[sections + back] = history[reach - 1 - back : reach - back]
    return (current, states)


def pack(states):
    rows = lax.broadcasted_iota(jnp.int32, (SLOT, LANES), 0)
    packed = jnp.zeros((SLOT, LANES), F32)
    for at, state in enumerate(states):
        packed = jnp.where(rows == at, state, packed)
    return packed


def rates_of(table, sections, taps_count, levels):
    rows = [table[at : at + 1] for at in range(sections * (levels + 1) + taps_count)]
    poles = [rows[at * levels : (at + 1) * levels] for at in range(sections)]
    zeros = rows[sections * levels : sections * (levels + 1)]
    return (poles, zeros, rows[sections * (levels + 1) :])


def predict_kernel(*refs):
    _, *refs = refs
    orders_hbm, lives_hbm, ratios_hbm, taps_hbm = refs[:4]
    residual_hbm, direction_hbm, diagonal_hbm, design_hbm = refs[4:8]
    predicted_ref, rates_ref, spread_ref, steps_ref, design_ref = refs[8:13]
    orders_ref, lives_ref, ratios_ref, taps_ref, remaining_ref, search_ref, diagonal_ref, sems = refs[13:]
    components = taps_ref.shape[0]
    length = design_ref.shape[0] // components
    copies = [
        pltpu.make_async_copy(source, target, sems.at[at])
        for at, (source, target) in enumerate(
            [
                (direction_hbm.at[:, 0, :], search_ref),
                (orders_hbm, orders_ref),
                (lives_hbm, lives_ref),
                (ratios_hbm, ratios_ref),
                (taps_hbm, taps_ref),
                (design_hbm, design_ref),
                (residual_hbm.at[:, 0, :], remaining_ref),
                (diagonal_hbm, diagonal_ref),
            ]
        )
    ]
    for copy in copies:
        copy.start()
    half = LANES // 2
    segments, sections_each, _ = lives_ref.shape
    sections = segments * sections_each
    taps_count = taps_ref.shape[1]
    for copy in copies[1:5]:
        copy.wait()
    lane = lax.broadcasted_iota(jnp.int32, (components, LANES), 1)
    component = lax.broadcasted_iota(jnp.int32, (components, LANES), 0)
    count = half // components
    spreader = jnp.where(lane % half // count == component, 1.0, 0.0)

    def over_lanes(rows):
        return jnp.dot(rows, spreader, precision=HIGHEST, preferred_element_type=F32)

    def flat(ref):
        return jnp.concatenate([ref[at] for at in range(segments)], axis=0)

    life = over_lanes(flat(lives_ref))
    ratio = over_lanes(flat(ratios_ref))
    orders = over_lanes(orders_ref[...].astype(F32))
    tap_rows = lax.dot_general(
        taps_ref[...], spreader, (((0,), (0,)), ((), ())), precision=HIGHEST,
        preferred_element_type=F32,
    )
    spare = jnp.concatenate(
        [orders[at : at + 1] - (each + 0.5) for at in range(segments) for each in range(sections_each)],
        axis=0,
    )
    active = spare > 0.0
    pole_all = jnp.exp(-1.0 / life)
    pole_rate = jnp.where(active, pole_all, 0.0)
    zero_rate = jnp.where(active, 1.0 - ratio * (1.0 - pole_all), 0.0)
    levels = length.bit_length() - 1
    power = pole_rate
    for level in range(levels):
        for section in range(sections):
            at = section * levels + level
            rates_ref[at : at + 1, :] = power[section : section + 1]
        power = power * power
    rates_ref[sections * levels : sections * (levels + 1), :] = zero_rate
    rates_ref[sections * (levels + 1) : sections * (levels + 1) + taps_count, :] = tap_rows

    reach = taps_count - 1
    kinds = sections + reach
    poles, zeros, taps = rates_of(rates_ref, sections, taps_count, length.bit_length() - 1)
    lane = lax.broadcasted_iota(jnp.int32, (1, LANES), 1)
    slot = jnp.where(lane >= half, lane % SLOT, SLOT)
    units = [jnp.where(slot == at, 1.0, 0.0) for at in range(kinds)]
    rows = lax.broadcasted_iota(jnp.int32, (reach, LANES), 0)
    history = jnp.where(slot == kinds - 1 - rows, 1.0, 0.0)
    nothing = jnp.zeros((length, LANES), F32)
    filtered, ends = forward_block(nothing, units[: sections + 1], history, poles, zeros, taps)
    local, heads = backward_block(filtered, None, poles, zeros, taps)
    reply, replies = backward_block(nothing, units, poles, zeros, taps)
    spread_ref[...] = jnp.where(lane < half, pltpu.roll(local, half, 1), reply)
    stacked = jnp.concatenate([pack(ends), pack(heads), pack(replies)], axis=0)
    source = lax.broadcasted_iota(jnp.int32, (LANES, kinds * LANES), 0)
    target = lax.broadcasted_iota(jnp.int32, (LANES, kinds * LANES), 1)
    within = target % LANES
    wanted = half + within // SLOT * SLOT + target // LANES
    pick = jnp.where((within < half) & (source == wanted), 1.0, 0.0)
    steps_ref[...] = jnp.dot(stacked, pick, precision=HIGHEST, preferred_element_type=F32)

    copies[0].wait()
    search = search_ref[...]
    high = search.astype(BF16)
    rest = search - high.astype(F32)
    middle = rest.astype(BF16)
    low = (rest - middle.astype(F32)).astype(BF16)
    split = jnp.concatenate([high, middle, low], axis=0)
    copies[5].wait()
    sums = lax.dot_general(
        design_ref[...], split, (((1,), (1,)), ((), ())), preferred_element_type=F32
    )
    pieces = [sums[at * length : (at + 1) * length] for at in range(components)]
    coarse = [piece[:, :count] for piece in pieces]
    fine = [piece[:, count : 2 * count] + piece[:, 2 * count :] for piece in pieces]
    predicted_ref[:length, :] = jnp.concatenate(coarse + fine, axis=1)
    for copy in copies[6:]:
        copy.wait()
    remaining = remaining_ref[...]
    energy = jnp.sum(remaining * diagonal_ref[...] * remaining, axis=1, keepdims=True)
    predicted_ref[length:, :] = jnp.broadcast_to(energy, (count, LANES))


def slices_kernel(width, first_bits, *refs):
    place_ref, vectors_hbm, diagonal_hbm = (refs[0], refs[1:4], refs[4])
    slices = refs[5:9]
    current_ref, remaining_ref, search_ref, diagonal_ref, sems = refs[9:]
    sources = [current_ref, remaining_ref, search_ref]
    copies = [
        pltpu.make_async_copy(vector.at[:, 0, :], target, sems.at[at])
        for at, (vector, target) in enumerate(zip(vectors_hbm, sources))
    ]
    copies.append(pltpu.make_async_copy(diagonal_hbm, diagonal_ref, sems.at[len(sources)]))
    for copy in copies:
        copy.start()
    for copy in copies:
        copy.wait()
    mine = place_ref[0]
    vectors = [diagonal_ref, remaining_ref, search_ref, current_ref]
    for source_ref, target_ref in zip(vectors, slices):
        for at in range(target_ref.shape[0]):
            block = mine if target_ref.shape[0] == 1 else at * first_bits + mine % first_bits
            part = column_block(source_ref, block, width, target_ref.shape[2])
            target_ref[at] = jnp.broadcast_to(part, target_ref.shape[1:])


def filter_kernel(sections, taps_count, length, parts, *refs):
    counts_ref, rates_ref = refs[:2]
    gathered = refs[2 : 2 + parts]
    send_ref, keep_ref, energy_ref = refs[2 + parts :]
    half = LANES // 2
    received = gathered[0][...]
    for other in gathered[1:]:
        received = received + other[...]
    energy_ref[...] = received[length:]
    received = received[:length]
    low_half = lax.broadcasted_iota(jnp.int32, (1, LANES), 1) < half
    data = jnp.where(low_half & (rows_of(received) < counts_ref[0]), received, 0.0)
    poles, zeros, taps = rates_of(rates_ref, sections, taps_count, length.bit_length() - 1)
    history = jnp.zeros((taps_count - 1, LANES), F32)
    filtered, ends = forward_block(data, None, history, poles, zeros, taps)
    local, heads = backward_block(filtered, None, poles, zeros, taps)
    sent = jnp.where(low_half, pack(ends), pltpu.roll(pack(heads), half, 1))
    for block in range(send_ref.shape[0]):
        send_ref[block] = sent
    keep_ref[...] = jnp.where(low_half, local, received + pltpu.roll(received, half, 1))


def normal_kernel(kinds, width, first_bits, *refs):
    place_ref, counts_ref, all_ref, keep_ref, spread_ref, steps_ref, design_ref = refs[:7]
    out_refs, (entering_ref, normal_ref) = (refs[7:-2], refs[-2:])
    blocks = all_ref.shape[0]
    mine = place_ref[0]
    half = LANES // 2

    def apply(which, state):
        total = None
        for at in range(kinds):
            column = steps_ref[which * SLOT : (which + 1) * SLOT, at * LANES : (at + 1) * LANES]
            term = column * state[at : at + 1]
            total = term if total is None else total + term
        return total

    def advance(block, state):
        entering_ref[block] = state
        return apply(0, state) + all_ref[block]

    def retreat(step, state):
        block = blocks - 1 - step
        later = apply(2, state) + (apply(1, entering_ref[block]) + pltpu.roll(all_ref[block], half, 1))
        return jnp.where(block > mine, later, state)

    empty = jnp.zeros((SLOT, LANES), F32)
    unroll = blocks if blocks <= 16 else 4
    lax.fori_loop(0, blocks, advance, empty, unroll=unroll)
    leaving = lax.fori_loop(0, blocks, retreat, empty, unroll=unroll)
    entering = entering_ref[mine]

    groups = half // SLOT
    row = lax.broadcasted_iota(jnp.int32, (half, LANES), 0)
    lane = lax.broadcasted_iota(jnp.int32, (half, LANES), 1)
    own = row // SLOT == lane // SLOT
    expanded = [
        jnp.where(own, jnp.concatenate([state] * groups, axis=0), 0.0)
        for state in (entering, leaving)
    ]
    correction = jnp.dot(
        spread_ref[...],
        jnp.concatenate(expanded, axis=0),
        precision=HIGHEST,
        preferred_element_type=F32,
    )
    kept = keep_ref[...]
    live = (row < counts_ref[0]) & (lane < half)
    weighted = jnp.where(live, kept + correction, 0.0)
    weighted = weighted.astype(BF16).astype(F32)
    product = weighted * pltpu.roll(kept, half, 1)
    turned = jnp.transpose(weighted)
    count = out_refs[0].shape[-2]
    low = jnp.concatenate(
        [turned[at * count : (at + 1) * count] for at in range(half // count)], axis=1
    ).astype(BF16)
    along = jnp.sum(product, axis=0, keepdims=True)
    total = along
    for at in range(1, half // count):
        total = total + pltpu.roll(along, LANES - at * count, 1)
    row = lax.broadcasted_iota(jnp.int32, (count, LANES), 0)
    lane = lax.broadcasted_iota(jnp.int32, (count, LANES), 1)
    curvature = jnp.sum(jnp.where(row == lane, total, 0.0), axis=1, keepdims=True)
    normal_ref[...] = jnp.dot(low, design_ref[...], preferred_element_type=F32)
    padded = out_refs[0].shape[-1]
    column = lax.broadcasted_iota(jnp.int32, (count, padded), 1)
    curvature = jnp.broadcast_to(curvature, (count, padded))
    low_bits = mine % first_bits
    for apart, out_ref in enumerate(out_refs):
        for at in range(out_ref.shape[0]):
            block = at * first_bits + (low_bits ^ apart)
            part = column_block(normal_ref, block, width, padded)
            out_ref[at] = jnp.where(column < width, part, curvature)


def update_kernel(width, first_bits, *refs):
    place_ref, held_ref, got_ref, energy_ref = refs[:4]
    remaining_ref, diagonal_ref, current_ref, search_ref = refs[4:8]
    next_ref, new_solution_ref, new_residual_ref, conditioned_ref, entering_ref = refs[8:]
    parts, count, padded = held_ref.shape
    column = lax.broadcasted_iota(jnp.int32, (count, padded), 1)
    at_curve = column == width
    normal = held_ref[0] + got_ref[0]
    curvature = jnp.sum(jnp.where(at_curve, normal, 0.0), axis=1, keepdims=True)
    step = energy_ref[:, :1] / curvature
    total = jnp.zeros((count, padded), F32)
    for at in range(parts):
        normal = held_ref[at] + got_ref[at]
        changed = remaining_ref[at] - step * normal
        scaled = diagonal_ref[at] * changed
        entering_ref[at] = changed
        total = total + jnp.where(column < width, changed * scaled, 0.0)
    share = jnp.sum(total, axis=1, keepdims=True)
    next_ref[...] = jnp.broadcast_to(share, next_ref.shape)
    own = place_ref[0] // first_bits
    changed = entering_ref[own]
    new_residual_ref[...] = changed
    conditioned_ref[...] = diagonal_ref[own] * changed
    new_solution_ref[...] = current_ref[0] + step * search_ref[0]


def finish_kernel(parts, *refs):
    energy_ref, conditioned_ref, search_ref = refs[:3]
    early_refs, shares = (refs[3:5], refs[5 : 5 + parts])
    out_hbm, scratch = (refs[5 + parts : 8 + parts], refs[8 + parts :])
    width = scratch[0].shape[1]
    sems = scratch[3]
    copies = [
        pltpu.make_async_copy(scratch[at], out_hbm[at].at[:, 0, :], sems.at[at]) for at in range(3)
    ]
    for source_ref, target_ref, copy in zip(early_refs, scratch, copies):
        target_ref[...] = source_ref[:, :width]
        copy.start()
    energy_next = shares[0][...]
    for share_ref in shares[1:]:
        energy_next = energy_next + share_ref[...]
    turn = (energy_next / energy_ref[...])[:, :1]
    scratch[2][...] = (conditioned_ref[...] + turn * search_ref[0])[:, :width]
    copies[2].start()
    for copy in copies:
        copy.wait()


def exchange(value, axis, bit):
    size = lax.axis_size(axis)
    return lax.ppermute(value, axis, [(at, at ^ bit) for at in range(size)])


def over_order(value):
    if lax.axis_size("order") == 2:
        return [value, exchange(value, "order", 1)]
    return [lax.psum(value, "order")]


def shards(
    solution,
    residual,
    direction,
    precond,
    design,
    epoch_counts,
    segment_orders,
    pole_life,
    zero_ratio,
    fir_taps,
):
    count, _, wide = direction.shape
    components, length = design.shape[:2]
    sections = pole_life.shape[1] * pole_life.shape[2]
    taps_count = fir_taps.shape[1]
    kinds = sections + taps_count - 1
    blocks = lax.axis_size("tm")
    width = wide // blocks
    padded = (width // LANES + 1) * LANES
    bits = blocks.bit_length() - 1
    halved = bits // 2
    classes = 1 << halved
    parts = blocks // classes
    place = lax.axis_index("tm").astype(jnp.int32).reshape(1)
    levels = length.bit_length() - 1
    hbm = pl.BlockSpec(memory_space=pltpu.HBM)
    small = [
        segment_orders.T,
        jnp.transpose(pole_life, (1, 2, 0)),
        jnp.transpose(zero_ratio, (1, 2, 0)),
        fir_taps,
    ]

    predicted, rates, spread, steps, design_kept = call(
        predict_kernel,
        (
            shape(length + count, LANES),
            shape(sections * (levels + 1) + taps_count, LANES),
            shape(length, LANES),
            shape(3 * SLOT, kinds * LANES),
            jax.ShapeDtypeStruct((components * length, wide), BF16),
        ),
        place,
        *small,
        residual,
        direction,
        precond,
        design.reshape(components * length, wide),
        specs=[smem()] + [hbm] * 8,
        scratch=[pltpu.VMEM(each.shape, each.dtype) for each in small]
        + [pltpu.VMEM((count, wide), F32)] * 2
        + [pltpu.VMEM((1, wide), F32), pltpu.SemaphoreType.DMA((8,))],
    )
    arrived = over_order(predicted)
    send, keep, energy = call(
        functools.partial(filter_kernel, sections, taps_count, length, len(arrived)),
        (shape(blocks, SLOT, LANES), shape(length, LANES), shape(count, LANES)),
        epoch_counts,
        rates,
        *arrived,
        specs=[smem()] + [vmem()] * (1 + len(arrived)),
    )
    everyone = lax.all_to_all(send, "tm", 0, 0)
    pieces = call(
        functools.partial(normal_kernel, kinds, width, classes),
        [shape(parts, count, padded)] * classes,
        place,
        epoch_counts,
        everyone,
        keep,
        spread,
        steps,
        design_kept,
        specs=[smem()] * 2 + [vmem()] * 5,
        scratch=[pltpu.VMEM((blocks, SLOT, LANES), F32), pltpu.VMEM((count, wide), F32)],
    )
    diagonal_parts, remaining_parts, search_own, current_own = call(
        functools.partial(slices_kernel, width, classes),
        (
            shape(parts, count, padded),
            shape(parts, count, padded),
            shape(1, count, padded),
            shape(1, count, padded),
        ),
        place,
        solution,
        residual,
        direction,
        precond,
        specs=[smem()] + [hbm] * 4,
        scratch=[pltpu.VMEM((count, wide), F32)] * 3
        + [pltpu.VMEM((1, wide), F32), pltpu.SemaphoreType.DMA((4,))],
    )
    arriving = [exchange(pieces[apart], "tm", apart) for apart in range(1, classes)]
    buffer = pieces[0] + sum(arriving[1:], arriving[0])
    for bit in range(halved, bits - 1):
        buffer = buffer + exchange(buffer, "tm", 1 << bit)
    arriving = exchange(buffer, "tm", 1 << bits - 1)
    share, new_solution, new_residual, conditioned = call(
        functools.partial(update_kernel, width, classes),
        (
            shape(count, LANES),
            shape(count, padded),
            shape(count, padded),
            shape(count, padded),
        ),
        place,
        buffer,
        arriving,
        energy,
        remaining_parts,
        diagonal_parts,
        current_own,
        search_own,
        specs=[smem()] + [vmem()] * 7,
        scratch=[pltpu.VMEM((parts, count, padded), F32)],
    )
    for bit in range(halved):
        share = share + exchange(share, "tm", 1 << bit)
    shares = over_order(share)
    return call(
        functools.partial(finish_kernel, len(shares)),
        (pltpu.HBM((count, 1, width), F32),) * 3,
        energy,
        conditioned,
        search_own,
        new_solution,
        new_residual,
        *shares,
        scratch=[pltpu.VMEM((count, width), F32)] * 3 + [pltpu.SemaphoreType.DMA((3,))],
    )


def solution(mesh):
    placed = (
        P(None, "order", None),
        P(None, "order", None),
        P(None, "order", None),
        P("order", None),
        P(None, "tm", "order", None),
        P("tm"),
        P(),
        P(),
        P(),
        P(),
    )
    return jax.shard_map(
        shards,
        mesh=mesh,
        in_specs=placed,
        out_specs=(P(None, "order", "tm"), P(None, "order", "tm"), P(None, "order", "tm")),
        check_vma=False,
    )
```

```python
import functools

import jax
import jax.numpy as jnp
from jax import lax
from jax.experimental import pallas as pl
from jax.experimental.pallas import tpu as pltpu
from jax.sharding import PartitionSpec as P

HIGHEST = lax.Precision.HIGHEST
F32 = jnp.float32
BF16 = jnp.bfloat16
LANES = 128
SLOT = 16
VMEM_LIMIT = 16 * 1024 * 1024


def vmem():
    return pl.BlockSpec(memory_space=pltpu.VMEM)


def smem():
    return pl.BlockSpec(memory_space=pltpu.SMEM)


def call(kernel, outs, *args, specs=None, scratch=()):
    args = [
        pltpu.with_memory_space_constraint(arg, pltpu.HBM)
        if specs and specs[at].memory_space == pltpu.HBM
        else arg
        for at, arg in enumerate(args)
    ]
    return pl.pallas_call(
        kernel,
        out_shape=outs,
        in_specs=specs or [vmem()] * len(args),
        out_specs=jax.tree.map(
            lambda out: pl.BlockSpec(memory_space=getattr(out, "memory_space", pltpu.VMEM)), outs
        ),
        scratch_shapes=scratch,
        compiler_params=pltpu.CompilerParams(vmem_limit_bytes=VMEM_LIMIT),
    )(*args)


def shape(*dims):
    return jax.ShapeDtypeStruct(dims, F32)


def column_block(source_ref, block, width, padded):
    wide = source_ref.shape[-1]
    window = min(padded + LANES, wide)
    start = block * width
    base = jnp.minimum(start // LANES * LANES, wide - window)
    part = source_ref[:, pl.ds(pl.multiple_of(base, LANES), window)]
    return pltpu.roll(part, (window - (start - base)) % window, 1)[:, :padded]


def rows_of(value):
    return lax.broadcasted_iota(jnp.int32, value.shape, 0)


def down(value, by):
    moved = pltpu.roll(value, by, 0)
    return jnp.where(rows_of(value) >= by, moved, 0.0)


def up(value, by):
    length = value.shape[0]
    moved = pltpu.roll(value, length - by, 0)
    return jnp.where(rows_of(value) < length - by, moved, 0.0)


def recur(value, powers, move):
    by = 1
    for power in powers:
        value = value + power * move(value, by)
        by *= 2
    return value


def forward_block(series, starts, history, poles, zeros, taps):
    length = series.shape[0]
    first = rows_of(series) == 0
    current, states = (series, [series[length - 1 :]])
    for section, (powers, zero) in enumerate(zip(poles, zeros)):
        if starts is None:
            driven = current - zero * down(current, 1)
        else:
            before = jnp.where(first, starts[section], pltpu.roll(current, 1, 0))
            driven = current - zero * before
            driven = driven + jnp.where(first, powers[0] * starts[section + 1], 0.0)
        current = recur(driven, powers, down)
        states.append(current[length - 1 :])
    reach = history.shape[0]
    extended = jnp.concatenate([history, current], axis=0)
    filtered = taps[0] * current
    for lag in range(1, len(taps)):
        filtered = filtered + taps[lag] * pltpu.roll(extended, lag, 0)[reach:]
    for back in range(1, reach):
        states.append(current[length - 1 - back : length - back])
    return (filtered, states)


def backward_block(filtered, ends, poles, zeros, taps):
    length = filtered.shape[0]
    reach = len(taps) - 1
    border = jnp.zeros((reach, LANES), F32)
    padded = jnp.concatenate([border, filtered, border], axis=0)
    total = padded.shape[0]
    spread = taps[0] * padded
    for lag in range(1, reach + 1):
        spread = spread + taps[lag] * pltpu.roll(padded, total - lag, 0)
    history = spread[:reach]
    current = spread[reach : reach + length]
    sections = len(poles)
    rows = rows_of(current)
    if ends is not None:
        for back in range(reach):
            current = current + jnp.where(rows == length - 1 - back, ends[sections + back], 0.0)
    states = [None] * (sections + reach)
    from_later = None
    for section in reversed(range(sections)):
        value = recur(current, poles[section], up)
        current = value - zeros[section] * up(value, 1)
        if ends is not None:
            current = current + jnp.where(rows == length - 1, ends[section], 0.0)
        to_output = poles[section][0] * value[:1]
        states[section + 1] = to_output if from_later is None else to_output + from_later
        from_later = -zeros[section] * value[:1]
    states[0] = from_later
    states[sections] = states[sections] + history[reach - 1 :]
    for back in range(1, reach):
        states[sections + back] = history[reach - 1 - back : reach - back]
    return (current, states)


def pack(states):
    rows = lax.broadcasted_iota(jnp.int32, (SLOT, LANES), 0)
    packed = jnp.zeros((SLOT, LANES), F32)
    for at, state in enumerate(states):
        packed = jnp.where(rows == at, state, packed)
    return packed


def rates_of(table, sections, taps_count, levels):
    rows = [table[at : at + 1] for at in range(sections * (levels + 1) + taps_count)]
    poles = [rows[at * levels : (at + 1) * levels] for at in range(sections)]
    zeros = rows[sections * levels : sections * (levels + 1)]
    return (poles, zeros, rows[sections * (levels + 1) :])


def predict_kernel(*refs):
    _, *refs = refs
    orders_hbm, lives_hbm, ratios_hbm, taps_hbm = refs[:4]
    residual_hbm, direction_hbm, diagonal_hbm, design_hbm = refs[4:8]
    predicted_ref, rates_ref, spread_ref, steps_ref, design_ref = refs[8:13]
    orders_ref, lives_ref, ratios_ref, taps_ref, remaining_ref, search_ref, diagonal_ref, sems = refs[13:]
    components = taps_ref.shape[0]
    length = design_ref.shape[0] // components
    copies = [
        pltpu.make_async_copy(source, target, sems.at[at])
        for at, (source, target) in enumerate(
            [
                (direction_hbm.at[:, 0, :], search_ref),
                (orders_hbm, orders_ref),
                (lives_hbm, lives_ref),
                (ratios_hbm, ratios_ref),
                (taps_hbm, taps_ref),
                (design_hbm, design_ref),
                (residual_hbm.at[:, 0, :], remaining_ref),
                (diagonal_hbm, diagonal_ref),
            ]
        )
    ]
    for copy in copies:
        copy.start()
    half = LANES // 2
    segments, sections_each, _ = lives_ref.shape
    sections = segments * sections_each
    taps_count = taps_ref.shape[1]
    for copy in copies[1:5]:
        copy.wait()
    lane = lax.broadcasted_iota(jnp.int32, (components, LANES), 1)
    component = lax.broadcasted_iota(jnp.int32, (components, LANES), 0)
    count = half // components
    spreader = jnp.where(lane % half // count == component, 1.0, 0.0)

    def over_lanes(rows):
        return jnp.dot(rows, spreader, precision=HIGHEST, preferred_element_type=F32)

    def flat(ref):
        return jnp.concatenate([ref[at] for at in range(segments)], axis=0)

    life = over_lanes(flat(lives_ref))
    ratio = over_lanes(flat(ratios_ref))
    orders = over_lanes(orders_ref[...].astype(F32))
    tap_rows = lax.dot_general(
        taps_ref[...], spreader, (((0,), (0,)), ((), ())), precision=HIGHEST,
        preferred_element_type=F32,
    )
    spare = jnp.concatenate(
        [orders[at : at + 1] - (each + 0.5) for at in range(segments) for each in range(sections_each)],
        axis=0,
    )
    active = spare > 0.0
    pole_all = jnp.exp(-1.0 / life)
    pole_rate = jnp.where(active, pole_all, 0.0)
    zero_rate = jnp.where(active, 1.0 - ratio * (1.0 - pole_all), 0.0)
    levels = length.bit_length() - 1
    power = pole_rate
    for level in range(levels):
        for section in range(sections):
            at = section * levels + level
            rates_ref[at : at + 1, :] = power[section : section + 1]
        power = power * power
    rates_ref[sections * levels : sections * (levels + 1), :] = zero_rate
    rates_ref[sections * (levels + 1) : sections * (levels + 1) + taps_count, :] = tap_rows

    reach = taps_count - 1
    kinds = sections + reach
    poles, zeros, taps = rates_of(rates_ref, sections, taps_count, length.bit_length() - 1)
    lane = lax.broadcasted_iota(jnp.int32, (1, LANES), 1)
    slot = jnp.where(lane >= half, lane % SLOT, SLOT)
    units = [jnp.where(slot == at, 1.0, 0.0) for at in range(kinds)]
    rows = lax.broadcasted_iota(jnp.int32, (reach, LANES), 0)
    history = jnp.where(slot == kinds - 1 - rows, 1.0, 0.0)
    nothing = jnp.zeros((length, LANES), F32)
    filtered, ends = forward_block(nothing, units[: sections + 1], history, poles, zeros, taps)
    local, heads = backward_block(filtered, None, poles, zeros, taps)
    reply, replies = backward_block(nothing, units, poles, zeros, taps)
    spread_ref[...] = jnp.where(lane < half, pltpu.roll(local, half, 1), reply)
    stacked = jnp.concatenate([pack(ends), pack(heads), pack(replies)], axis=0)
    source = lax.broadcasted_iota(jnp.int32, (LANES, kinds * LANES), 0)
    target = lax.broadcasted_iota(jnp.int32, (LANES, kinds * LANES), 1)
    within = target % LANES
    wanted = half + within // SLOT * SLOT + target // LANES
    pick = jnp.where((within < half) & (source == wanted), 1.0, 0.0)
    steps_ref[...] = jnp.dot(stacked, pick, precision=HIGHEST, preferred_element_type=F32)

    copies[0].wait()
    search = search_ref[...]
    high = search.astype(BF16)
    rest = search - high.astype(F32)
    middle = rest.astype(BF16)
    low = (rest - middle.astype(F32)).astype(BF16)
    split = jnp.concatenate([high, middle, low], axis=0)
    copies[5].wait()
    sums = lax.dot_general(
        design_ref[...], split, (((1,), (1,)), ((), ())), preferred_element_type=F32
    )
    pieces = [sums[at * length : (at + 1) * length] for at in range(components)]
    coarse = [piece[:, :count] for piece in pieces]
    fine = [piece[:, count : 2 * count] + piece[:, 2 * count :] for piece in pieces]
    predicted_ref[:length, :] = jnp.concatenate(coarse + fine, axis=1)
    for copy in copies[6:]:
        copy.wait()
    remaining = remaining_ref[...]
    energy = jnp.sum(remaining * diagonal_ref[...] * remaining, axis=1, keepdims=True)
    predicted_ref[length:, :] = jnp.broadcast_to(energy, (count, LANES))


def slices_kernel(width, first_bits, *refs):
    place_ref, vectors_hbm, diagonal_hbm = (refs[0], refs[1:4], refs[4])
    slices = refs[5:9]
    current_ref, remaining_ref, search_ref, diagonal_ref, sems = refs[9:]
    sources = [current_ref, remaining_ref, search_ref]
    copies = [
        pltpu.make_async_copy(vector.at[:, 0, :], target, sems.at[at])
        for at, (vector, target) in enumerate(zip(vectors_hbm, sources))
    ]
    copies.append(pltpu.make_async_copy(diagonal_hbm, diagonal_ref, sems.at[len(sources)]))
    for copy in copies:
        copy.start()
    for copy in copies:
        copy.wait()
    mine = place_ref[0]
    vectors = [diagonal_ref, remaining_ref, search_ref, current_ref]
    for source_ref, target_ref in zip(vectors, slices):
        for at in range(target_ref.shape[0]):
            block = mine if target_ref.shape[0] == 1 else at * first_bits + mine % first_bits
            part = column_block(source_ref, block, width, target_ref.shape[2])
            target_ref[at] = jnp.broadcast_to(part, target_ref.shape[1:])


def filter_kernel(sections, taps_count, length, parts, *refs):
    counts_ref, rates_ref = refs[:2]
    gathered = refs[2 : 2 + parts]
    send_ref, keep_ref, energy_ref = refs[2 + parts :]
    half = LANES // 2
    received = gathered[0][...]
    for other in gathered[1:]:
        received = received + other[...]
    energy_ref[...] = received[length:]
    received = received[:length]
    low_half = lax.broadcasted_iota(jnp.int32, (1, LANES), 1) < half
    data = jnp.where(low_half & (rows_of(received) < counts_ref[0]), received, 0.0)
    poles, zeros, taps = rates_of(rates_ref, sections, taps_count, length.bit_length() - 1)
    history = jnp.zeros((taps_count - 1, LANES), F32)
    filtered, ends = forward_block(data, None, history, poles, zeros, taps)
    local, heads = backward_block(filtered, None, poles, zeros, taps)
    sent = jnp.where(low_half, pack(ends), pltpu.roll(pack(heads), half, 1))
    for block in range(send_ref.shape[0]):
        send_ref[block] = sent
    keep_ref[...] = jnp.where(low_half, local, received + pltpu.roll(received, half, 1))


def normal_kernel(kinds, width, first_bits, *refs):
    place_ref, counts_ref, all_ref, keep_ref, spread_ref, steps_ref, design_ref = refs[:7]
    out_refs, (entering_ref, cut_ref) = (refs[7:-2], refs[-2:])
    blocks = all_ref.shape[0]
    mine = place_ref[0]
    half = LANES // 2

    def apply(which, state):
        terms = []
        for at in range(kinds):
            column = steps_ref[which * SLOT : (which + 1) * SLOT, at * LANES : (at + 1) * LANES]
            terms.append(column * state[at : at + 1])
        while len(terms) > 1:
            pairs = [sum(terms[at : at + 2][1:], terms[at]) for at in range(0, len(terms), 2)]
            terms = pairs
        return terms[0]

    def advance(block, state):
        entering_ref[block] = state
        return apply(0, state) + all_ref[block]

    def retreat(step, state):
        block = blocks - 1 - step
        later = apply(2, state) + (apply(1, entering_ref[block]) + pltpu.roll(all_ref[block], half, 1))
        return jnp.where(block > mine, later, state)

    empty = jnp.zeros((SLOT, LANES), F32)
    unroll = blocks if blocks <= 16 else 4
    lax.fori_loop(0, blocks, advance, empty, unroll=unroll)
    leaving = lax.fori_loop(0, blocks, retreat, empty, unroll=unroll)
    entering = entering_ref[mine]

    groups = half // SLOT
    row = lax.broadcasted_iota(jnp.int32, (half, LANES), 0)
    lane = lax.broadcasted_iota(jnp.int32, (half, LANES), 1)
    own = row // SLOT == lane // SLOT
    expanded = [
        jnp.where(own, jnp.concatenate([state] * groups, axis=0), 0.0)
        for state in (entering, leaving)
    ]
    correction = jnp.dot(
        spread_ref[...],
        jnp.concatenate(expanded, axis=0),
        precision=HIGHEST,
        preferred_element_type=F32,
    )
    kept = keep_ref[...]
    live = (row < counts_ref[0]) & (lane < half)
    weighted = jnp.where(live, kept + correction, 0.0)
    weighted = weighted.astype(BF16).astype(F32)
    product = weighted * pltpu.roll(kept, half, 1)
    turned = jnp.transpose(weighted)
    count = out_refs[0].shape[-2]
    low = jnp.concatenate(
        [turned[at * count : (at + 1) * count] for at in range(half // count)], axis=1
    ).astype(BF16)
    along = jnp.sum(product, axis=0, keepdims=True)
    total = along
    for at in range(1, half // count):
        total = total + pltpu.roll(along, LANES - at * count, 1)
    row = lax.broadcasted_iota(jnp.int32, (count, LANES), 0)
    lane = lax.broadcasted_iota(jnp.int32, (count, LANES), 1)
    curvature = jnp.sum(jnp.where(row == lane, total, 0.0), axis=1, keepdims=True)
    normal = jnp.dot(low, design_ref[...], preferred_element_type=F32)
    padded = out_refs[0].shape[-1]
    column = lax.broadcasted_iota(jnp.int32, (count, padded), 1)
    curvature = jnp.broadcast_to(curvature, (count, padded))
    low_bits = mine % first_bits
    wide = normal.shape[1]
    window = min(padded + LANES, wide)
    for block in range(wide // width):
        start = block * width
        base = min(start // LANES * LANES, wide - window)
        part = normal[:, base : base + window]
        if start != base:
            part = pltpu.roll(part, window - (start - base), 1)
        cut_ref[block] = jnp.where(column < width, part[:, :padded], curvature)
    for apart, out_ref in enumerate(out_refs):
        for at in range(out_ref.shape[0]):
            out_ref[at] = cut_ref[at * first_bits + (low_bits ^ apart)]


def update_kernel(width, first_bits, *refs):
    place_ref, held_ref, got_ref, energy_ref = refs[:4]
    remaining_ref, diagonal_ref, current_ref, search_ref = refs[4:8]
    next_ref, new_solution_ref, new_residual_ref, conditioned_ref, entering_ref = refs[8:]
    parts, count, padded = held_ref.shape
    column = lax.broadcasted_iota(jnp.int32, (count, padded), 1)
    at_curve = column == width
    normal = held_ref[0] + got_ref[0]
    curvature = jnp.sum(jnp.where(at_curve, normal, 0.0), axis=1, keepdims=True)
    step = energy_ref[:, :1] / curvature
    total = jnp.zeros((count, padded), F32)
    for at in range(parts):
        normal = held_ref[at] + got_ref[at]
        changed = remaining_ref[at] - step * normal
        scaled = diagonal_ref[at] * changed
        entering_ref[at] = changed
        total = total + jnp.where(column < width, changed * scaled, 0.0)
    share = jnp.sum(total, axis=1, keepdims=True)
    next_ref[...] = jnp.broadcast_to(share, next_ref.shape)
    own = place_ref[0] // first_bits
    changed = entering_ref[own]
    new_residual_ref[...] = changed
    conditioned_ref[...] = diagonal_ref[own] * changed
    new_solution_ref[...] = current_ref[0] + step * search_ref[0]


def finish_kernel(parts, *refs):
    energy_ref, conditioned_ref, search_ref = refs[:3]
    early_refs, shares = (refs[3:5], refs[5 : 5 + parts])
    out_hbm, scratch = (refs[5 + parts : 8 + parts], refs[8 + parts :])
    width = scratch[0].shape[1]
    sems = scratch[3]
    copies = [
        pltpu.make_async_copy(scratch[at], out_hbm[at].at[:, 0, :], sems.at[at]) for at in range(3)
    ]
    for source_ref, target_ref, copy in zip(early_refs, scratch, copies):
        target_ref[...] = source_ref[:, :width]
        copy.start()
    energy_next = shares[0][...]
    for share_ref in shares[1:]:
        energy_next = energy_next + share_ref[...]
    turn = (energy_next / energy_ref[...])[:, :1]
    scratch[2][...] = (conditioned_ref[...] + turn * search_ref[0])[:, :width]
    copies[2].start()
    for copy in copies:
        copy.wait()


def exchange(value, axis, bit):
    size = lax.axis_size(axis)
    return lax.ppermute(value, axis, [(at, at ^ bit) for at in range(size)])


def over_order(value):
    if lax.axis_size("order") == 2:
        return [value, exchange(value, "order", 1)]
    return [lax.psum(value, "order")]


def shards(
    solution,
    residual,
    direction,
    precond,
    design,
    epoch_counts,
    segment_orders,
    pole_life,
    zero_ratio,
    fir_taps,
):
    count, _, wide = direction.shape
    components, length = design.shape[:2]
    sections = pole_life.shape[1] * pole_life.shape[2]
    taps_count = fir_taps.shape[1]
    kinds = sections + taps_count - 1
    blocks = lax.axis_size("tm")
    width = wide // blocks
    padded = (width // LANES + 1) * LANES
    bits = blocks.bit_length() - 1
    halved = bits // 2
    classes = 1 << halved
    parts = blocks // classes
    place = lax.axis_index("tm").astype(jnp.int32).reshape(1)
    levels = length.bit_length() - 1
    hbm = pl.BlockSpec(memory_space=pltpu.HBM)
    small = [
        segment_orders.T,
        jnp.transpose(pole_life, (1, 2, 0)),
        jnp.transpose(zero_ratio, (1, 2, 0)),
        fir_taps,
    ]

    predicted, rates, spread, steps, design_kept = call(
        predict_kernel,
        (
            shape(length + count, LANES),
            shape(sections * (levels + 1) + taps_count, LANES),
            shape(length, LANES),
            shape(3 * SLOT, kinds * LANES),
            jax.ShapeDtypeStruct((components * length, wide), BF16),
        ),
        place,
        *small,
        residual,
        direction,
        precond,
        design.reshape(components * length, wide),
        specs=[smem()] + [hbm] * 8,
        scratch=[pltpu.VMEM(each.shape, each.dtype) for each in small]
        + [pltpu.VMEM((count, wide), F32)] * 2
        + [pltpu.VMEM((1, wide), F32), pltpu.SemaphoreType.DMA((8,))],
    )
    arrived = over_order(predicted)
    send, keep, energy = call(
        functools.partial(filter_kernel, sections, taps_count, length, len(arrived)),
        (shape(blocks, SLOT, LANES), shape(length, LANES), shape(count, LANES)),
        epoch_counts,
        rates,
        *arrived,
        specs=[smem()] + [vmem()] * (1 + len(arrived)),
    )
    everyone = lax.all_to_all(send, "tm", 0, 0)
    pieces = call(
        functools.partial(normal_kernel, kinds, width, classes),
        [shape(parts, count, padded)] * classes,
        place,
        epoch_counts,
        everyone,
        keep,
        spread,
        steps,
        design_kept,
        specs=[smem()] * 2 + [vmem()] * 5,
        scratch=[pltpu.VMEM((blocks, SLOT, LANES), F32), pltpu.VMEM((blocks, count, padded), F32)],
    )
    diagonal_parts, remaining_parts, search_own, current_own = call(
        functools.partial(slices_kernel, width, classes),
        (
            shape(parts, count, padded),
            shape(parts, count, padded),
            shape(1, count, padded),
            shape(1, count, padded),
        ),
        place,
        solution,
        residual,
        direction,
        precond,
        specs=[smem()] + [hbm] * 4,
        scratch=[pltpu.VMEM((count, wide), F32)] * 3
        + [pltpu.VMEM((1, wide), F32), pltpu.SemaphoreType.DMA((4,))],
    )
    arriving = [exchange(pieces[apart], "tm", apart) for apart in range(1, classes)]
    buffer = pieces[0] + sum(arriving[1:], arriving[0])
    for bit in range(halved, bits - 1):
        buffer = buffer + exchange(buffer, "tm", 1 << bit)
    arriving = exchange(buffer, "tm", 1 << bits - 1)
    share, new_solution, new_residual, conditioned = call(
        functools.partial(update_kernel, width, classes),
        (
            shape(count, LANES),
            shape(count, padded),
            shape(count, padded),
            shape(count, padded),
        ),
        place,
        buffer,
        arriving,
        energy,
        remaining_parts,
        diagonal_parts,
        current_own,
        search_own,
        specs=[smem()] + [vmem()] * 7,
        scratch=[pltpu.VMEM((parts, count, padded), F32)],
    )
    for bit in range(halved):
        share = share + exchange(share, "tm", 1 << bit)
    shares = over_order(share)
    return call(
        functools.partial(finish_kernel, len(shares)),
        (pltpu.HBM((count, 1, width), F32),) * 3,
        energy,
        conditioned,
        search_own,
        new_solution,
        new_residual,
        *shares,
        scratch=[pltpu.VMEM((count, width), F32)] * 3 + [pltpu.SemaphoreType.DMA((3,))],
    )


def solution(mesh):
    placed = (
        P(None, "order", None),
        P(None, "order", None),
        P(None, "order", None),
        P("order", None),
        P(None, "tm", "order", None),
        P("tm"),
        P(),
        P(),
        P(),
        P(),
    )
    return jax.shard_map(
        shards,
        mesh=mesh,
        in_specs=placed,
        out_specs=(P(None, "order", "tm"), P(None, "order", "tm"), P(None, "order", "tm")),
        check_vma=False,
    )
```

```python
import functools

import jax
import jax.numpy as jnp
from jax import lax
from jax.experimental import pallas as pl
from jax.experimental.pallas import tpu as pltpu
from jax.sharding import PartitionSpec as P

HIGHEST = lax.Precision.HIGHEST
F32 = jnp.float32
BF16 = jnp.bfloat16
LANES = 128
SLOT = 16
VMEM_LIMIT = 16 * 1024 * 1024


def vmem():
    return pl.BlockSpec(memory_space=pltpu.VMEM)


def smem():
    return pl.BlockSpec(memory_space=pltpu.SMEM)


def call(kernel, outs, *args, specs=None, scratch=()):
    args = [
        pltpu.with_memory_space_constraint(arg, pltpu.HBM)
        if specs and specs[at].memory_space == pltpu.HBM
        else arg
        for at, arg in enumerate(args)
    ]
    return pl.pallas_call(
        kernel,
        out_shape=outs,
        in_specs=specs or [vmem()] * len(args),
        out_specs=jax.tree.map(
            lambda out: pl.BlockSpec(memory_space=getattr(out, "memory_space", pltpu.VMEM)), outs
        ),
        scratch_shapes=scratch,
        compiler_params=pltpu.CompilerParams(vmem_limit_bytes=VMEM_LIMIT),
    )(*args)


def shape(*dims):
    return jax.ShapeDtypeStruct(dims, F32)


def halves(value):
    high = value.astype(BF16)
    return (high, (value - high.astype(F32)).astype(BF16))


def column_block(source_ref, block, width, padded):
    wide = source_ref.shape[-1]
    window = min(padded + LANES, wide)
    start = block * width
    base = jnp.minimum(start // LANES * LANES, wide - window)
    part = source_ref[:, pl.ds(pl.multiple_of(base, LANES), window)]
    return pltpu.roll(part, (window - (start - base)) % window, 1)[:, :padded]


def rows_of(value):
    return lax.broadcasted_iota(jnp.int32, value.shape, 0)


def down(value, by):
    moved = pltpu.roll(value, by, 0)
    return jnp.where(rows_of(value) >= by, moved, 0.0)


def up(value, by):
    length = value.shape[0]
    moved = pltpu.roll(value, length - by, 0)
    return jnp.where(rows_of(value) < length - by, moved, 0.0)


def recur(value, powers, move):
    by = 1
    for power in powers:
        value = value + power * move(value, by)
        by *= 2
    return value


def forward_block(series, starts, history, poles, zeros, taps):
    length = series.shape[0]
    first = rows_of(series) == 0
    current, states = (series, [series[length - 1 :]])
    for section, (powers, zero) in enumerate(zip(poles, zeros)):
        if starts is None:
            driven = current - zero * down(current, 1)
        else:
            before = jnp.where(first, starts[section], pltpu.roll(current, 1, 0))
            driven = current - zero * before
            driven = driven + jnp.where(first, powers[0] * starts[section + 1], 0.0)
        current = recur(driven, powers, down)
        states.append(current[length - 1 :])
    reach = history.shape[0]
    extended = jnp.concatenate([history, current], axis=0)
    filtered = taps[0] * current
    for lag in range(1, len(taps)):
        filtered = filtered + taps[lag] * pltpu.roll(extended, lag, 0)[reach:]
    for back in range(1, reach):
        states.append(current[length - 1 - back : length - back])
    return (filtered, states)


def backward_block(filtered, ends, poles, zeros, taps):
    length = filtered.shape[0]
    reach = len(taps) - 1
    border = jnp.zeros((reach, LANES), F32)
    padded = jnp.concatenate([border, filtered, border], axis=0)
    total = padded.shape[0]
    spread = taps[0] * padded
    for lag in range(1, reach + 1):
        spread = spread + taps[lag] * pltpu.roll(padded, total - lag, 0)
    history = spread[:reach]
    current = spread[reach : reach + length]
    sections = len(poles)
    rows = rows_of(current)
    if ends is not None:
        for back in range(reach):
            current = current + jnp.where(rows == length - 1 - back, ends[sections + back], 0.0)
    states = [None] * (sections + reach)
    from_later = None
    for section in reversed(range(sections)):
        value = recur(current, poles[section], up)
        current = value - zeros[section] * up(value, 1)
        if ends is not None:
            current = current + jnp.where(rows == length - 1, ends[section], 0.0)
        to_output = poles[section][0] * value[:1]
        states[section + 1] = to_output if from_later is None else to_output + from_later
        from_later = -zeros[section] * value[:1]
    states[0] = from_later
    states[sections] = states[sections] + history[reach - 1 :]
    for back in range(1, reach):
        states[sections + back] = history[reach - 1 - back : reach - back]
    return (current, states)


def pack(states):
    rows = lax.broadcasted_iota(jnp.int32, (SLOT, LANES), 0)
    packed = jnp.zeros((SLOT, LANES), F32)
    for at, state in enumerate(states):
        packed = jnp.where(rows == at, state, packed)
    return packed


def rates_of(table, sections, taps_count, levels):
    rows = [table[at : at + 1] for at in range(sections * (levels + 1) + taps_count)]
    poles = [rows[at * levels : (at + 1) * levels] for at in range(sections)]
    zeros = rows[sections * levels : sections * (levels + 1)]
    return (poles, zeros, rows[sections * (levels + 1) :])


def predict_kernel(*refs):
    _, *refs = refs
    orders_hbm, lives_hbm, ratios_hbm, taps_hbm = refs[:4]
    residual_hbm, direction_hbm, diagonal_hbm, design_hbm = refs[4:8]
    predicted_ref, rates_ref, spread_ref, steps_ref, design_ref = refs[8:13]
    orders_ref, lives_ref, ratios_ref, taps_ref, remaining_ref, search_ref, diagonal_ref, sems = refs[13:]
    components = taps_ref.shape[0]
    length = design_ref.shape[0] // components
    copies = [
        pltpu.make_async_copy(source, target, sems.at[at])
        for at, (source, target) in enumerate(
            [
                (direction_hbm.at[:, 0, :], search_ref),
                (orders_hbm, orders_ref),
                (lives_hbm, lives_ref),
                (ratios_hbm, ratios_ref),
                (taps_hbm, taps_ref),
                (design_hbm, design_ref),
                (residual_hbm.at[:, 0, :], remaining_ref),
                (diagonal_hbm, diagonal_ref),
            ]
        )
    ]
    for copy in copies:
        copy.start()
    half = LANES // 2
    segments, sections_each, _ = lives_ref.shape
    sections = segments * sections_each
    taps_count = taps_ref.shape[1]
    for copy in copies[1:5]:
        copy.wait()
    lane = lax.broadcasted_iota(jnp.int32, (components, LANES), 1)
    component = lax.broadcasted_iota(jnp.int32, (components, LANES), 0)
    count = half // components
    spreader = jnp.where(lane % half // count == component, 1.0, 0.0)

    def over_lanes(rows):
        return jnp.dot(rows, spreader, precision=HIGHEST, preferred_element_type=F32)

    def flat(ref):
        return jnp.concatenate([ref[at] for at in range(segments)], axis=0)

    life = over_lanes(flat(lives_ref))
    ratio = over_lanes(flat(ratios_ref))
    orders = over_lanes(orders_ref[...].astype(F32))
    tap_rows = lax.dot_general(
        taps_ref[...], spreader, (((0,), (0,)), ((), ())), precision=HIGHEST,
        preferred_element_type=F32,
    )
    spare = jnp.concatenate(
        [orders[at : at + 1] - (each + 0.5) for at in range(segments) for each in range(sections_each)],
        axis=0,
    )
    active = spare > 0.0
    pole_all = jnp.exp(-1.0 / life)
    pole_rate = jnp.where(active, pole_all, 0.0)
    zero_rate = jnp.where(active, 1.0 - ratio * (1.0 - pole_all), 0.0)
    levels = length.bit_length() - 1
    power = pole_rate
    for level in range(levels):
        for section in range(sections):
            at = section * levels + level
            rates_ref[at : at + 1, :] = power[section : section + 1]
        power = power * power
    rates_ref[sections * levels : sections * (levels + 1), :] = zero_rate
    rates_ref[sections * (levels + 1) : sections * (levels + 1) + taps_count, :] = tap_rows

    reach = taps_count - 1
    kinds = sections + reach
    poles, zeros, taps = rates_of(rates_ref, sections, taps_count, length.bit_length() - 1)
    lane = lax.broadcasted_iota(jnp.int32, (1, LANES), 1)
    slot = jnp.where(lane >= half, lane % SLOT, SLOT)
    units = [jnp.where(slot == at, 1.0, 0.0) for at in range(kinds)]
    rows = lax.broadcasted_iota(jnp.int32, (reach, LANES), 0)
    history = jnp.where(slot == kinds - 1 - rows, 1.0, 0.0)
    nothing = jnp.zeros((length, LANES), F32)
    filtered, ends = forward_block(nothing, units[: sections + 1], history, poles, zeros, taps)
    local, heads = backward_block(filtered, None, poles, zeros, taps)
    reply, replies = backward_block(nothing, units, poles, zeros, taps)
    spread = jnp.where(lane < half, pltpu.roll(local, half, 1), reply)
    spread_high, spread_low = halves(spread)
    spread_ref[...] = jnp.concatenate([spread_high, spread_high, spread_low], axis=1)
    stacked = jnp.concatenate([pack(ends), pack(heads), pack(replies)], axis=0)
    source = lax.broadcasted_iota(jnp.int32, (LANES, kinds * LANES), 0)
    target = lax.broadcasted_iota(jnp.int32, (LANES, kinds * LANES), 1)
    within = target % LANES
    wanted = half + within // SLOT * SLOT + target // LANES
    pick = jnp.where((within < half) & (source == wanted), 1.0, 0.0)
    steps_ref[...] = jnp.dot(stacked, pick, precision=HIGHEST, preferred_element_type=F32)

    copies[0].wait()
    search = search_ref[...]
    high = search.astype(BF16)
    rest = search - high.astype(F32)
    middle = rest.astype(BF16)
    low = (rest - middle.astype(F32)).astype(BF16)
    split = jnp.concatenate([high, middle, low], axis=0)
    copies[5].wait()
    sums = lax.dot_general(
        design_ref[...], split, (((1,), (1,)), ((), ())), preferred_element_type=F32
    )
    pieces = [sums[at * length : (at + 1) * length] for at in range(components)]
    coarse = [piece[:, :count] for piece in pieces]
    fine = [piece[:, count : 2 * count] + piece[:, 2 * count :] for piece in pieces]
    predicted_ref[:length, :] = jnp.concatenate(coarse + fine, axis=1)
    for copy in copies[6:]:
        copy.wait()
    remaining = remaining_ref[...]
    energy = jnp.sum(remaining * diagonal_ref[...] * remaining, axis=1, keepdims=True)
    predicted_ref[length:, :] = jnp.broadcast_to(energy, (count, LANES))


def slices_kernel(width, first_bits, *refs):
    place_ref, vectors_hbm, diagonal_hbm = (refs[0], refs[1:4], refs[4])
    slices = refs[5:9]
    current_ref, remaining_ref, search_ref, diagonal_ref, sems = refs[9:]
    sources = [current_ref, remaining_ref, search_ref]
    copies = [
        pltpu.make_async_copy(vector.at[:, 0, :], target, sems.at[at])
        for at, (vector, target) in enumerate(zip(vectors_hbm, sources))
    ]
    copies.append(pltpu.make_async_copy(diagonal_hbm, diagonal_ref, sems.at[len(sources)]))
    for copy in copies:
        copy.start()
    for copy in copies:
        copy.wait()
    mine = place_ref[0]
    vectors = [diagonal_ref, remaining_ref, search_ref, current_ref]
    for source_ref, target_ref in zip(vectors, slices):
        for at in range(target_ref.shape[0]):
            block = mine if target_ref.shape[0] == 1 else at * first_bits + mine % first_bits
            part = column_block(source_ref, block, width, target_ref.shape[2])
            target_ref[at] = jnp.broadcast_to(part, target_ref.shape[1:])


def filter_kernel(sections, taps_count, length, parts, *refs):
    counts_ref, rates_ref = refs[:2]
    gathered = refs[2 : 2 + parts]
    send_ref, keep_ref, energy_ref = refs[2 + parts :]
    half = LANES // 2
    received = gathered[0][...]
    for other in gathered[1:]:
        received = received + other[...]
    energy_ref[...] = received[length:]
    received = received[:length]
    low_half = lax.broadcasted_iota(jnp.int32, (1, LANES), 1) < half
    data = jnp.where(low_half & (rows_of(received) < counts_ref[0]), received, 0.0)
    poles, zeros, taps = rates_of(rates_ref, sections, taps_count, length.bit_length() - 1)
    history = jnp.zeros((taps_count - 1, LANES), F32)
    filtered, ends = forward_block(data, None, history, poles, zeros, taps)
    local, heads = backward_block(filtered, None, poles, zeros, taps)
    sent = jnp.where(low_half, pack(ends), pltpu.roll(pack(heads), half, 1))
    for block in range(send_ref.shape[0]):
        send_ref[block] = sent
    keep_ref[...] = jnp.where(low_half, local, received + pltpu.roll(received, half, 1))


def normal_kernel(kinds, width, first_bits, *refs):
    place_ref, counts_ref, all_ref, keep_ref, spread_ref, steps_ref, design_ref = refs[:7]
    out_refs, (entering_ref, cut_ref) = (refs[7:-2], refs[-2:])
    blocks = all_ref.shape[0]
    mine = place_ref[0]
    half = LANES // 2

    def apply(which, state):
        terms = []
        for at in range(kinds):
            column = steps_ref[which * SLOT : (which + 1) * SLOT, at * LANES : (at + 1) * LANES]
            terms.append(column * state[at : at + 1])
        while len(terms) > 1:
            pairs = [sum(terms[at : at + 2][1:], terms[at]) for at in range(0, len(terms), 2)]
            terms = pairs
        return terms[0]

    def advance(block, state):
        entering_ref[block] = state
        return apply(0, state) + all_ref[block]

    def retreat(step, state):
        block = blocks - 1 - step
        later = apply(2, state) + (apply(1, entering_ref[block]) + pltpu.roll(all_ref[block], half, 1))
        return jnp.where(block > mine, later, state)

    empty = jnp.zeros((SLOT, LANES), F32)
    unroll = blocks if blocks <= 16 else 4
    lax.fori_loop(0, blocks, advance, empty, unroll=unroll)
    leaving = lax.fori_loop(0, blocks, retreat, empty, unroll=unroll)
    entering = entering_ref[mine]

    groups = half // SLOT
    row = lax.broadcasted_iota(jnp.int32, (half, LANES), 0)
    lane = lax.broadcasted_iota(jnp.int32, (half, LANES), 1)
    own = row // SLOT == lane // SLOT
    expanded = [
        jnp.where(own, jnp.concatenate([state] * groups, axis=0), 0.0)
        for state in (entering, leaving)
    ]
    state_high, state_low = halves(jnp.concatenate(expanded, axis=0))
    correction = jnp.dot(
        spread_ref[...],
        jnp.concatenate([state_high, state_low, state_high], axis=0),
        preferred_element_type=F32,
    )
    kept = keep_ref[...]
    live = (row < counts_ref[0]) & (lane < half)
    weighted = jnp.where(live, kept + correction, 0.0)
    weighted = weighted.astype(BF16).astype(F32)
    product = weighted * pltpu.roll(kept, half, 1)
    turned = jnp.transpose(weighted)
    count = out_refs[0].shape[-2]
    low = jnp.concatenate(
        [turned[at * count : (at + 1) * count] for at in range(half // count)], axis=1
    ).astype(BF16)
    along = jnp.sum(product, axis=0, keepdims=True)
    total = along
    for at in range(1, half // count):
        total = total + pltpu.roll(along, LANES - at * count, 1)
    row = lax.broadcasted_iota(jnp.int32, (count, LANES), 0)
    lane = lax.broadcasted_iota(jnp.int32, (count, LANES), 1)
    curvature = jnp.sum(jnp.where(row == lane, total, 0.0), axis=1, keepdims=True)
    normal = jnp.dot(low, design_ref[...], preferred_element_type=F32)
    padded = out_refs[0].shape[-1]
    column = lax.broadcasted_iota(jnp.int32, (count, padded), 1)
    curvature = jnp.broadcast_to(curvature, (count, padded))
    low_bits = mine % first_bits
    wide = normal.shape[1]
    window = min(padded + LANES, wide)
    for block in range(wide // width):
        start = block * width
        base = min(start // LANES * LANES, wide - window)
        part = normal[:, base : base + window]
        if start != base:
            part = pltpu.roll(part, window - (start - base), 1)
        cut_ref[block] = jnp.where(column < width, part[:, :padded], curvature)
    for apart, out_ref in enumerate(out_refs):
        for at in range(out_ref.shape[0]):
            out_ref[at] = cut_ref[at * first_bits + (low_bits ^ apart)]


def update_kernel(width, first_bits, *refs):
    place_ref, held_ref, got_ref, energy_ref = refs[:4]
    remaining_ref, diagonal_ref, current_ref, search_ref = refs[4:8]
    next_ref, new_solution_ref, new_residual_ref, conditioned_ref, entering_ref = refs[8:]
    parts, count, padded = held_ref.shape
    column = lax.broadcasted_iota(jnp.int32, (count, padded), 1)
    at_curve = column == width
    normal = held_ref[0] + got_ref[0]
    curvature = jnp.sum(jnp.where(at_curve, normal, 0.0), axis=1, keepdims=True)
    step = energy_ref[:, :1] / curvature
    total = jnp.zeros((count, padded), F32)
    for at in range(parts):
        normal = held_ref[at] + got_ref[at]
        changed = remaining_ref[at] - step * normal
        scaled = diagonal_ref[at] * changed
        entering_ref[at] = changed
        total = total + jnp.where(column < width, changed * scaled, 0.0)
    share = jnp.sum(total, axis=1, keepdims=True)
    next_ref[...] = jnp.broadcast_to(share, next_ref.shape)
    own = place_ref[0] // first_bits
    changed = entering_ref[own]
    new_residual_ref[...] = changed
    conditioned_ref[...] = diagonal_ref[own] * changed
    new_solution_ref[...] = current_ref[0] + step * search_ref[0]


def finish_kernel(parts, *refs):
    energy_ref, conditioned_ref, search_ref = refs[:3]
    early_refs, shares = (refs[3:5], refs[5 : 5 + parts])
    out_hbm, scratch = (refs[5 + parts : 8 + parts], refs[8 + parts :])
    width = scratch[0].shape[1]
    sems = scratch[3]
    copies = [
        pltpu.make_async_copy(scratch[at], out_hbm[at].at[:, 0, :], sems.at[at]) for at in range(3)
    ]
    for source_ref, target_ref, copy in zip(early_refs, scratch, copies):
        target_ref[...] = source_ref[:, :width]
        copy.start()
    energy_next = shares[0][...]
    for share_ref in shares[1:]:
        energy_next = energy_next + share_ref[...]
    turn = (energy_next / energy_ref[...])[:, :1]
    scratch[2][...] = (conditioned_ref[...] + turn * search_ref[0])[:, :width]
    copies[2].start()
    for copy in copies:
        copy.wait()


def exchange(value, axis, bit):
    size = lax.axis_size(axis)
    return lax.ppermute(value, axis, [(at, at ^ bit) for at in range(size)])


def over_order(value):
    if lax.axis_size("order") == 2:
        return [value, exchange(value, "order", 1)]
    return [lax.psum(value, "order")]


def shards(
    solution,
    residual,
    direction,
    precond,
    design,
    epoch_counts,
    segment_orders,
    pole_life,
    zero_ratio,
    fir_taps,
):
    count, _, wide = direction.shape
    components, length = design.shape[:2]
    sections = pole_life.shape[1] * pole_life.shape[2]
    taps_count = fir_taps.shape[1]
    kinds = sections + taps_count - 1
    blocks = lax.axis_size("tm")
    width = wide // blocks
    padded = (width // LANES + 1) * LANES
    bits = blocks.bit_length() - 1
    halved = bits // 2
    classes = 1 << halved
    parts = blocks // classes
    place = lax.axis_index("tm").astype(jnp.int32).reshape(1)
    levels = length.bit_length() - 1
    hbm = pl.BlockSpec(memory_space=pltpu.HBM)
    small = [
        segment_orders.T,
        jnp.transpose(pole_life, (1, 2, 0)),
        jnp.transpose(zero_ratio, (1, 2, 0)),
        fir_taps,
    ]

    predicted, rates, spread, steps, design_kept = call(
        predict_kernel,
        (
            shape(length + count, LANES),
            shape(sections * (levels + 1) + taps_count, LANES),
            jax.ShapeDtypeStruct((length, 3 * LANES), BF16),
            shape(3 * SLOT, kinds * LANES),
            jax.ShapeDtypeStruct((components * length, wide), BF16),
        ),
        place,
        *small,
        residual,
        direction,
        precond,
        design.reshape(components * length, wide),
        specs=[smem()] + [hbm] * 8,
        scratch=[pltpu.VMEM(each.shape, each.dtype) for each in small]
        + [pltpu.VMEM((count, wide), F32)] * 2
        + [pltpu.VMEM((1, wide), F32), pltpu.SemaphoreType.DMA((8,))],
    )
    arrived = over_order(predicted)
    send, keep, energy = call(
        functools.partial(filter_kernel, sections, taps_count, length, len(arrived)),
        (shape(blocks, SLOT, LANES), shape(length, LANES), shape(count, LANES)),
        epoch_counts,
        rates,
        *arrived,
        specs=[smem()] + [vmem()] * (1 + len(arrived)),
    )
    everyone = lax.all_to_all(send, "tm", 0, 0)
    pieces = call(
        functools.partial(normal_kernel, kinds, width, classes),
        [shape(parts, count, padded)] * classes,
        place,
        epoch_counts,
        everyone,
        keep,
        spread,
        steps,
        design_kept,
        specs=[smem()] * 2 + [vmem()] * 5,
        scratch=[pltpu.VMEM((blocks, SLOT, LANES), F32), pltpu.VMEM((blocks, count, padded), F32)],
    )
    diagonal_parts, remaining_parts, search_own, current_own = call(
        functools.partial(slices_kernel, width, classes),
        (
            shape(parts, count, padded),
            shape(parts, count, padded),
            shape(1, count, padded),
            shape(1, count, padded),
        ),
        place,
        solution,
        residual,
        direction,
        precond,
        specs=[smem()] + [hbm] * 4,
        scratch=[pltpu.VMEM((count, wide), F32)] * 3
        + [pltpu.VMEM((1, wide), F32), pltpu.SemaphoreType.DMA((4,))],
    )
    arriving = [exchange(pieces[apart], "tm", apart) for apart in range(1, classes)]
    buffer = pieces[0] + sum(arriving[1:], arriving[0])
    for bit in range(halved, bits - 1):
        buffer = buffer + exchange(buffer, "tm", 1 << bit)
    arriving = exchange(buffer, "tm", 1 << bits - 1)
    share, new_solution, new_residual, conditioned = call(
        functools.partial(update_kernel, width, classes),
        (
            shape(count, LANES),
            shape(count, padded),
            shape(count, padded),
            shape(count, padded),
        ),
        place,
        buffer,
        arriving,
        energy,
        remaining_parts,
        diagonal_parts,
        current_own,
        search_own,
        specs=[smem()] + [vmem()] * 7,
        scratch=[pltpu.VMEM((parts, count, padded), F32)],
    )
    for bit in range(halved):
        share = share + exchange(share, "tm", 1 << bit)
    shares = over_order(share)
    return call(
        functools.partial(finish_kernel, len(shares)),
        (pltpu.HBM((count, 1, width), F32),) * 3,
        energy,
        conditioned,
        search_own,
        new_solution,
        new_residual,
        *shares,
        scratch=[pltpu.VMEM((count, width), F32)] * 3 + [pltpu.SemaphoreType.DMA((3,))],
    )


def solution(mesh):
    placed = (
        P(None, "order", None),
        P(None, "order", None),
        P(None, "order", None),
        P("order", None),
        P(None, "tm", "order", None),
        P("tm"),
        P(),
        P(),
        P(),
        P(),
    )
    return jax.shard_map(
        shards,
        mesh=mesh,
        in_specs=placed,
        out_specs=(P(None, "order", "tm"), P(None, "order", "tm"), P(None, "order", "tm")),
        check_vma=False,
    )
```

```python
import functools

import jax
import jax.numpy as jnp
from jax import lax
from jax.experimental import pallas as pl
from jax.experimental.pallas import tpu as pltpu
from jax.sharding import PartitionSpec as P

HIGHEST = lax.Precision.HIGHEST
F32 = jnp.float32
BF16 = jnp.bfloat16
LANES = 128
SLOT = 16
VMEM_LIMIT = 16 * 1024 * 1024


def vmem():
    return pl.BlockSpec(memory_space=pltpu.VMEM)


def smem():
    return pl.BlockSpec(memory_space=pltpu.SMEM)


def call(kernel, outs, *args, specs=None, scratch=()):
    args = [
        pltpu.with_memory_space_constraint(arg, pltpu.HBM)
        if specs and specs[at].memory_space == pltpu.HBM
        else arg
        for at, arg in enumerate(args)
    ]
    return pl.pallas_call(
        kernel,
        out_shape=outs,
        in_specs=specs or [vmem()] * len(args),
        out_specs=jax.tree.map(
            lambda out: pl.BlockSpec(memory_space=getattr(out, "memory_space", pltpu.VMEM)), outs
        ),
        scratch_shapes=scratch,
        compiler_params=pltpu.CompilerParams(vmem_limit_bytes=VMEM_LIMIT),
    )(*args)


def shape(*dims):
    return jax.ShapeDtypeStruct(dims, F32)


def column_block(source_ref, block, width, padded):
    wide = source_ref.shape[-1]
    window = min(padded + LANES, wide)
    start = block * width
    base = jnp.minimum(start // LANES * LANES, wide - window)
    part = source_ref[:, pl.ds(pl.multiple_of(base, LANES), window)]
    return pltpu.roll(part, (window - (start - base)) % window, 1)[:, :padded]


def rows_of(value):
    return lax.broadcasted_iota(jnp.int32, value.shape, 0)


def down(value, by):
    moved = pltpu.roll(value, by, 0)
    return jnp.where(rows_of(value) >= by, moved, 0.0)


def up(value, by):
    length = value.shape[0]
    moved = pltpu.roll(value, length - by, 0)
    return jnp.where(rows_of(value) < length - by, moved, 0.0)


def recur(value, powers, move):
    by = 1
    for power in powers:
        value = value + power * move(value, by)
        by *= 2
    return value


def forward_block(series, starts, history, poles, zeros, taps):
    length = series.shape[0]
    first = rows_of(series) == 0
    current, states = (series, [series[length - 1 :]])
    for section, (powers, zero) in enumerate(zip(poles, zeros)):
        if starts is None:
            driven = current - zero * down(current, 1)
        else:
            before = jnp.where(first, starts[section], pltpu.roll(current, 1, 0))
            driven = current - zero * before
            driven = driven + jnp.where(first, powers[0] * starts[section + 1], 0.0)
        current = recur(driven, powers, down)
        states.append(current[length - 1 :])
    reach = history.shape[0]
    extended = jnp.concatenate([history, current], axis=0)
    filtered = taps[0] * current
    for lag in range(1, len(taps)):
        filtered = filtered + taps[lag] * pltpu.roll(extended, lag, 0)[reach:]
    for back in range(1, reach):
        states.append(current[length - 1 - back : length - back])
    return (filtered, states)


def backward_block(filtered, ends, poles, zeros, taps):
    length = filtered.shape[0]
    reach = len(taps) - 1
    border = jnp.zeros((reach, LANES), F32)
    padded = jnp.concatenate([border, filtered, border], axis=0)
    total = padded.shape[0]
    spread = taps[0] * padded
    for lag in range(1, reach + 1):
        spread = spread + taps[lag] * pltpu.roll(padded, total - lag, 0)
    history = spread[:reach]
    current = spread[reach : reach + length]
    sections = len(poles)
    rows = rows_of(current)
    if ends is not None:
        for back in range(reach):
            current = current + jnp.where(rows == length - 1 - back, ends[sections + back], 0.0)
    states = [None] * (sections + reach)
    from_later = None
    for section in reversed(range(sections)):
        value = recur(current, poles[section], up)
        current = value - zeros[section] * up(value, 1)
        if ends is not None:
            current = current + jnp.where(rows == length - 1, ends[section], 0.0)
        to_output = poles[section][0] * value[:1]
        states[section + 1] = to_output if from_later is None else to_output + from_later
        from_later = -zeros[section] * value[:1]
    states[0] = from_later
    states[sections] = states[sections] + history[reach - 1 :]
    for back in range(1, reach):
        states[sections + back] = history[reach - 1 - back : reach - back]
    return (current, states)


def pack(states):
    rows = lax.broadcasted_iota(jnp.int32, (SLOT, LANES), 0)
    packed = jnp.zeros((SLOT, LANES), F32)
    for at, state in enumerate(states):
        packed = jnp.where(rows == at, state, packed)
    return packed


def rates_of(table, sections, taps_count, levels):
    rows = [table[at : at + 1] for at in range(sections * (levels + 1) + taps_count)]
    poles = [rows[at * levels : (at + 1) * levels] for at in range(sections)]
    zeros = rows[sections * levels : sections * (levels + 1)]
    return (poles, zeros, rows[sections * (levels + 1) :])


def predict_kernel(*refs):
    _, *refs = refs
    orders_hbm, lives_hbm, ratios_hbm, taps_hbm = refs[:4]
    residual_hbm, direction_hbm, diagonal_hbm, design_hbm = refs[4:8]
    predicted_ref, rates_ref, spread_ref, steps_ref, design_ref = refs[8:13]
    orders_ref, lives_ref, ratios_ref, taps_ref, remaining_ref, search_ref, diagonal_ref, sems = refs[13:]
    components = taps_ref.shape[0]
    length = design_ref.shape[0] // components
    copies = [
        pltpu.make_async_copy(source, target, sems.at[at])
        for at, (source, target) in enumerate(
            [
                (direction_hbm.at[:, 0, :], search_ref),
                (orders_hbm, orders_ref),
                (lives_hbm, lives_ref),
                (ratios_hbm, ratios_ref),
                (taps_hbm, taps_ref),
                (design_hbm, design_ref),
                (residual_hbm.at[:, 0, :], remaining_ref),
                (diagonal_hbm, diagonal_ref),
            ]
        )
    ]
    for copy in copies:
        copy.start()
    half = LANES // 2
    segments, sections_each, _ = lives_ref.shape
    sections = segments * sections_each
    taps_count = taps_ref.shape[1]
    for copy in copies[1:5]:
        copy.wait()
    lane = lax.broadcasted_iota(jnp.int32, (components, LANES), 1)
    component = lax.broadcasted_iota(jnp.int32, (components, LANES), 0)
    count = half // components
    spreader = jnp.where(lane % half // count == component, 1.0, 0.0)

    def over_lanes(rows):
        return jnp.dot(rows, spreader, precision=HIGHEST, preferred_element_type=F32)

    def flat(ref):
        return jnp.concatenate([ref[at] for at in range(segments)], axis=0)

    life = over_lanes(flat(lives_ref))
    ratio = over_lanes(flat(ratios_ref))
    orders = over_lanes(orders_ref[...].astype(F32))
    tap_rows = lax.dot_general(
        taps_ref[...], spreader, (((0,), (0,)), ((), ())), precision=HIGHEST,
        preferred_element_type=F32,
    )
    spare = jnp.concatenate(
        [orders[at : at + 1] - (each + 0.5) for at in range(segments) for each in range(sections_each)],
        axis=0,
    )
    active = spare > 0.0
    pole_all = jnp.exp(-1.0 / life)
    pole_rate = jnp.where(active, pole_all, 0.0)
    zero_rate = jnp.where(active, 1.0 - ratio * (1.0 - pole_all), 0.0)
    levels = length.bit_length() - 1
    power = pole_rate
    for level in range(levels):
        for section in range(sections):
            at = section * levels + level
            rates_ref[at : at + 1, :] = power[section : section + 1]
        power = power * power
    rates_ref[sections * levels : sections * (levels + 1), :] = zero_rate
    rates_ref[sections * (levels + 1) : sections * (levels + 1) + taps_count, :] = tap_rows

    reach = taps_count - 1
    kinds = sections + reach
    poles, zeros, taps = rates_of(rates_ref, sections, taps_count, length.bit_length() - 1)
    lane = lax.broadcasted_iota(jnp.int32, (1, LANES), 1)
    slot = jnp.where(lane >= half, lane % SLOT, SLOT)
    units = [jnp.where(slot == at, 1.0, 0.0) for at in range(kinds)]
    rows = lax.broadcasted_iota(jnp.int32, (reach, LANES), 0)
    history = jnp.where(slot == kinds - 1 - rows, 1.0, 0.0)
    nothing = jnp.zeros((length, LANES), F32)
    filtered, ends = forward_block(nothing, units[: sections + 1], history, poles, zeros, taps)
    local, heads = backward_block(filtered, None, poles, zeros, taps)
    reply, replies = backward_block(nothing, units, poles, zeros, taps)
    spread_ref[...] = jnp.where(lane < half, pltpu.roll(local, half, 1), reply)
    stacked = jnp.concatenate([pack(ends), pack(heads), pack(replies)], axis=0)
    source = lax.broadcasted_iota(jnp.int32, (LANES, kinds * LANES), 0)
    target = lax.broadcasted_iota(jnp.int32, (LANES, kinds * LANES), 1)
    within = target % LANES
    wanted = half + within // SLOT * SLOT + target // LANES
    pick = jnp.where((within < half) & (source == wanted), 1.0, 0.0).astype(BF16)
    top = stacked.astype(BF16)
    left = stacked - top.astype(F32)
    centre = left.astype(BF16)
    bottom = (left - centre.astype(F32)).astype(BF16)
    thirds = jnp.concatenate([top, centre, bottom], axis=0)
    picked = jnp.dot(thirds, pick, preferred_element_type=F32)
    depth = stacked.shape[0]
    steps_ref[...] = picked[:depth] + (picked[depth : 2 * depth] + picked[2 * depth :])

    copies[0].wait()
    search = search_ref[...]
    high = search.astype(BF16)
    rest = search - high.astype(F32)
    middle = rest.astype(BF16)
    low = (rest - middle.astype(F32)).astype(BF16)
    split = jnp.concatenate([high, middle, low], axis=0)
    copies[5].wait()
    sums = lax.dot_general(
        design_ref[...], split, (((1,), (1,)), ((), ())), preferred_element_type=F32
    )
    pieces = [sums[at * length : (at + 1) * length] for at in range(components)]
    coarse = [piece[:, :count] for piece in pieces]
    fine = [piece[:, count : 2 * count] + piece[:, 2 * count :] for piece in pieces]
    predicted_ref[:length, :] = jnp.concatenate(coarse + fine, axis=1)
    for copy in copies[6:]:
        copy.wait()
    remaining = remaining_ref[...]
    energy = jnp.sum(remaining * diagonal_ref[...] * remaining, axis=1, keepdims=True)
    predicted_ref[length:, :] = jnp.broadcast_to(energy, (count, LANES))


def slices_kernel(width, first_bits, *refs):
    place_ref, vectors_hbm, diagonal_hbm = (refs[0], refs[1:4], refs[4])
    slices = refs[5:9]
    current_ref, remaining_ref, search_ref, diagonal_ref, sems = refs[9:]
    sources = [current_ref, remaining_ref, search_ref]
    copies = [
        pltpu.make_async_copy(vector.at[:, 0, :], target, sems.at[at])
        for at, (vector, target) in enumerate(zip(vectors_hbm, sources))
    ]
    copies.append(pltpu.make_async_copy(diagonal_hbm, diagonal_ref, sems.at[len(sources)]))
    for copy in copies:
        copy.start()
    for copy in copies:
        copy.wait()
    mine = place_ref[0]
    vectors = [diagonal_ref, remaining_ref, search_ref, current_ref]
    for source_ref, target_ref in zip(vectors, slices):
        for at in range(target_ref.shape[0]):
            block = mine if target_ref.shape[0] == 1 else at * first_bits + mine % first_bits
            part = column_block(source_ref, block, width, target_ref.shape[2])
            target_ref[at] = jnp.broadcast_to(part, target_ref.shape[1:])


def filter_kernel(sections, taps_count, length, parts, *refs):
    counts_ref, rates_ref = refs[:2]
    gathered = refs[2 : 2 + parts]
    send_ref, keep_ref, energy_ref = refs[2 + parts :]
    half = LANES // 2
    received = gathered[0][...]
    for other in gathered[1:]:
        received = received + other[...]
    energy_ref[...] = received[length:]
    received = received[:length]
    low_half = lax.broadcasted_iota(jnp.int32, (1, LANES), 1) < half
    data = jnp.where(low_half & (rows_of(received) < counts_ref[0]), received, 0.0)
    poles, zeros, taps = rates_of(rates_ref, sections, taps_count, length.bit_length() - 1)
    history = jnp.zeros((taps_count - 1, LANES), F32)
    filtered, ends = forward_block(data, None, history, poles, zeros, taps)
    local, heads = backward_block(filtered, None, poles, zeros, taps)
    sent = jnp.where(low_half, pack(ends), pltpu.roll(pack(heads), half, 1))
    for block in range(send_ref.shape[0]):
        send_ref[block] = sent
    keep_ref[...] = jnp.where(low_half, local, received + pltpu.roll(received, half, 1))


def normal_kernel(kinds, width, first_bits, *refs):
    place_ref, counts_ref, all_ref, keep_ref, spread_ref, steps_ref, design_ref = refs[:7]
    out_refs, (entering_ref, cut_ref) = (refs[7:-2], refs[-2:])
    blocks = all_ref.shape[0]
    mine = place_ref[0]
    half = LANES // 2

    def apply(which, state):
        terms = []
        for at in range(kinds):
            column = steps_ref[which * SLOT : (which + 1) * SLOT, at * LANES : (at + 1) * LANES]
            terms.append(column * state[at : at + 1])
        while len(terms) > 1:
            pairs = [sum(terms[at : at + 2][1:], terms[at]) for at in range(0, len(terms), 2)]
            terms = pairs
        return terms[0]

    def advance(block, state):
        entering_ref[block] = state
        return apply(0, state) + all_ref[block]

    def retreat(step, state):
        block = blocks - 1 - step
        later = apply(2, state) + (apply(1, entering_ref[block]) + pltpu.roll(all_ref[block], half, 1))
        return jnp.where(block > mine, later, state)

    empty = jnp.zeros((SLOT, LANES), F32)
    unroll = blocks if blocks <= 16 else 4
    lax.fori_loop(0, blocks, advance, empty, unroll=unroll)
    leaving = lax.fori_loop(0, blocks, retreat, empty, unroll=unroll)
    entering = entering_ref[mine]

    groups = half // SLOT
    row = lax.broadcasted_iota(jnp.int32, (half, LANES), 0)
    lane = lax.broadcasted_iota(jnp.int32, (half, LANES), 1)
    own = row // SLOT == lane // SLOT
    expanded = [
        jnp.where(own, jnp.concatenate([state] * groups, axis=0), 0.0)
        for state in (entering, leaving)
    ]
    correction = jnp.dot(
        spread_ref[...],
        jnp.concatenate(expanded, axis=0),
        precision=HIGHEST,
        preferred_element_type=F32,
    )
    kept = keep_ref[...]
    live = (row < counts_ref[0]) & (lane < half)
    weighted = jnp.where(live, kept + correction, 0.0)
    weighted = weighted.astype(BF16).astype(F32)
    product = weighted * pltpu.roll(kept, half, 1)
    turned = jnp.transpose(weighted)
    count = out_refs[0].shape[-2]
    low = jnp.concatenate(
        [turned[at * count : (at + 1) * count] for at in range(half // count)], axis=1
    ).astype(BF16)
    along = jnp.sum(product, axis=0, keepdims=True)
    total = along
    for at in range(1, half // count):
        total = total + pltpu.roll(along, LANES - at * count, 1)
    row = lax.broadcasted_iota(jnp.int32, (count, LANES), 0)
    lane = lax.broadcasted_iota(jnp.int32, (count, LANES), 1)
    curvature = jnp.sum(jnp.where(row == lane, total, 0.0), axis=1, keepdims=True)
    normal = jnp.dot(low, design_ref[...], preferred_element_type=F32)
    padded = out_refs[0].shape[-1]
    column = lax.broadcasted_iota(jnp.int32, (count, padded), 1)
    curvature = jnp.broadcast_to(curvature, (count, padded))
    low_bits = mine % first_bits
    wide = normal.shape[1]
    window = min(padded + LANES, wide)
    for block in range(wide // width):
        start = block * width
        base = min(start // LANES * LANES, wide - window)
        part = normal[:, base : base + window]
        if start != base:
            part = pltpu.roll(part, window - (start - base), 1)
        cut_ref[block] = jnp.where(column < width, part[:, :padded], curvature)
    for apart, out_ref in enumerate(out_refs):
        for at in range(out_ref.shape[0]):
            out_ref[at] = cut_ref[at * first_bits + (low_bits ^ apart)]


def update_kernel(width, first_bits, *refs):
    place_ref, held_ref, got_ref, energy_ref = refs[:4]
    remaining_ref, diagonal_ref, current_ref, search_ref = refs[4:8]
    next_ref, new_solution_ref, new_residual_ref, conditioned_ref, entering_ref = refs[8:]
    parts, count, padded = held_ref.shape
    column = lax.broadcasted_iota(jnp.int32, (count, padded), 1)
    at_curve = column == width
    normal = held_ref[0] + got_ref[0]
    curvature = jnp.sum(jnp.where(at_curve, normal, 0.0), axis=1, keepdims=True)
    step = energy_ref[:, :1] / curvature
    total = jnp.zeros((count, padded), F32)
    for at in range(parts):
        normal = held_ref[at] + got_ref[at]
        changed = remaining_ref[at] - step * normal
        scaled = diagonal_ref[at] * changed
        entering_ref[at] = changed
        total = total + jnp.where(column < width, changed * scaled, 0.0)
    share = jnp.sum(total, axis=1, keepdims=True)
    next_ref[...] = jnp.broadcast_to(share, next_ref.shape)
    own = place_ref[0] // first_bits
    changed = entering_ref[own]
    new_residual_ref[...] = changed
    conditioned_ref[...] = diagonal_ref[own] * changed
    new_solution_ref[...] = current_ref[0] + step * search_ref[0]


def finish_kernel(parts, *refs):
    energy_ref, conditioned_ref, search_ref = refs[:3]
    early_refs, shares = (refs[3:5], refs[5 : 5 + parts])
    out_hbm, scratch = (refs[5 + parts : 8 + parts], refs[8 + parts :])
    width = scratch[0].shape[1]
    sems = scratch[3]
    copies = [
        pltpu.make_async_copy(scratch[at], out_hbm[at].at[:, 0, :], sems.at[at]) for at in range(3)
    ]
    for source_ref, target_ref, copy in zip(early_refs, scratch, copies):
        target_ref[...] = source_ref[:, :width]
        copy.start()
    energy_next = shares[0][...]
    for share_ref in shares[1:]:
        energy_next = energy_next + share_ref[...]
    turn = (energy_next / energy_ref[...])[:, :1]
    scratch[2][...] = (conditioned_ref[...] + turn * search_ref[0])[:, :width]
    copies[2].start()
    for copy in copies:
        copy.wait()


def exchange(value, axis, bit):
    size = lax.axis_size(axis)
    return lax.ppermute(value, axis, [(at, at ^ bit) for at in range(size)])


def over_order(value):
    if lax.axis_size("order") == 2:
        return [value, exchange(value, "order", 1)]
    return [lax.psum(value, "order")]


def shards(
    solution,
    residual,
    direction,
    precond,
    design,
    epoch_counts,
    segment_orders,
    pole_life,
    zero_ratio,
    fir_taps,
):
    count, _, wide = direction.shape
    components, length = design.shape[:2]
    sections = pole_life.shape[1] * pole_life.shape[2]
    taps_count = fir_taps.shape[1]
    kinds = sections + taps_count - 1
    blocks = lax.axis_size("tm")
    width = wide // blocks
    padded = (width // LANES + 1) * LANES
    bits = blocks.bit_length() - 1
    halved = bits // 2
    classes = 1 << halved
    parts = blocks // classes
    place = lax.axis_index("tm").astype(jnp.int32).reshape(1)
    levels = length.bit_length() - 1
    hbm = pl.BlockSpec(memory_space=pltpu.HBM)
    small = [
        segment_orders.T,
        jnp.transpose(pole_life, (1, 2, 0)),
        jnp.transpose(zero_ratio, (1, 2, 0)),
        fir_taps,
    ]

    predicted, rates, spread, steps, design_kept = call(
        predict_kernel,
        (
            shape(length + count, LANES),
            shape(sections * (levels + 1) + taps_count, LANES),
            shape(length, LANES),
            shape(3 * SLOT, kinds * LANES),
            jax.ShapeDtypeStruct((components * length, wide), BF16),
        ),
        place,
        *small,
        residual,
        direction,
        precond,
        design.reshape(components * length, wide),
        specs=[smem()] + [hbm] * 8,
        scratch=[pltpu.VMEM(each.shape, each.dtype) for each in small]
        + [pltpu.VMEM((count, wide), F32)] * 2
        + [pltpu.VMEM((1, wide), F32), pltpu.SemaphoreType.DMA((8,))],
    )
    arrived = over_order(predicted)
    send, keep, energy = call(
        functools.partial(filter_kernel, sections, taps_count, length, len(arrived)),
        (shape(blocks, SLOT, LANES), shape(length, LANES), shape(count, LANES)),
        epoch_counts,
        rates,
        *arrived,
        specs=[smem()] + [vmem()] * (1 + len(arrived)),
    )
    everyone = lax.all_to_all(send, "tm", 0, 0)
    pieces = call(
        functools.partial(normal_kernel, kinds, width, classes),
        [shape(parts, count, padded)] * classes,
        place,
        epoch_counts,
        everyone,
        keep,
        spread,
        steps,
        design_kept,
        specs=[smem()] * 2 + [vmem()] * 5,
        scratch=[pltpu.VMEM((blocks, SLOT, LANES), F32), pltpu.VMEM((blocks, count, padded), F32)],
    )
    diagonal_parts, remaining_parts, search_own, current_own = call(
        functools.partial(slices_kernel, width, classes),
        (
            shape(parts, count, padded),
            shape(parts, count, padded),
            shape(1, count, padded),
            shape(1, count, padded),
        ),
        place,
        solution,
        residual,
        direction,
        precond,
        specs=[smem()] + [hbm] * 4,
        scratch=[pltpu.VMEM((count, wide), F32)] * 3
        + [pltpu.VMEM((1, wide), F32), pltpu.SemaphoreType.DMA((4,))],
    )
    arriving = [exchange(pieces[apart], "tm", apart) for apart in range(1, classes)]
    buffer = pieces[0] + sum(arriving[1:], arriving[0])
    for bit in range(halved, bits - 1):
        buffer = buffer + exchange(buffer, "tm", 1 << bit)
    arriving = exchange(buffer, "tm", 1 << bits - 1)
    share, new_solution, new_residual, conditioned = call(
        functools.partial(update_kernel, width, classes),
        (
            shape(count, LANES),
            shape(count, padded),
            shape(count, padded),
            shape(count, padded),
        ),
        place,
        buffer,
        arriving,
        energy,
        remaining_parts,
        diagonal_parts,
        current_own,
        search_own,
        specs=[smem()] + [vmem()] * 7,
        scratch=[pltpu.VMEM((parts, count, padded), F32)],
    )
    for bit in range(halved):
        share = share + exchange(share, "tm", 1 << bit)
    shares = over_order(share)
    return call(
        functools.partial(finish_kernel, len(shares)),
        (pltpu.HBM((count, 1, width), F32),) * 3,
        energy,
        conditioned,
        search_own,
        new_solution,
        new_residual,
        *shares,
        scratch=[pltpu.VMEM((count, width), F32)] * 3 + [pltpu.SemaphoreType.DMA((3,))],
    )


def solution(mesh):
    placed = (
        P(None, "order", None),
        P(None, "order", None),
        P(None, "order", None),
        P("order", None),
        P(None, "tm", "order", None),
        P("tm"),
        P(),
        P(),
        P(),
        P(),
    )
    return jax.shard_map(
        shards,
        mesh=mesh,
        in_specs=placed,
        out_specs=(P(None, "order", "tm"), P(None, "order", "tm"), P(None, "order", "tm")),
        check_vma=False,
    )
```

```python
import functools

import jax
import jax.numpy as jnp
from jax import lax
from jax.experimental import pallas as pl
from jax.experimental.pallas import tpu as pltpu
from jax.sharding import PartitionSpec as P

HIGHEST = lax.Precision.HIGHEST
F32 = jnp.float32
BF16 = jnp.bfloat16
LANES = 128
SLOT = 16
VMEM_LIMIT = 16 * 1024 * 1024


def vmem():
    return pl.BlockSpec(memory_space=pltpu.VMEM)


def smem():
    return pl.BlockSpec(memory_space=pltpu.SMEM)


def call(kernel, outs, *args, specs=None, scratch=()):
    args = [
        pltpu.with_memory_space_constraint(arg, pltpu.HBM)
        if specs and specs[at].memory_space == pltpu.HBM
        else arg
        for at, arg in enumerate(args)
    ]
    return pl.pallas_call(
        kernel,
        out_shape=outs,
        in_specs=specs or [vmem()] * len(args),
        out_specs=jax.tree.map(
            lambda out: pl.BlockSpec(memory_space=getattr(out, "memory_space", pltpu.VMEM)), outs
        ),
        scratch_shapes=scratch,
        compiler_params=pltpu.CompilerParams(vmem_limit_bytes=VMEM_LIMIT),
    )(*args)


def shape(*dims):
    return jax.ShapeDtypeStruct(dims, F32)


def halves(value):
    high = value.astype(BF16)
    return (high, (value - high.astype(F32)).astype(BF16))


def column_block(source_ref, block, width, padded):
    wide = source_ref.shape[-1]
    window = min(padded + LANES, wide)
    start = block * width
    base = jnp.minimum(start // LANES * LANES, wide - window)
    part = source_ref[:, pl.ds(pl.multiple_of(base, LANES), window)]
    return pltpu.roll(part, (window - (start - base)) % window, 1)[:, :padded]


def rows_of(value):
    return lax.broadcasted_iota(jnp.int32, value.shape, 0)


def down(value, by):
    moved = pltpu.roll(value, by, 0)
    return jnp.where(rows_of(value) >= by, moved, 0.0)


def up(value, by):
    length = value.shape[0]
    moved = pltpu.roll(value, length - by, 0)
    return jnp.where(rows_of(value) < length - by, moved, 0.0)


def recur(value, powers, move):
    by = 1
    for power in powers:
        value = value + power * move(value, by)
        by *= 2
    return value


def forward_block(series, starts, history, poles, zeros, taps):
    length = series.shape[0]
    first = rows_of(series) == 0
    current, states = (series, [series[length - 1 :]])
    for section, (powers, zero) in enumerate(zip(poles, zeros)):
        if starts is None:
            driven = current - zero * down(current, 1)
        else:
            before = jnp.where(first, starts[section], pltpu.roll(current, 1, 0))
            driven = current - zero * before
            driven = driven + jnp.where(first, powers[0] * starts[section + 1], 0.0)
        current = recur(driven, powers, down)
        states.append(current[length - 1 :])
    reach = history.shape[0]
    extended = jnp.concatenate([history, current], axis=0)
    filtered = taps[0] * current
    for lag in range(1, len(taps)):
        filtered = filtered + taps[lag] * pltpu.roll(extended, lag, 0)[reach:]
    for back in range(1, reach):
        states.append(current[length - 1 - back : length - back])
    return (filtered, states)


def backward_block(filtered, ends, poles, zeros, taps):
    length = filtered.shape[0]
    reach = len(taps) - 1
    border = jnp.zeros((reach, LANES), F32)
    padded = jnp.concatenate([border, filtered, border], axis=0)
    total = padded.shape[0]
    spread = taps[0] * padded
    for lag in range(1, reach + 1):
        spread = spread + taps[lag] * pltpu.roll(padded, total - lag, 0)
    history = spread[:reach]
    current = spread[reach : reach + length]
    sections = len(poles)
    rows = rows_of(current)
    if ends is not None:
        for back in range(reach):
            current = current + jnp.where(rows == length - 1 - back, ends[sections + back], 0.0)
    states = [None] * (sections + reach)
    from_later = None
    for section in reversed(range(sections)):
        value = recur(current, poles[section], up)
        current = value - zeros[section] * up(value, 1)
        if ends is not None:
            current = current + jnp.where(rows == length - 1, ends[section], 0.0)
        to_output = poles[section][0] * value[:1]
        states[section + 1] = to_output if from_later is None else to_output + from_later
        from_later = -zeros[section] * value[:1]
    states[0] = from_later
    states[sections] = states[sections] + history[reach - 1 :]
    for back in range(1, reach):
        states[sections + back] = history[reach - 1 - back : reach - back]
    return (current, states)


def pack(states):
    rows = lax.broadcasted_iota(jnp.int32, (SLOT, LANES), 0)
    packed = jnp.zeros((SLOT, LANES), F32)
    for at, state in enumerate(states):
        packed = jnp.where(rows == at, state, packed)
    return packed


def rates_of(table, sections, taps_count, levels):
    rows = [table[at : at + 1] for at in range(sections * (levels + 1) + taps_count)]
    poles = [rows[at * levels : (at + 1) * levels] for at in range(sections)]
    zeros = rows[sections * levels : sections * (levels + 1)]
    return (poles, zeros, rows[sections * (levels + 1) :])


def predict_kernel(*refs):
    _, *refs = refs
    orders_hbm, lives_hbm, ratios_hbm, taps_hbm = refs[:4]
    residual_hbm, direction_hbm, diagonal_hbm, design_hbm = refs[4:8]
    predicted_ref, rates_ref, spread_ref, steps_ref, design_ref = refs[8:13]
    orders_ref, lives_ref, ratios_ref, taps_ref, remaining_ref, search_ref, diagonal_ref, sems = refs[13:]
    components = taps_ref.shape[0]
    length = design_ref.shape[0] // components
    copies = [
        pltpu.make_async_copy(source, target, sems.at[at])
        for at, (source, target) in enumerate(
            [
                (direction_hbm.at[:, 0, :], search_ref),
                (orders_hbm, orders_ref),
                (lives_hbm, lives_ref),
                (ratios_hbm, ratios_ref),
                (taps_hbm, taps_ref),
                (design_hbm, design_ref),
                (residual_hbm.at[:, 0, :], remaining_ref),
                (diagonal_hbm, diagonal_ref),
            ]
        )
    ]
    for copy in copies:
        copy.start()
    half = LANES // 2
    segments, sections_each, _ = lives_ref.shape
    sections = segments * sections_each
    taps_count = taps_ref.shape[1]
    for copy in copies[1:5]:
        copy.wait()
    lane = lax.broadcasted_iota(jnp.int32, (components, LANES), 1)
    component = lax.broadcasted_iota(jnp.int32, (components, LANES), 0)
    count = half // components
    spreader = jnp.where(lane % half // count == component, 1.0, 0.0)

    def over_lanes(rows):
        return jnp.dot(rows, spreader, precision=HIGHEST, preferred_element_type=F32)

    def flat(ref):
        return jnp.concatenate([ref[at] for at in range(segments)], axis=0)

    life = over_lanes(flat(lives_ref))
    ratio = over_lanes(flat(ratios_ref))
    orders = over_lanes(orders_ref[...].astype(F32))
    tap_rows = lax.dot_general(
        taps_ref[...], spreader, (((0,), (0,)), ((), ())), precision=HIGHEST,
        preferred_element_type=F32,
    )
    spare = jnp.concatenate(
        [orders[at : at + 1] - (each + 0.5) for at in range(segments) for each in range(sections_each)],
        axis=0,
    )
    active = spare > 0.0
    pole_all = jnp.exp(-1.0 / life)
    pole_rate = jnp.where(active, pole_all, 0.0)
    zero_rate = jnp.where(active, 1.0 - ratio * (1.0 - pole_all), 0.0)
    levels = length.bit_length() - 1
    power = pole_rate
    for level in range(levels):
        for section in range(sections):
            at = section * levels + level
            rates_ref[at : at + 1, :] = power[section : section + 1]
        power = power * power
    rates_ref[sections * levels : sections * (levels + 1), :] = zero_rate
    rates_ref[sections * (levels + 1) : sections * (levels + 1) + taps_count, :] = tap_rows

    reach = taps_count - 1
    kinds = sections + reach
    poles, zeros, taps = rates_of(rates_ref, sections, taps_count, length.bit_length() - 1)
    lane = lax.broadcasted_iota(jnp.int32, (1, LANES), 1)
    slot = jnp.where(lane >= half, lane % SLOT, SLOT)
    units = [jnp.where(slot == at, 1.0, 0.0) for at in range(kinds)]
    rows = lax.broadcasted_iota(jnp.int32, (reach, LANES), 0)
    history = jnp.where(slot == kinds - 1 - rows, 1.0, 0.0)
    nothing = jnp.zeros((length, LANES), F32)
    filtered, ends = forward_block(nothing, units[: sections + 1], history, poles, zeros, taps)
    local, heads = backward_block(filtered, None, poles, zeros, taps)
    reply, replies = backward_block(nothing, units, poles, zeros, taps)
    spread = jnp.where(lane < half, pltpu.roll(local, half, 1), reply)
    spread_high, spread_low = halves(spread)
    spread_ref[...] = jnp.concatenate([spread_high, spread_high, spread_low], axis=1)
    stacked = jnp.concatenate([pack(ends), pack(heads), pack(replies)], axis=0)
    source = lax.broadcasted_iota(jnp.int32, (LANES, kinds * LANES), 0)
    target = lax.broadcasted_iota(jnp.int32, (LANES, kinds * LANES), 1)
    within = target % LANES
    wanted = half + within // SLOT * SLOT + target // LANES
    pick = jnp.where((within < half) & (source == wanted), 1.0, 0.0).astype(BF16)
    top = stacked.astype(BF16)
    left = stacked - top.astype(F32)
    centre = left.astype(BF16)
    bottom = (left - centre.astype(F32)).astype(BF16)
    thirds = jnp.concatenate([top, centre, bottom], axis=0)
    picked = jnp.dot(thirds, pick, preferred_element_type=F32)
    depth = stacked.shape[0]
    steps_ref[...] = picked[:depth] + (picked[depth : 2 * depth] + picked[2 * depth :])

    copies[0].wait()
    search = search_ref[...]
    high = search.astype(BF16)
    rest = search - high.astype(F32)
    middle = rest.astype(BF16)
    low = (rest - middle.astype(F32)).astype(BF16)
    split = jnp.concatenate([high, middle, low], axis=0)
    copies[5].wait()
    sums = lax.dot_general(
        design_ref[...], split, (((1,), (1,)), ((), ())), preferred_element_type=F32
    )
    pieces = [sums[at * length : (at + 1) * length] for at in range(components)]
    coarse = [piece[:, :count] for piece in pieces]
    fine = [piece[:, count : 2 * count] + piece[:, 2 * count :] for piece in pieces]
    predicted_ref[:length, :] = jnp.concatenate(coarse + fine, axis=1)
    for copy in copies[6:]:
        copy.wait()
    remaining = remaining_ref[...]
    energy = jnp.sum(remaining * diagonal_ref[...] * remaining, axis=1, keepdims=True)
    predicted_ref[length:, :] = jnp.broadcast_to(energy, (count, LANES))


def slices_kernel(width, first_bits, *refs):
    place_ref, vectors_hbm, diagonal_hbm = (refs[0], refs[1:4], refs[4])
    slices = refs[5:9]
    current_ref, remaining_ref, search_ref, diagonal_ref, sems = refs[9:]
    sources = [current_ref, remaining_ref, search_ref]
    copies = [
        pltpu.make_async_copy(vector.at[:, 0, :], target, sems.at[at])
        for at, (vector, target) in enumerate(zip(vectors_hbm, sources))
    ]
    copies.append(pltpu.make_async_copy(diagonal_hbm, diagonal_ref, sems.at[len(sources)]))
    for copy in copies:
        copy.start()
    for copy in copies:
        copy.wait()
    mine = place_ref[0]
    vectors = [diagonal_ref, remaining_ref, search_ref, current_ref]
    for source_ref, target_ref in zip(vectors, slices):
        for at in range(target_ref.shape[0]):
            block = mine if target_ref.shape[0] == 1 else at * first_bits + mine % first_bits
            part = column_block(source_ref, block, width, target_ref.shape[2])
            target_ref[at] = jnp.broadcast_to(part, target_ref.shape[1:])


def filter_kernel(sections, taps_count, length, parts, *refs):
    counts_ref, rates_ref = refs[:2]
    gathered = refs[2 : 2 + parts]
    send_ref, keep_ref, energy_ref = refs[2 + parts :]
    half = LANES // 2
    received = gathered[0][...]
    for other in gathered[1:]:
        received = received + other[...]
    energy_ref[...] = received[length:]
    received = received[:length]
    low_half = lax.broadcasted_iota(jnp.int32, (1, LANES), 1) < half
    data = jnp.where(low_half & (rows_of(received) < counts_ref[0]), received, 0.0)
    poles, zeros, taps = rates_of(rates_ref, sections, taps_count, length.bit_length() - 1)
    history = jnp.zeros((taps_count - 1, LANES), F32)
    filtered, ends = forward_block(data, None, history, poles, zeros, taps)
    local, heads = backward_block(filtered, None, poles, zeros, taps)
    sent = jnp.where(low_half, pack(ends), pltpu.roll(pack(heads), half, 1))
    for block in range(send_ref.shape[0]):
        send_ref[block] = sent
    keep_ref[...] = jnp.where(low_half, local, received + pltpu.roll(received, half, 1))


def normal_kernel(kinds, width, first_bits, *refs):
    place_ref, counts_ref, all_ref, keep_ref, spread_ref, steps_ref, design_ref = refs[:7]
    out_refs, (entering_ref, cut_ref) = (refs[7:-2], refs[-2:])
    blocks = all_ref.shape[0]
    mine = place_ref[0]
    half = LANES // 2

    def apply(which, state):
        terms = []
        for at in range(kinds):
            column = steps_ref[which * SLOT : (which + 1) * SLOT, at * LANES : (at + 1) * LANES]
            terms.append(column * state[at : at + 1])
        while len(terms) > 1:
            pairs = [sum(terms[at : at + 2][1:], terms[at]) for at in range(0, len(terms), 2)]
            terms = pairs
        return terms[0]

    def advance(block, state):
        entering_ref[block] = state
        return apply(0, state) + all_ref[block]

    def retreat(step, state):
        block = blocks - 1 - step
        later = apply(2, state) + (apply(1, entering_ref[block]) + pltpu.roll(all_ref[block], half, 1))
        return jnp.where(block > mine, later, state)

    empty = jnp.zeros((SLOT, LANES), F32)
    unroll = blocks if blocks <= 16 else 4
    lax.fori_loop(0, blocks, advance, empty, unroll=unroll)
    leaving = lax.fori_loop(0, blocks, retreat, empty, unroll=unroll)
    entering = entering_ref[mine]

    groups = half // SLOT
    row = lax.broadcasted_iota(jnp.int32, (half, LANES), 0)
    lane = lax.broadcasted_iota(jnp.int32, (half, LANES), 1)
    own = row // SLOT == lane // SLOT
    expanded = [
        jnp.where(own, jnp.concatenate([state] * groups, axis=0), 0.0)
        for state in (entering, leaving)
    ]
    state_high, state_low = halves(jnp.concatenate(expanded, axis=0))
    correction = jnp.dot(
        spread_ref[...],
        jnp.concatenate([state_high, state_low, state_high], axis=0),
        preferred_element_type=F32,
    )
    kept = keep_ref[...]
    live = (row < counts_ref[0]) & (lane < half)
    weighted = jnp.where(live, kept + correction, 0.0)
    weighted = weighted.astype(BF16).astype(F32)
    product = weighted * pltpu.roll(kept, half, 1)
    turned = jnp.transpose(weighted)
    count = out_refs[0].shape[-2]
    low = jnp.concatenate(
        [turned[at * count : (at + 1) * count] for at in range(half // count)], axis=1
    ).astype(BF16)
    along = jnp.sum(product, axis=0, keepdims=True)
    total = along
    for at in range(1, half // count):
        total = total + pltpu.roll(along, LANES - at * count, 1)
    row = lax.broadcasted_iota(jnp.int32, (count, LANES), 0)
    lane = lax.broadcasted_iota(jnp.int32, (count, LANES), 1)
    curvature = jnp.sum(jnp.where(row == lane, total, 0.0), axis=1, keepdims=True)
    normal = jnp.dot(low, design_ref[...], preferred_element_type=F32)
    padded = out_refs[0].shape[-1]
    column = lax.broadcasted_iota(jnp.int32, (count, padded), 1)
    curvature = jnp.broadcast_to(curvature, (count, padded))
    low_bits = mine % first_bits
    wide = normal.shape[1]
    window = min(padded + LANES, wide)
    for block in range(wide // width):
        start = block * width
        base = min(start // LANES * LANES, wide - window)
        part = normal[:, base : base + window]
        if start != base:
            part = pltpu.roll(part, window - (start - base), 1)
        cut_ref[block] = jnp.where(column < width, part[:, :padded], curvature)
    for apart, out_ref in enumerate(out_refs):
        for at in range(out_ref.shape[0]):
            out_ref[at] = cut_ref[at * first_bits + (low_bits ^ apart)]


def update_kernel(width, first_bits, *refs):
    place_ref, held_ref, got_ref, energy_ref = refs[:4]
    remaining_ref, diagonal_ref, current_ref, search_ref = refs[4:8]
    next_ref, new_solution_ref, new_residual_ref, conditioned_ref, entering_ref = refs[8:]
    parts, count, padded = held_ref.shape
    column = lax.broadcasted_iota(jnp.int32, (count, padded), 1)
    at_curve = column == width
    normal = held_ref[0] + got_ref[0]
    curvature = jnp.sum(jnp.where(at_curve, normal, 0.0), axis=1, keepdims=True)
    step = energy_ref[:, :1] / curvature
    total = jnp.zeros((count, padded), F32)
    for at in range(parts):
        normal = held_ref[at] + got_ref[at]
        changed = remaining_ref[at] - step * normal
        scaled = diagonal_ref[at] * changed
        entering_ref[at] = changed
        total = total + jnp.where(column < width, changed * scaled, 0.0)
    share = jnp.sum(total, axis=1, keepdims=True)
    next_ref[...] = jnp.broadcast_to(share, next_ref.shape)
    own = place_ref[0] // first_bits
    changed = entering_ref[own]
    new_residual_ref[...] = changed
    conditioned_ref[...] = diagonal_ref[own] * changed
    new_solution_ref[...] = current_ref[0] + step * search_ref[0]


def finish_kernel(parts, *refs):
    energy_ref, conditioned_ref, search_ref = refs[:3]
    early_refs, shares = (refs[3:5], refs[5 : 5 + parts])
    out_hbm, scratch = (refs[5 + parts : 8 + parts], refs[8 + parts :])
    width = scratch[0].shape[1]
    sems = scratch[3]
    copies = [
        pltpu.make_async_copy(scratch[at], out_hbm[at].at[:, 0, :], sems.at[at]) for at in range(3)
    ]
    for source_ref, target_ref, copy in zip(early_refs, scratch, copies):
        target_ref[...] = source_ref[:, :width]
        copy.start()
    energy_next = shares[0][...]
    for share_ref in shares[1:]:
        energy_next = energy_next + share_ref[...]
    turn = (energy_next / energy_ref[...])[:, :1]
    scratch[2][...] = (conditioned_ref[...] + turn * search_ref[0])[:, :width]
    copies[2].start()
    for copy in copies:
        copy.wait()


def exchange(value, axis, bit):
    size = lax.axis_size(axis)
    return lax.ppermute(value, axis, [(at, at ^ bit) for at in range(size)])


def over_order(value):
    if lax.axis_size("order") == 2:
        return [value, exchange(value, "order", 1)]
    return [lax.psum(value, "order")]


def shards(
    solution,
    residual,
    direction,
    precond,
    design,
    epoch_counts,
    segment_orders,
    pole_life,
    zero_ratio,
    fir_taps,
):
    count, _, wide = direction.shape
    components, length = design.shape[:2]
    sections = pole_life.shape[1] * pole_life.shape[2]
    taps_count = fir_taps.shape[1]
    kinds = sections + taps_count - 1
    blocks = lax.axis_size("tm")
    width = wide // blocks
    padded = (width // LANES + 1) * LANES
    bits = blocks.bit_length() - 1
    halved = bits // 2
    classes = 1 << halved
    parts = blocks // classes
    place = lax.axis_index("tm").astype(jnp.int32).reshape(1)
    levels = length.bit_length() - 1
    hbm = pl.BlockSpec(memory_space=pltpu.HBM)
    small = [
        segment_orders.T,
        jnp.transpose(pole_life, (1, 2, 0)),
        jnp.transpose(zero_ratio, (1, 2, 0)),
        fir_taps,
    ]

    predicted, rates, spread, steps, design_kept = call(
        predict_kernel,
        (
            shape(length + count, LANES),
            shape(sections * (levels + 1) + taps_count, LANES),
            jax.ShapeDtypeStruct((length, 3 * LANES), BF16),
            shape(3 * SLOT, kinds * LANES),
            jax.ShapeDtypeStruct((components * length, wide), BF16),
        ),
        place,
        *small,
        residual,
        direction,
        precond,
        design.reshape(components * length, wide),
        specs=[smem()] + [hbm] * 8,
        scratch=[pltpu.VMEM(each.shape, each.dtype) for each in small]
        + [pltpu.VMEM((count, wide), F32)] * 2
        + [pltpu.VMEM((1, wide), F32), pltpu.SemaphoreType.DMA((8,))],
    )
    arrived = over_order(predicted)
    send, keep, energy = call(
        functools.partial(filter_kernel, sections, taps_count, length, len(arrived)),
        (shape(blocks, SLOT, LANES), shape(length, LANES), shape(count, LANES)),
        epoch_counts,
        rates,
        *arrived,
        specs=[smem()] + [vmem()] * (1 + len(arrived)),
    )
    everyone = lax.all_to_all(send, "tm", 0, 0)
    pieces = call(
        functools.partial(normal_kernel, kinds, width, classes),
        [shape(parts, count, padded)] * classes,
        place,
        epoch_counts,
        everyone,
        keep,
        spread,
        steps,
        design_kept,
        specs=[smem()] * 2 + [vmem()] * 5,
        scratch=[pltpu.VMEM((blocks, SLOT, LANES), F32), pltpu.VMEM((blocks, count, padded), F32)],
    )
    diagonal_parts, remaining_parts, search_own, current_own = call(
        functools.partial(slices_kernel, width, classes),
        (
            shape(parts, count, padded),
            shape(parts, count, padded),
            shape(1, count, padded),
            shape(1, count, padded),
        ),
        place,
        solution,
        residual,
        direction,
        precond,
        specs=[smem()] + [hbm] * 4,
        scratch=[pltpu.VMEM((count, wide), F32)] * 3
        + [pltpu.VMEM((1, wide), F32), pltpu.SemaphoreType.DMA((4,))],
    )
    arriving = [exchange(pieces[apart], "tm", apart) for apart in range(1, classes)]
    buffer = pieces[0] + sum(arriving[1:], arriving[0])
    for bit in range(halved, bits - 1):
        buffer = buffer + exchange(buffer, "tm", 1 << bit)
    arriving = exchange(buffer, "tm", 1 << bits - 1)
    share, new_solution, new_residual, conditioned = call(
        functools.partial(update_kernel, width, classes),
        (
            shape(count, LANES),
            shape(count, padded),
            shape(count, padded),
            shape(count, padded),
        ),
        place,
        buffer,
        arriving,
        energy,
        remaining_parts,
        diagonal_parts,
        current_own,
        search_own,
        specs=[smem()] + [vmem()] * 7,
        scratch=[pltpu.VMEM((parts, count, padded), F32)],
    )
    for bit in range(halved):
        share = share + exchange(share, "tm", 1 << bit)
    shares = over_order(share)
    return call(
        functools.partial(finish_kernel, len(shares)),
        (pltpu.HBM((count, 1, width), F32),) * 3,
        energy,
        conditioned,
        search_own,
        new_solution,
        new_residual,
        *shares,
        scratch=[pltpu.VMEM((count, width), F32)] * 3 + [pltpu.SemaphoreType.DMA((3,))],
    )


def solution(mesh):
    placed = (
        P(None, "order", None),
        P(None, "order", None),
        P(None, "order", None),
        P("order", None),
        P(None, "tm", "order", None),
        P("tm"),
        P(),
        P(),
        P(),
        P(),
    )
    return jax.shard_map(
        shards,
        mesh=mesh,
        in_specs=placed,
        out_specs=(P(None, "order", "tm"), P(None, "order", "tm"), P(None, "order", "tm")),
        check_vma=False,
    )
```
